32 devices in a mesh: dp: 8 (over y, x, core), tensor: 4 (over z).
Axes of the slice: x: 2, y: 2, z: 4, core: 2. Of those that a mesh axis runs over, the one named last changes fastest.
Arguments:
- layer_input: bfloat16 [16384, 1024], P('dp'), may hold values from -6 to 6
- output_grad: bfloat16 [16384, 1024], P('dp'), may hold values from -6 to 6
- segments: int32 [8, 2048], P('dp'), may hold values from 0 to 15, never falling along the last dimension, each value on 1 to 1024 neighbouring positions
- adapter_ids: int32 [8, 1], P('dp'), may hold values from 0 to 7
- ln_gain: float32 [2, 1024], replicated, may hold values from 0.5 to 1.5
- ln_bias: float32 [2, 1024], replicated, may hold values from -3 to 3
- w_qkv: bfloat16 [3, 1024, 1024], P(None, None, 'tensor'), may hold values from -0.1875 to 0.1875
- w_out: bfloat16 [1024, 1024], P('tensor'), may hold values from -1 to 1
- w_gate_up: bfloat16 [2, 1024, 4096], P(None, None, 'tensor'), may hold values from -0.1875 to 0.1875
- w_down: bfloat16 [4096, 1024], P('tensor'), may hold values from -0.09375 to 0.09375
- qkv_a: bfloat16 [8, 48, 1024], replicated, may hold values from -0.1875 to 0.1875
- qkv_b: bfloat16 [8, 48, 1024], P(None, None, 'tensor'), may hold values from -0.75 to 0.75
- out_a: bfloat16 [8, 16, 1024], P(None, None, 'tensor'), may hold values from -1 to 1
- out_b: bfloat16 [8, 16, 1024], replicated, may hold values from -0.75 to 0.75
- ffn_a: bfloat16 [8, 32, 1024], replicated, may hold values from -0.1875 to 0.1875
- ffn_b: bfloat16 [8, 32, 4096], P(None, None, 'tensor'), may hold values from -0.75 to 0.75
- down_a: bfloat16 [8, 16, 4096], P(None, None, 'tensor'), may hold values from -0.09375 to 0.09375
- down_b: bfloat16 [8, 16, 1024], replicated, may hold values from -0.75 to 0.75
Outputs:
- layer_output: bfloat16 [16384, 1024], P('dp')
- input_grad: float32 [16384, 1024], P('dp')
- qkv_a_grad: float32 [8, 48, 1024], replicated
- qkv_b_grad: float32 [8, 48, 1024], P(None, None, 'tensor')
- out_a_grad: float32 [8, 16, 1024], P(None, None, 'tensor')
- out_b_grad: float32 [8, 16, 1024], replicated
- ffn_a_grad: float32 [8, 32, 1024], replicated
- ffn_b_grad: float32 [8, 32, 4096], P(None, None, 'tensor')
- down_a_grad: float32 [8, 16, 4096], P(None, None, 'tensor')
- down_b_grad: float32 [8, 16, 1024], replicated
The draws below stay inside these ranges and needn't reach their ends.
Inputs may be any that keep to these rules, and one draw needn't show every extreme that they name: In each sequence segment numbers never fall; each of the 16 segments holds 1 to 1024 tokens, and one holds exactly 1024. `adapter_ids`: every adapter is named by some sequence.
All inputs are finite; a program needn't handle non-finite values.
Results may differ from the reference program's by a relative error of at most 0.022.
Values may be sent and summed in bfloat16 or wider, within the bound.
No kernel may reach another device: no remote copies, remote signals or barrier semaphores. Data moves between devices by JAX's collectives and lax.ppermute only.
A program may use at most 256 MiB of HBM per device.

```python
import math
import jax
import jax.numpy as jnp
import numpy as np
from jax import lax

D = 1024
HEADS = 16
HEAD_DIM = 64
FF = 4096
RANK = 16
ADAPTERS = 8
LEN = 2048
SEGS = 16
SEQS = 8
TOKENS = 16384


def block_scale(rng, extent, cuts, smallest, high):
    factor_of = 1.0
    for position, blocks in cuts:
        steps = jax.random.uniform(jax.random.fold_in(jax.random.fold_in(rng, 6), position), (blocks,), jnp.float32, smallest / len(cuts), high / len(cuts))
        factor_of = factor_of * jnp.repeat(jnp.exp(steps), extent[position] // blocks).reshape((-1,) + (1,) * (len(extent) - 1 - position))
    return factor_of


def picks_of(own_key, rows, count, top, lift):
    ranking = jax.random.permutation(jax.random.fold_in(own_key, 1), count)
    favour = ranking
    for power in range(3):
        favour = favour * favour // count
    favour = favour * lift // count
    tickets = jax.random.randint(jax.random.fold_in(own_key, 2), (rows, count), 0, 4096) + favour
    fixed_rows = jax.random.permutation(jax.random.fold_in(own_key, 3), rows)[jnp.arange(count) % rows]
    tickets = jnp.where(jnp.arange(rows)[:, None] == fixed_rows[None, :], 1 << 14, tickets)
    merit = tickets * count + jnp.arange(count)
    return lax.top_k(merit.astype(jnp.int32), top)[1].astype(jnp.int32)


def length_profile(amount, total, limit, slope):
    weights = [(1 << 20) // math.isqrt(standing ** slope) + 1 for standing in range(2, amount + 1)]
    rest, holding = total - limit - (amount - 1), [1] * (amount - 1)
    while rest > 0:
        candidates = [i for i in range(amount - 1) if holding[i] < limit]
        pool, left = sum([weights[i] for i in candidates]), rest
        for i in candidates:
            addition = min(limit - holding[i], max(1, left * weights[i] // pool), rest)
            holding[i] = holding[i] + addition
            rest = rest - addition
    return np.array([limit] + holding)


def ragged(rng, amount, total, limit, skew):
    if amount == 2:
        one = jax.random.randint(rng, (), max(1, total - limit), min(limit, total - 1) + 1)
        return jnp.stack([one, total - one])
    tallies = jnp.asarray(length_profile(amount, total, limit, skew), jnp.int32)
    couples = (amount - 1) // 2
    donor, receiver = tallies[1:1 + 2 * couples:2], tallies[2:2 + 2 * couples:2]
    room = jnp.minimum(donor - 1, limit - receiver)
    passed = jax.random.randint(jax.random.fold_in(rng, 1), (couples,), 0, 1 << 20) % (room + 1)
    tallies = tallies.at[1:1 + 2 * couples:2].set(donor - passed).at[2:2 + 2 * couples:2].set(receiver + passed)
    return tallies[jax.random.permutation(jax.random.fold_in(rng, 2), amount)]


def noise(key, extent, scale, most, shards=(), kind=jnp.bfloat16):
    values = scale * jax.random.normal(key, extent, jnp.float32)
    if shards:
        values = values * block_scale(key, extent, shards, -0.22, 0.18)
    return jnp.clip(values, -most, most).astype(kind)


def setup_inputs(seed: int = 0) -> dict:
    key_of = jax.random.split(jax.random.key(seed), 19)
    layer_input = noise(key_of[0], (TOKENS, D), 1.0, 6.0, ((0, 8),))
    output_grad = noise(key_of[1], (TOKENS, D), 1.0, 6.0, ((0, 8),))
    segments = jax.vmap(lambda own: jnp.searchsorted(jnp.cumsum(ragged(own, SEGS, LEN, LEN // 2, 2)), jnp.arange(LEN), side="right"))(jax.random.split(key_of[2], SEQS)).reshape((SEQS, LEN)).astype(jnp.int32)
    adapter_ids = picks_of(key_of[3], SEQS, ADAPTERS, 1, 0)
    ln_gain = jnp.clip(1.0 + 0.1 * jax.random.normal(key_of[4], (2, D), jnp.float32), 0.5, 1.5)
    ln_bias = noise(key_of[5], (2, D), 0.5, 3.0, (), jnp.float32)
    w_qkv = noise(key_of[6], (3, D, D), D ** -0.5, 0.1875, ((2, 4),))
    w_out = noise(key_of[7], (D, D), (D // 32) ** -0.5, 1.0, ((0, 4),))
    w_gate_up = noise(key_of[8], (2, D, FF), D ** -0.5, 0.1875, ((2, 4),))
    w_down = noise(key_of[9], (FF, D), FF ** -0.5, 0.09375, ((0, 4),))
    qkv_a = noise(key_of[10], (ADAPTERS, 3 * RANK, D), D ** -0.5, 0.1875)
    qkv_b = noise(key_of[11], (ADAPTERS, 3 * RANK, D), (4 * RANK) ** -0.5, 0.75, ((2, 4),))
    out_a = noise(key_of[12], (ADAPTERS, RANK, D), (D // 32) ** -0.5, 1.0, ((2, 4),))
    out_b = noise(key_of[13], (ADAPTERS, RANK, D), (4 * RANK) ** -0.5, 0.75)
    ffn_a = noise(key_of[14], (ADAPTERS, 2 * RANK, D), D ** -0.5, 0.1875)
    ffn_b = noise(key_of[15], (ADAPTERS, 2 * RANK, FF), (4 * RANK) ** -0.5, 0.75, ((2, 4),))
    down_a = noise(key_of[16], (ADAPTERS, RANK, FF), FF ** -0.5, 0.09375, ((2, 4),))
    down_b = noise(key_of[17], (ADAPTERS, RANK, D), (4 * RANK) ** -0.5, 0.75)
    return {"layer_input": layer_input, "output_grad": output_grad, "segments": segments, "adapter_ids": adapter_ids, "ln_gain": ln_gain, "ln_bias": ln_bias, "w_qkv": w_qkv, "w_out": w_out, "w_gate_up": w_gate_up, "w_down": w_down, "qkv_a": qkv_a, "qkv_b": qkv_b, "out_a": out_a, "out_b": out_b, "ffn_a": ffn_a, "ffn_b": ffn_b, "down_a": down_a, "down_b": down_b}


HIGHEST = lax.Precision.HIGHEST

@jax.custom_vjp
def low(v):
    return lax.optimization_barrier(v.astype(jnp.bfloat16)).astype(jnp.float32)

@jax.custom_vjp
def low_back(v):
    return v

def low_keep(v):
    return (low(v), None)

def low_pass(kept, grad):
    return (grad,)

def back_keep(v):
    return (v, None)

def back_low(kept, grad):
    return (low(grad),)
low.defvjp(low_keep, low_pass)
low_back.defvjp(back_keep, back_low)

def matmul(left, right):
    return jnp.dot(left, right, precision=HIGHEST)

def norm_rows(rows, gain, shift):
    centre = lax.optimization_barrier(jnp.mean(rows, axis=-1, keepdims=True))
    centred = rows - centre
    spread = lax.optimization_barrier(jnp.mean(centred * centred, axis=-1, keepdims=True))
    return centred * lax.rsqrt(spread + 1e-12) * gain + shift

def tables(length, head_dim):
    half_dim = head_dim // 2
    freq = 10000.0 ** (-(2.0 * jnp.arange(half_dim, dtype=jnp.float32)) / head_dim)
    angle = jnp.arange(length, dtype=jnp.float32)[:, None] * freq[None, :]
    return (jnp.cos(angle)[:, None, :], jnp.sin(angle)[:, None, :])

def rotate(values, cosine, sine):
    half_dim = values.shape[-1] // 2
    first_half = values[..., :half_dim]
    second_half = values[..., half_dim:]
    return jnp.concatenate([first_half * cosine - second_half * sine, second_half * cosine + first_half * sine], axis=-1)

def reduce_rank(rows, stack, one_hot):
    full = jnp.einsum('ti,aki->tak', rows, stack, precision=HIGHEST)
    return jnp.einsum('tak,a->tk', full, one_hot, precision=HIGHEST)

def expand_rank(latent, stack, one_hot):
    widened = one_hot[None, :, None] * latent[:, None, :]
    return jnp.einsum('tak,ako->to', widened, stack, precision=HIGHEST)

def attend(query, keys, values, labels):
    length = query.shape[1]
    block = min(512, length)
    count = length // block
    scale = query.shape[2] ** (-0.5)

    def one_block(index):
        start = index * block
        rows = lax.dynamic_slice_in_dim(query, start, block, 1)
        row_labels = lax.dynamic_slice_in_dim(labels, start, block, 0)
        raw = low_back(jnp.einsum('hqd,hkd->hqk', rows, keys, precision=HIGHEST))
        scores = raw * scale
        same = row_labels[:, None] == labels[None, :]
        scores = jnp.where(same[None], scores, -1e+30)
        weights = low(jax.nn.softmax(scores, axis=-1))
        return jnp.einsum('hqk,hkd->hqd', weights, values, precision=HIGHEST)
    blocks = lax.map(jax.checkpoint(one_block), jnp.arange(count, dtype=jnp.int32))
    return jnp.transpose(blocks, (1, 0, 2, 3)).reshape(query.shape)

def layer(inputs, weights, adapters, one_hot, labels, cosine, sine):
    w_qkv, w_out, w_gate_up, w_down, ln_gain, ln_bias = weights
    qkv_a, qkv_b, out_a, out_b, ffn_a, ffn_b, down_a, down_b = adapters
    rank = out_b.shape[1]
    length = inputs.shape[0]
    latent = low_back(low(reduce_rank(inputs, qkv_a, one_hot)))
    parts = []
    for part in range(3):
        piece = latent[:, part * rank:(part + 1) * rank]
        parts.append(matmul(inputs, w_qkv[part]) + expand_rank(piece, qkv_b[:, part * rank:(part + 1) * rank], one_hot))
    query = low_back(parts[0]).reshape(length, HEADS, HEAD_DIM)
    keys = low_back(parts[1]).reshape(length, HEADS, HEAD_DIM)
    query = low_back(low(rotate(query, cosine, sine)))
    keys = low_back(low(rotate(keys, cosine, sine)))
    values = low_back(low(parts[2])).reshape(length, HEADS, HEAD_DIM)
    mixed = attend(jnp.transpose(query, (1, 0, 2)), jnp.transpose(keys, (1, 0, 2)), jnp.transpose(values, (1, 0, 2)), labels)
    mixed = jnp.transpose(mixed, (1, 0, 2)).reshape(length, D)
    mixed = low_back(low(mixed))
    latent_out = low_back(low(reduce_rank(mixed, out_a, one_hot)))
    branch = low_back(matmul(mixed, w_out) + expand_rank(latent_out, out_b, one_hot))
    hidden = norm_rows(inputs + branch, ln_gain[0], ln_bias[0])
    hidden_low = low(hidden)
    latent_ffn = low_back(low(reduce_rank(hidden_low, ffn_a, one_hot)))
    gate = low_back(matmul(hidden_low, w_gate_up[0]) + expand_rank(latent_ffn[:, :rank], ffn_b[:, :rank], one_hot))
    upward = low_back(matmul(hidden_low, w_gate_up[1]) + expand_rank(latent_ffn[:, rank:], ffn_b[:, rank:], one_hot))
    active = low(jax.nn.silu(gate) * upward)
    latent_down = low_back(low(reduce_rank(active, down_a, one_hot)))
    branch_ffn = low_back(matmul(active, w_down) + expand_rank(latent_down, down_b, one_hot))
    return norm_rows(hidden + branch_ffn, ln_gain[1], ln_bias[1])

def reference(layer_input, output_grad, segments, adapter_ids, ln_gain, ln_bias, w_qkv, w_out, w_gate_up, w_down, qkv_a, qkv_b, out_a, out_b, ffn_a, ffn_b, down_a, down_b):
    weights = (w_qkv.astype(jnp.float32), w_out.astype(jnp.float32), w_gate_up.astype(jnp.float32), w_down.astype(jnp.float32), ln_gain.astype(jnp.float32), ln_bias.astype(jnp.float32))
    adapters = (qkv_a.astype(jnp.float32), qkv_b.astype(jnp.float32), out_a.astype(jnp.float32), out_b.astype(jnp.float32), ffn_a.astype(jnp.float32), ffn_b.astype(jnp.float32), down_a.astype(jnp.float32), down_b.astype(jnp.float32))
    one_hot = (adapter_ids[:, 0][:, None] == jnp.arange(ADAPTERS, dtype=jnp.int32)[None, :]).astype(jnp.float32)
    cosine, sine = tables(LEN, HEAD_DIM)
    inputs = layer_input.astype(jnp.float32).reshape(SEQS, LEN, D)
    cotangents = output_grad.astype(jnp.float32).reshape(SEQS, LEN, D)

    def one_sequence(totals, item):
        seq_inputs, seq_cotangent, seq_labels, seq_hot = item

        def forward(layer_in, adapter_set):
            return layer(layer_in, weights, adapter_set, seq_hot, seq_labels, cosine, sine)
        result, pullback = jax.vjp(forward, seq_inputs, adapters)
        grad_in, grad_adapters = pullback(seq_cotangent)
        return (jax.tree.map(jnp.add, totals, grad_adapters), (result, grad_in))
    zeros = jax.tree.map(jnp.zeros_like, adapters)
    totals, (results, grads) = lax.scan(one_sequence, zeros, (inputs, cotangents, segments, one_hot))
    return (results.reshape(TOKENS, D).astype(jnp.bfloat16), grads.reshape(TOKENS, D), totals[0], totals[1], totals[2], totals[3], totals[4], totals[5], totals[6], totals[7])
```

```python
import jax
import jax.numpy as jnp
import numpy as np
from jax import lax
from jax.experimental import pallas as pl
from jax.experimental.pallas import tpu as pltpu
from jax.sharding import Mesh
from jax.sharding import PartitionSpec as P

HEAD_DIM = 64
LANES = 128
DP = ("yx", "core")
ALL = ("tensor", "yx", "core")
F32 = jnp.float32
BF16 = jnp.bfloat16


def nt(left, right):
    return lax.dot_general(left, right, (((1,), (1,)), ((), ())), preferred_element_type=F32)


def tn(left, right):
    return lax.dot_general(left, right, (((0,), (0,)), ((), ())), preferred_element_type=F32)


def nn(left, right):
    return jnp.dot(left, right, preferred_element_type=F32)


def roll_rows(rows, shift, count, dtype):
    length, width = rows.shape
    block = LANES
    blocks = length // block
    shift = lax.rem(shift + length, length)
    first = shift // block
    scalars = jnp.stack([first, shift - first * block]).astype(jnp.int32)

    def kernel(scalar_ref, low_ref, high_ref, out_ref):
        offset = scalar_ref[1]
        row = lax.broadcasted_iota(jnp.int32, (block, block), 0)
        column = lax.broadcasted_iota(jnp.int32, (block, block), 1)
        low = jnp.where(column == row + offset, 1.0, 0.0).astype(BF16)
        high = jnp.where(column + block == row + offset, 1.0, 0.0).astype(BF16)
        out_ref[...] = (nn(low, low_ref[...]) + nn(high, high_ref[...])).astype(dtype)

    return pl.pallas_call(
        kernel,
        grid_spec=pltpu.PrefetchScalarGridSpec(
            num_scalar_prefetch=1,
            grid=(count // block,),
            in_specs=[
                pl.BlockSpec((block, width), lambda i, s: (lax.rem(s[0] + i, blocks), 0)),
                pl.BlockSpec((block, width), lambda i, s: (lax.rem(s[0] + i + 1, blocks), 0)),
            ],
            out_specs=pl.BlockSpec((block, width), lambda i, s: (i, 0)),
        ),
        out_shape=jax.ShapeDtypeStruct((count, width), dtype),
        cost_estimate=pl.CostEstimate(
            flops=4 * count * block * width, bytes_accessed=8 * count * width, transcendentals=0
        ),
        name="roll_rows",
    )(scalars, rows, rows)


def spin(values, cosine, sine):
    lane = lax.broadcasted_iota(jnp.int32, (1, LANES), 1)
    first = lax.rem(lane, HEAD_DIM) < HEAD_DIM // 2
    parts = []
    for start in range(0, values.shape[1], LANES):
        piece = values[:, start : start + LANES]
        ahead = pltpu.roll(piece, LANES - HEAD_DIM // 2, 1)
        behind = pltpu.roll(piece, HEAD_DIM // 2, 1)
        parts.append(piece * cosine + jnp.where(first, ahead, behind) * sine)
    return parts[0] if len(parts) == 1 else jnp.concatenate(parts, axis=1)


def project_qkv(group, own, weights, latent, latent_own, factors, tables, tables_own):
    shards, _, width, local = weights.shape
    count, total = own.shape[0], group.shape[0]
    rank = latent.shape[1] // 3
    scale = HEAD_DIM ** (-0.5)

    def kernel(x_ref, o_ref, w_ref, l_ref, lo_ref, f_ref, c_ref, s_ref, co_ref, so_ref, q_ref, k_ref, v_ref):
        x = x_ref[...]
        lat = l_ref[...]
        factor = f_ref[...]
        query = nn(o_ref[...], w_ref[0, 0]) + nn(lo_ref[...][:, :rank], factor[:rank])
        q_ref[...] = (spin(query, co_ref[...], so_ref[...]).astype(BF16) * scale).astype(BF16)
        key = nn(x, w_ref[0, 1]) + nn(lat[:, rank : 2 * rank], factor[rank : 2 * rank])
        k_ref[...] = spin(key, c_ref[...], s_ref[...]).astype(BF16)
        value = nn(x, w_ref[0, 2]) + nn(lat[:, 2 * rank :], factor[2 * rank :])
        v_ref[...] = value.astype(BF16)

    def whole(array):
        return pl.BlockSpec(array.shape, lambda i: (0,) * array.ndim)

    def columns(rows):
        return pl.BlockSpec((rows, local), lambda i: (0, i))

    cosine, sine = tables
    cosine_own, sine_own = tables_own
    return pl.pallas_call(
        kernel,
        grid=(shards,),
        in_specs=[
            whole(group),
            whole(own),
            pl.BlockSpec((1, 3, width, local), lambda i: (i, 0, 0, 0)),
            whole(latent),
            whole(latent_own),
            columns(factors.shape[0]),
            whole(cosine),
            whole(sine),
            whole(cosine_own),
            whole(sine_own),
        ],
        out_specs=[columns(count), columns(total), columns(total)],
        out_shape=[
            jax.ShapeDtypeStruct((count, width), BF16),
            jax.ShapeDtypeStruct((total, width), BF16),
            jax.ShapeDtypeStruct((total, width), BF16),
        ],
        cost_estimate=pl.CostEstimate(
            flops=2 * width * width * (count + 2 * total),
            bytes_accessed=2 * (4 * width * width + 6 * total * width),
            transcendentals=0,
        ),
        name="project_qkv",
    )(group, own, weights, latent, latent_own, factors, cosine, sine, cosine_own, sine_own)


def head_lanes():
    return lax.broadcasted_iota(jnp.int32, (1, LANES), 1) // HEAD_DIM


def attend(query, keys, values, labels_own, labels):
    count, width = query.shape
    total = keys.shape[0]
    pairs = width // LANES

    def kernel(q_ref, k_ref, v_ref, own_ref, all_ref, out_ref, log_ref):
        q = q_ref[...]
        k = k_ref[...]
        flipped = v_ref[...].astype(F32).T
        same = all_ref[...] == own_ref[...]
        lanes = head_lanes()
        sides = lax.broadcasted_iota(jnp.int32, (LANES, 1), 0) // HEAD_DIM
        outs = []
        logs = []
        for head in range(2):
            masked = jnp.where(lanes == head, q, jnp.zeros_like(q))
            scores = jnp.where(same, nt(k, masked), -1e30)
            top = jnp.max(scores, axis=0, keepdims=True)
            expo = jnp.exp(scores - top).astype(BF16)
            stacked = jnp.where(sides == head, flipped, 1.0).astype(BF16)
            product = nn(stacked, expo)
            other = (1 - head) * HEAD_DIM
            weight_sum = product[other : other + 1]
            outs.append(product[head * HEAD_DIM : (head + 1) * HEAD_DIM] / weight_sum)
            logs.append(top + jnp.log(weight_sum))
        out_ref[...] = jnp.concatenate(outs, axis=0).T.astype(BF16)
        log_ref[0, 0:1] = logs[0]
        log_ref[0, 1:2] = logs[1]

    pair = lambda rows: pl.BlockSpec((rows, LANES), lambda i: (0, i))
    return pl.pallas_call(
        kernel,
        grid=(pairs,),
        in_specs=[
            pair(count),
            pair(total),
            pair(total),
            pl.BlockSpec((1, count), lambda i: (0, 0)),
            pl.BlockSpec((total, 1), lambda i: (0, 0)),
        ],
        out_specs=[pair(count), pl.BlockSpec((1, 8, count), lambda i: (i, 0, 0))],
        out_shape=[
            jax.ShapeDtypeStruct((count, width), BF16),
            jax.ShapeDtypeStruct((pairs, 8, count), F32),
        ],
        cost_estimate=pl.CostEstimate(
            flops=16 * count * total * width,
            bytes_accessed=4 * (count + total) * width,
            transcendentals=2 * pairs * count * total,
        ),
        name="attend",
    )(query, keys, values, labels_own[None, :], labels[:, None])


def attend_back(query, keys, values, mixed, grads, logs, labels_own, labels, tables, tables_own):
    count, width = query.shape
    total = keys.shape[0]
    pairs = width // LANES
    scale = HEAD_DIM ** (-0.5)
    cosine, sine = tables
    cosine_own, sine_own = tables_own

    def kernel(q_ref, k_ref, v_ref, m_ref, g_ref, log_ref, own_ref, all_ref, c_ref, s_ref, co_ref, so_ref, dq_ref, dk_ref, dv_ref):
        q = q_ref[...]
        k = k_ref[...]
        v = v_ref[...]
        g = g_ref[...]
        same = all_ref[...] == own_ref[...]
        lanes = head_lanes()
        sides = lax.broadcasted_iota(jnp.int32, (LANES, 1), 0) // HEAD_DIM
        k_flipped = k.astype(F32).T
        product = g.astype(F32) * m_ref[...].astype(F32)
        high = product.astype(BF16)
        low = (product - high.astype(F32)).astype(BF16)
        picks = (
            lax.broadcasted_iota(jnp.int32, (8, LANES), 1) // HEAD_DIM
            == lax.broadcasted_iota(jnp.int32, (8, LANES), 0)
        ).astype(F32).astype(BF16)
        delta = nt(picks, high) + nt(picks, low)
        dq = jnp.zeros((LANES, count), F32)
        dk = jnp.zeros((total, LANES), F32)
        dv = jnp.zeros((total, LANES), F32)
        for head in range(2):
            q_masked = jnp.where(lanes == head, q, jnp.zeros_like(q))
            g_masked = jnp.where(lanes == head, g, jnp.zeros_like(g))
            scores = jnp.where(same, nt(k, q_masked), -1e30)
            prob = jnp.exp(scores - log_ref[0, head : head + 1])
            grad_prob = nt(v, g_masked)
            grad_score = (prob * (grad_prob - delta[head : head + 1])).astype(BF16)
            dv = dv + nn(prob.astype(BF16), g_masked)
            dk = dk + nn(grad_score, q_masked)
            k_side = jnp.where(sides == head, k_flipped, 0.0).astype(BF16)
            dq = dq + nn(k_side, grad_score)
        dq_ref[...] = spin(dq.T * scale, co_ref[...], -so_ref[...]).astype(BF16)
        dk_ref[...] = spin(dk, c_ref[...], -s_ref[...]).astype(BF16)
        dv_ref[...] = dv.astype(BF16)

    pair = lambda rows: pl.BlockSpec((rows, LANES), lambda i: (0, i))

    def whole(array):
        return pl.BlockSpec(array.shape, lambda i: (0,) * array.ndim)

    labels_own = labels_own[None, :]
    labels = labels[:, None]
    return pl.pallas_call(
        kernel,
        grid=(pairs,),
        in_specs=[
            pair(count),
            pair(total),
            pair(total),
            pair(count),
            pair(count),
            pl.BlockSpec((1, 8, count), lambda i: (i, 0, 0)),
            whole(labels_own),
            whole(labels),
            whole(cosine),
            whole(sine),
            whole(cosine_own),
            whole(sine_own),
        ],
        out_specs=[pair(count), pair(total), pair(total)],
        out_shape=[
            jax.ShapeDtypeStruct((count, width), BF16),
            jax.ShapeDtypeStruct((total, width), BF16),
            jax.ShapeDtypeStruct((total, width), BF16),
        ],
        cost_estimate=pl.CostEstimate(
            flops=40 * count * total * width,
            bytes_accessed=2 * (5 * count + 4 * total) * width,
            transcendentals=2 * pairs * count * total,
        ),
        name="attend_back",
    )(query, keys, values, mixed, grads, logs, labels_own, labels, cosine, sine, cosine_own, sine_own)


def norm_forward(rows, gain, shift):
    centre = jnp.mean(rows, axis=-1, keepdims=True)
    centred = rows - centre
    spread = jnp.mean(centred * centred, axis=-1, keepdims=True)
    inverse = lax.rsqrt(spread + 1e-12)
    normed = centred * inverse
    return (normed * gain + shift, normed, inverse)


def norm_backward(grads, normed, inverse, gain):
    scaled = grads * gain
    first_mean = jnp.mean(scaled, axis=-1, keepdims=True)
    second_mean = jnp.mean(scaled * normed, axis=-1, keepdims=True)
    return inverse * (scaled - first_mean - normed * second_mean)


def rope_tables(length, extra):
    half = HEAD_DIM // 2
    step = 64
    freq = 10000.0 ** (-(2.0 * np.arange(half)) / HEAD_DIM)
    freq = np.tile(freq, LANES // half)
    sign = np.where(np.arange(LANES) % HEAD_DIM < half, -1.0, 1.0)
    coarse = ((np.arange(length + extra) % length)[::step, None] * freq).astype(np.float64)
    fine = np.arange(step)[:, None] * freq
    f = lambda array: jnp.asarray(array, F32)
    cos_c, sin_c = f(np.cos(coarse))[:, None], f(np.sin(coarse))[:, None]
    cos_f, sin_f = f(np.cos(fine))[None], f(np.sin(fine))[None]
    cosine = (cos_c * cos_f - sin_c * sin_f).reshape(-1, LANES)
    sine = ((sin_c * cos_f + cos_c * sin_f) * f(sign)).reshape(-1, LANES)
    return cosine, sine


def window(array, start, count):
    return lax.dynamic_slice_in_dim(array, start, count, 0)


def gather_weight(local, parts, part):
    rows = local.shape[0] // parts
    piece = window(local, part * rows, rows)
    return lax.all_gather(piece, ALL, axis=0, tiled=True)


def gather_small(rows, shards, place):
    return lax.all_gather(rows, "tensor", axis=0)


def by_shard(array, shards):
    rows, width = array.shape
    return array.reshape(rows, shards, width // shards).transpose(1, 0, 2)


def reduce_grads(shared, split, hot, unit):
    shards = lax.axis_size("tensor")
    adapters = hot.shape[0]
    pieces = [by_shard(array, shards).reshape(shards, -1, unit) for array in shared + split]
    flag = jnp.zeros((shards, 16, unit), F32).at[:, 0, :adapters].set(hot.astype(F32) / shards)
    packed = jnp.concatenate(pieces + [flag], axis=1).astype(BF16)
    part = lax.psum_scatter(packed, "tensor", scatter_dimension=0, tiled=False)
    every = lax.all_gather(part, DP, axis=0).astype(F32)
    hots = every[:, -16, :adapters]
    placed = jnp.einsum("sj,srn->jrn", hots, every[:, :-16], precision=lax.Precision.HIGHEST)
    sizes = [piece.shape[1] for piece in pieces]
    offsets = np.concatenate([[0], np.cumsum(sizes)])
    cut = offsets[len(shared)]
    outs = []
    if shared:
        whole = lax.all_gather(placed[:, :cut].astype(BF16), "tensor", axis=2, tiled=True).astype(F32)
        for i, array in enumerate(shared):
            outs.append(whole[:, offsets[i] : offsets[i + 1]])
    for i, array in enumerate(split):
        j = len(shared) + i
        outs.append(
            placed[:, offsets[j] : offsets[j + 1]].reshape(adapters, array.shape[0], -1)
        )
    return outs


def body(
    layer_input,
    output_grad,
    segments,
    adapter_ids,
    ln_gain,
    ln_bias,
    w_qkv,
    w_out,
    w_gate_up,
    w_down,
    qkv_a,
    qkv_b,
    out_a,
    out_b,
    ffn_a,
    ffn_b,
    down_a,
    down_b,
):
    seq_count, length = segments.shape
    assert seq_count == 1
    width = layer_input.shape[1]
    shards = lax.axis_size("tensor")
    parts = lax.axis_size(DP)
    place = lax.axis_index("tensor")
    part = lax.axis_index(DP)
    members = shards // 2
    half = length // 2
    count = length // shards
    group = place // members
    member = lax.rem(place, members)
    local = w_qkv.shape[2]
    units = w_down.shape[0]
    rank = out_b.shape[1]

    qkv_all = gather_weight(w_qkv.reshape(3 * width, local), parts, part)
    qkv_all = qkv_all.reshape(shards, 3, width, local)
    out_all = gather_weight(w_out, parts, part)
    up_all = gather_weight(w_gate_up.reshape(2 * width, units), parts, part)
    up_all = up_all.reshape(shards, 2, width, units)
    down_all = gather_weight(w_down, parts, part).reshape(shards, units, width)

    adapter = adapter_ids[0, 0]
    pick = lambda stack: lax.dynamic_index_in_dim(stack, adapter, 0, keepdims=False)
    qa, ob, fa, db = pick(qkv_a), pick(out_b), pick(ffn_a), pick(down_b)
    small = jnp.concatenate(
        [
            pick(qkv_b),
            pick(out_a),
            pick(ffn_b).reshape(-1, local),
            pick(down_a).reshape(-1, local),
        ],
        axis=0,
    )
    small = gather_small(small, shards, place)
    cuts = np.cumsum([3 * rank, rank, 2 * rank * (units // local)])
    rejoin = lambda piece: piece.transpose(1, 0, 2).reshape(piece.shape[1], -1)
    qb = rejoin(small[:, : cuts[0]])
    oa = rejoin(small[:, cuts[0] : cuts[1]])
    fb = small[:, cuts[1] : cuts[2]].reshape(shards, 2 * rank, units)
    da = small[:, cuts[2] :].reshape(shards, rank, units)

    labels = segments[0]
    long = labels[: length - half + 1] == labels[half - 1 :]
    start = jnp.sum(jnp.where(long, jnp.arange(length - half + 1, dtype=jnp.int32), 0))
    group_start = start + group * half
    own_start = start + place * count
    x_group = roll_rows(layer_input, group_start, half, BF16)
    x_own_b = window(x_group, member * count, count)
    x_own = x_own_b.astype(F32)
    cotangent = roll_rows(output_grad, own_start, count, F32)
    labels_twice = jnp.concatenate([labels, labels[:half]])
    labels_group = window(labels_twice, group_start, half)
    labels_own = window(labels_group, member * count, count)
    cosine, sine = rope_tables(length, half)
    tables = (window(cosine, group_start, half), window(sine, group_start, half))
    tables_own = tuple(window(table, member * count, count) for table in tables)

    latent_qkv = nt(x_group, qa).astype(BF16)
    latent_own = window(latent_qkv, member * count, count)
    query, keys, values = project_qkv(
        x_group, x_own_b, qkv_all, latent_qkv, latent_own, qb, tables, tables_own
    )
    mixed, logs = attend(query, keys, values, labels_own, labels_group)
    latent_out = nt(mixed, oa).astype(BF16)
    branch = nn(mixed, out_all) + nn(latent_out, ob)
    hidden, normed_one, inverse_one = norm_forward(x_own + branch, ln_gain[0], ln_bias[0])
    hidden_b = hidden.astype(BF16)

    latent_ffn = nt(hidden_b, fa).astype(BF16)
    gates, ups, actives = [], [], []
    ffn_out = None
    latent_down = None
    for k in range(shards):
        gate = nn(hidden_b, up_all[k, 0]) + nn(latent_ffn[:, :rank], fb[k, :rank])
        up = nn(hidden_b, up_all[k, 1]) + nn(latent_ffn[:, rank:], fb[k, rank:])
        active = (gate * jax.nn.sigmoid(gate) * up).astype(BF16)
        term = nn(active, down_all[k])
        lat = nt(active, da[k])
        ffn_out = term if ffn_out is None else ffn_out + term
        latent_down = lat if latent_down is None else latent_down + lat
        gates.append(gate)
        ups.append(up)
        actives.append(active)
    latent_down = latent_down.astype(BF16)
    ffn_out = ffn_out + nn(latent_down, db)
    result, normed_two, inverse_two = norm_forward(hidden + ffn_out, ln_gain[1], ln_bias[1])
    rolled = lax.all_gather(result.astype(BF16), "tensor", axis=0, tiled=True)
    output = roll_rows(rolled, -start, length, BF16)

    grad_mid = norm_backward(cotangent, normed_two, inverse_two, ln_gain[1])
    grad_ffn = grad_mid.astype(BF16)
    down_b_part = tn(latent_down, grad_ffn)
    latent_down_grad = nt(grad_ffn, db).astype(BF16)
    grad_hidden = grad_mid
    gate_grads, up_grads, down_a_parts = [], [], []
    latent_gate_grad = None
    latent_up_grad = None
    for k in range(shards):
        grad_active = nt(grad_ffn, down_all[k]) + nn(latent_down_grad, da[k])
        sigma = jax.nn.sigmoid(gates[k])
        grad_gate = (grad_active * ups[k] * sigma * (1.0 + gates[k] * (1.0 - sigma))).astype(BF16)
        grad_up = (grad_active * (gates[k] * sigma)).astype(BF16)
        down_a_parts.append(tn(latent_down_grad, actives[k]))
        gate_grads.append(tn(latent_ffn[:, :rank], grad_gate))
        up_grads.append(tn(latent_ffn[:, rank:], grad_up))
        grad_hidden = grad_hidden + nt(grad_gate, up_all[k, 0]) + nt(grad_up, up_all[k, 1])
        one = nt(grad_gate, fb[k, :rank])
        two = nt(grad_up, fb[k, rank:])
        latent_gate_grad = one if latent_gate_grad is None else latent_gate_grad + one
        latent_up_grad = two if latent_up_grad is None else latent_up_grad + two
    latent_ffn_grad = jnp.concatenate([latent_gate_grad, latent_up_grad], axis=1).astype(BF16)
    grad_hidden = grad_hidden + nn(latent_ffn_grad, fa)
    down_a_part = jnp.concatenate(down_a_parts, axis=1)
    ffn_b_part = jnp.concatenate(
        [jnp.concatenate(gate_grads, axis=1), jnp.concatenate(up_grads, axis=1)], axis=0
    )
    ffn_a_part = tn(latent_ffn_grad, hidden_b)
    grad_first = norm_backward(grad_hidden, normed_one, inverse_one, ln_gain[0])
    grad_branch = grad_first.astype(BF16)
    out_b_part = tn(latent_out, grad_branch)
    latent_out_grad = nt(grad_branch, ob).astype(BF16)
    out_a_part = tn(latent_out_grad, mixed)
    grad_mixed = (nt(grad_branch, out_all) + nn(latent_out_grad, oa)).astype(BF16)

    hot = (adapter == jnp.arange(qkv_a.shape[0], dtype=jnp.int32)).astype(F32)
    out_b_grad, ffn_a_grad, down_b_grad, out_a_grad, ffn_b_grad, down_a_grad = reduce_grads(
        [out_b_part, ffn_a_part, down_b_part], [out_a_part, ffn_b_part, down_a_part], hot, local
    )

    dq, dk, dv = attend_back(
        query, keys, values, mixed, grad_mixed, logs, labels_own, labels_group, tables, tables_own
    )
    qb_q, qb_k, qb_v = qb[:rank], qb[rank : 2 * rank], qb[2 * rank :]
    lat_q = nt(dq, qb_q).astype(BF16)
    lat_k = nt(dk, qb_k).astype(BF16)
    lat_v = nt(dv, qb_v).astype(BF16)
    back = nn(lat_k, qa[rank : 2 * rank]) + nn(lat_v, qa[2 * rank :])
    back_own = nn(lat_q, qa[:rank])
    for k in range(shards):
        cols = slice(k * local, (k + 1) * local)
        back = back + nt(dk[:, cols], qkv_all[k, 1]) + nt(dv[:, cols], qkv_all[k, 2])
        back_own = back_own + nt(dq[:, cols], qkv_all[k, 0])
    qkv_b_part = jnp.concatenate(
        [
            tn(latent_own[:, :rank], dq),
            tn(latent_qkv[:, rank : 2 * rank], dk),
            tn(latent_qkv[:, 2 * rank :], dv),
        ],
        axis=0,
    )
    qkv_a_part = jnp.concatenate([tn(lat_q, x_own_b), tn(lat_k, x_group), tn(lat_v, x_group)], axis=0)
    back_b = back.astype(BF16)
    grad_input = grad_first + back_own + window(back, member * count, count)
    for d in range(1, members):
        target = lax.rem(member + d, members)
        sent = window(back_b, target * count, count)
        links = [
            (g * members + i, g * members + (i + d) % members)
            for g in range(2)
            for i in range(members)
        ]
        grad_input = grad_input + lax.ppermute(sent, "tensor", links).astype(F32)
    grad_rolled = lax.all_gather(grad_input.astype(BF16), "tensor", axis=0, tiled=True)
    grad_whole = roll_rows(grad_rolled, -start, length, F32)
    qkv_a_grad, qkv_b_grad = reduce_grads([qkv_a_part], [qkv_b_part], hot, local)
    return (
        output,
        grad_whole,
        qkv_a_grad,
        qkv_b_grad,
        out_a_grad,
        out_b_grad,
        ffn_a_grad,
        ffn_b_grad,
        down_a_grad,
        down_b_grad,
    )


def solution(mesh):
    devices = mesh.devices
    mesh = Mesh(
        devices.reshape(devices.shape[0] // 2, 2, devices.shape[1]), ("yx", "core", "tensor")
    )
    in_specs = (
        P(DP, None),
        P(DP, None),
        P(DP, None),
        P(DP, None),
        P(),
        P(),
        P(None, None, "tensor"),
        P("tensor", None),
        P(None, None, "tensor"),
        P("tensor", None),
        P(),
        P(None, None, "tensor"),
        P(None, None, "tensor"),
        P(),
        P(),
        P(None, None, "tensor"),
        P(None, None, "tensor"),
        P(),
    )
    out_specs = (
        P(DP, None),
        P(DP, None),
        P(),
        P(None, None, "tensor"),
        P(None, None, "tensor"),
        P(),
        P(),
        P(None, None, "tensor"),
        P(None, None, "tensor"),
        P(),
    )
    return jax.shard_map(body, mesh=mesh, in_specs=in_specs, out_specs=out_specs, check_vma=False)
```

```python
import jax
import jax.numpy as jnp
import numpy as np
from jax import lax
from jax.experimental import pallas as pl
from jax.experimental.pallas import tpu as pltpu
from jax.sharding import Mesh
from jax.sharding import PartitionSpec as P


HEAD_DIM = 64
LANES = 128
DP = ("yx", "core")
ALL = ("tensor", "yx", "core")
F32 = jnp.float32
BF16 = jnp.bfloat16


def nt(left, right):
    return lax.dot_general(left, right, (((1,), (1,)), ((), ())), preferred_element_type=F32)


def tn(left, right):
    return lax.dot_general(left, right, (((0,), (0,)), ((), ())), preferred_element_type=F32)


def nn(left, right):
    return jnp.dot(left, right, preferred_element_type=F32)


def roll_rows(pieces, place, shift, count, dtype):
    number = len(pieces)
    size, width = pieces[0].shape
    length = number * size
    unit = LANES
    units = length // unit
    block = min(512, count)
    shift = lax.rem(shift + length, length)
    first = shift // unit
    scalars = jnp.stack([first, shift - first * unit, place]).astype(jnp.int32)

    def kernel(scalar_ref, *refs):
        out_ref = refs[number]
        step = pl.program_id(0)
        if number > 1:
            rows_ref = refs[number + 1]

            @pl.when(step == 0)
            def _():
                for k in range(number):
                    member = lax.rem(scalar_ref[2] + (number - k), number)
                    rows_ref[pl.ds(pl.multiple_of(member * size, size), size)] = refs[k][...]
        else:
            rows_ref = refs[0]
        offset = scalar_ref[1]
        row = lax.broadcasted_iota(jnp.int32, (unit, 2 * unit), 0)
        column = lax.broadcasted_iota(jnp.int32, (unit, 2 * unit), 1)
        move = jnp.where(column == row + offset, 1.0, 0.0).astype(BF16)
        for s in range(block // unit):
            base = scalar_ref[0] + step * (block // unit) + s
            low = rows_ref[pl.ds(pl.multiple_of(lax.rem(base, units) * unit, unit), unit)]
            high = rows_ref[pl.ds(pl.multiple_of(lax.rem(base + 1, units) * unit, unit), unit)]
            pair = jnp.concatenate([low, high], axis=0)
            out_ref[s * unit : (s + 1) * unit] = nn(move, pair).astype(dtype)

    return pl.pallas_call(
        kernel,
        grid_spec=pltpu.PrefetchScalarGridSpec(
            num_scalar_prefetch=1,
            grid=(count // block,),
            in_specs=[pl.BlockSpec((size, width), lambda i, s: (0, 0))] * number,
            out_specs=pl.BlockSpec((block, width), lambda i, s: (i, 0)),
            scratch_shapes=[pltpu.VMEM((length, width), BF16)] if number > 1 else [],
        ),
        out_shape=jax.ShapeDtypeStruct((count, width), dtype),
        cost_estimate=pl.CostEstimate(
            flops=4 * count * unit * width,
            bytes_accessed=2 * length * width + 4 * count * width,
            transcendentals=0,
        ),
        name="roll_rows",
    )(scalars, *pieces)


def spin(values, cosine, sine):
    lane = lax.broadcasted_iota(jnp.int32, (1, LANES), 1)
    first = lax.rem(lane, HEAD_DIM) < HEAD_DIM // 2
    parts = []
    for start in range(0, values.shape[1], LANES):
        piece = values[:, start : start + LANES]
        ahead = pltpu.roll(piece, LANES - HEAD_DIM // 2, 1)
        behind = pltpu.roll(piece, HEAD_DIM // 2, 1)
        parts.append(piece * cosine + jnp.where(first, ahead, behind) * sine)
    return parts[0] if len(parts) == 1 else jnp.concatenate(parts, axis=1)


def project_qkv(group, own, weights, latent, latent_own, factors, tables, tables_own):
    shards, _, width, local = weights.shape
    count, total = own.shape[0], group.shape[0]
    rank = latent.shape[1] // 3
    scale = HEAD_DIM ** (-0.5)

    def kernel(x_ref, o_ref, w_ref, l_ref, lo_ref, f_ref, c_ref, s_ref, co_ref, so_ref, q_ref, k_ref, v_ref):
        x = x_ref[...]
        lat = l_ref[...]
        factor = f_ref[...]
        query = nn(o_ref[...], w_ref[0, 0]) + nn(lo_ref[...][:, :rank], factor[:rank])
        q_ref[...] = (spin(query, co_ref[...], so_ref[...]).astype(BF16) * scale).astype(BF16)
        key = nn(x, w_ref[0, 1]) + nn(lat[:, rank : 2 * rank], factor[rank : 2 * rank])
        k_ref[...] = spin(key, c_ref[...], s_ref[...]).astype(BF16)
        value = nn(x, w_ref[0, 2]) + nn(lat[:, 2 * rank :], factor[2 * rank :])
        v_ref[...] = value.astype(BF16)

    def whole(array):
        return pl.BlockSpec(array.shape, lambda i: (0,) * array.ndim)

    def columns(rows):
        return pl.BlockSpec((rows, local), lambda i: (0, i))

    cosine, sine = tables
    cosine_own, sine_own = tables_own
    return pl.pallas_call(
        kernel,
        grid=(shards,),
        in_specs=[
            whole(group),
            whole(own),
            pl.BlockSpec((1, 3, width, local), lambda i: (i, 0, 0, 0)),
            whole(latent),
            whole(latent_own),
            columns(factors.shape[0]),
            whole(cosine),
            whole(sine),
            whole(cosine_own),
            whole(sine_own),
        ],
        out_specs=[columns(count), columns(total), columns(total)],
        out_shape=[
            jax.ShapeDtypeStruct((count, width), BF16),
            jax.ShapeDtypeStruct((total, width), BF16),
            jax.ShapeDtypeStruct((total, width), BF16),
        ],
        cost_estimate=pl.CostEstimate(
            flops=2 * width * width * (count + 2 * total),
            bytes_accessed=2 * (4 * width * width + 6 * total * width),
            transcendentals=0,
        ),
        name="project_qkv",
    )(group, own, weights, latent, latent_own, factors, cosine, sine, cosine_own, sine_own)


def head_lanes():
    return lax.broadcasted_iota(jnp.int32, (1, LANES), 1) // HEAD_DIM


def attend(query, keys, values, labels_own, labels):
    count, width = query.shape
    total = keys.shape[0]
    pairs = width // LANES

    def kernel(q_ref, k_ref, v_ref, own_ref, all_ref, out_ref, log_ref):
        q = q_ref[...]
        k = k_ref[...]
        flipped = v_ref[...].astype(F32).T
        same = all_ref[...] == own_ref[...]
        lanes = head_lanes()
        sides = lax.broadcasted_iota(jnp.int32, (LANES, 1), 0) // HEAD_DIM
        outs = []
        logs = []
        for head in range(2):
            masked = jnp.where(lanes == head, q, jnp.zeros_like(q))
            scores = jnp.where(same, nt(k, masked), -1e30)
            top = jnp.max(scores, axis=0, keepdims=True)
            expo = jnp.exp(scores - top).astype(BF16)
            stacked = jnp.where(sides == head, flipped, 1.0).astype(BF16)
            product = nn(stacked, expo)
            other = (1 - head) * HEAD_DIM
            weight_sum = product[other : other + 1]
            outs.append(product[head * HEAD_DIM : (head + 1) * HEAD_DIM] / weight_sum)
            logs.append(top + jnp.log(weight_sum))
        out_ref[...] = jnp.concatenate(outs, axis=0).T.astype(BF16)
        log_ref[0, 0:1] = logs[0]
        log_ref[0, 1:2] = logs[1]

    pair = lambda rows: pl.BlockSpec((rows, LANES), lambda i: (0, i))
    return pl.pallas_call(
        kernel,
        grid=(pairs,),
        in_specs=[
            pair(count),
            pair(total),
            pair(total),
            pl.BlockSpec((1, count), lambda i: (0, 0)),
            pl.BlockSpec((total, 1), lambda i: (0, 0)),
        ],
        out_specs=[pair(count), pl.BlockSpec((1, 8, count), lambda i: (i, 0, 0))],
        out_shape=[
            jax.ShapeDtypeStruct((count, width), BF16),
            jax.ShapeDtypeStruct((pairs, 8, count), F32),
        ],
        cost_estimate=pl.CostEstimate(
            flops=16 * count * total * width,
            bytes_accessed=4 * (count + total) * width,
            transcendentals=2 * pairs * count * total,
        ),
        name="attend",
    )(query, keys, values, labels_own[None, :], labels[:, None])


def attend_back(query, keys, values, mixed, grads, logs, labels_own, labels, tables, tables_own, block, before, last):
    count, width = query.shape
    pairs = width // LANES
    scale = HEAD_DIM ** (-0.5)
    cosine, sine = tables
    cosine_own, sine_own = tables_own
    chained = before is not None

    def kernel(block_ref, q_ref, k_ref, v_ref, m_ref, g_ref, log_ref, own_ref, all_ref, c_ref, s_ref, co_ref, so_ref, *rest):
        before_ref = rest[0] if chained else None
        dq_ref, dk_ref, dv_ref = rest[-3:]
        q = q_ref[...]
        k = k_ref[...]
        v = v_ref[...]
        g = g_ref[...]
        same = all_ref[...] == own_ref[...]
        lanes = head_lanes()
        sides = lax.broadcasted_iota(jnp.int32, (LANES, 1), 0) // HEAD_DIM
        k_flipped = k.astype(F32).T
        product = g.astype(F32) * m_ref[...].astype(F32)
        high = product.astype(BF16)
        low = (product - high.astype(F32)).astype(BF16)
        picks = (
            lax.broadcasted_iota(jnp.int32, (8, LANES), 1) // HEAD_DIM
            == lax.broadcasted_iota(jnp.int32, (8, LANES), 0)
        ).astype(F32).astype(BF16)
        delta = nt(picks, high) + nt(picks, low)
        dq = jnp.zeros((LANES, count), F32)
        dk = jnp.zeros((count, LANES), F32)
        dv = jnp.zeros((count, LANES), F32)
        for head in range(2):
            q_masked = jnp.where(lanes == head, q, jnp.zeros_like(q))
            g_masked = jnp.where(lanes == head, g, jnp.zeros_like(g))
            scores = jnp.where(same, nt(k, q_masked), -1e30)
            prob = jnp.exp(scores - log_ref[0, head : head + 1])
            grad_prob = nt(v, g_masked)
            grad_score = (prob * (grad_prob - delta[head : head + 1])).astype(BF16)
            dv = dv + nn(prob.astype(BF16), g_masked)
            dk = dk + nn(grad_score, q_masked)
            k_side = jnp.where(sides == head, k_flipped, 0.0).astype(BF16)
            dq = dq + nn(k_side, grad_score)
        dq = dq.T * scale
        if chained:
            dq = dq + before_ref[...]
        dq_ref[...] = spin(dq, co_ref[...], -so_ref[...]).astype(BF16) if last else dq
        dk_ref[...] = spin(dk, c_ref[...], -s_ref[...]).astype(BF16)
        dv_ref[...] = dv.astype(BF16)

    pair = pl.BlockSpec((count, LANES), lambda i, s: (0, i))
    chosen = pl.BlockSpec((count, LANES), lambda i, s: (s[0], i))
    rows = lambda array: pl.BlockSpec((count, array.shape[1]), lambda i, s: (s[0], 0))
    whole = lambda array: pl.BlockSpec(array.shape, lambda i, s: (0,) * array.ndim)
    labels_own = labels_own[None, :]
    labels = labels[:, None]
    operands = [query, keys, values, mixed, grads, logs, labels_own, labels, cosine, sine, cosine_own, sine_own]
    specs = [
        pair,
        chosen,
        chosen,
        pair,
        pair,
        pl.BlockSpec((1, 8, count), lambda i, s: (i, 0, 0)),
        whole(labels_own),
        rows(labels),
        rows(cosine),
        rows(sine),
        whole(cosine_own),
        whole(sine_own),
    ]
    if chained:
        operands.append(before)
        specs.append(pair)
    return pl.pallas_call(
        kernel,
        grid_spec=pltpu.PrefetchScalarGridSpec(
            num_scalar_prefetch=1, grid=(pairs,), in_specs=specs, out_specs=[pair] * 3
        ),
        out_shape=[
            jax.ShapeDtypeStruct((count, width), BF16 if last else F32),
            jax.ShapeDtypeStruct((count, width), BF16),
            jax.ShapeDtypeStruct((count, width), BF16),
        ],
        cost_estimate=pl.CostEstimate(
            flops=40 * count * count * width,
            bytes_accessed=2 * 9 * count * width,
            transcendentals=2 * pairs * count * count,
        ),
        name="attend_back",
    )(jnp.reshape(block, (1,)), *operands)


def project_back(grads, first, weights, factors, outer, latent, rows, block, base, before):
    shards, _, width, local = weights.shape
    count = grads[0].shape[0]
    rank = factors.shape[0] // 3
    number = len(grads)
    based = base is not None
    added = before is not None
    depth = number * rank

    def kernel(block_ref, w_ref, f_ref, a_ref, l_ref, x_ref, *rest):
        g_refs = rest[:number]
        base_ref = rest[number] if based else None
        before_ref = rest[number + based] if added else None
        out_ref, part_ref, acc_ref, lat_ref, b_ref = rest[-5:]
        step = pl.program_id(0)

        @pl.when(step == 0)
        def _():
            acc_ref[...] = base_ref[...] if based else jnp.zeros_like(acc_ref)
            lat_ref[...] = jnp.zeros_like(lat_ref)

        total = acc_ref[...]
        lats = []
        parts = []
        for j in range(number):
            p = first + j
            g = g_refs[j][...]
            total = total + nt(g, w_ref[0, p])
            lats.append(nt(g, f_ref[p * rank : (p + 1) * rank]))
            parts.append(tn(l_ref[:, p * rank : (p + 1) * rank], g))
        acc_ref[...] = total
        lat_ref[...] += jnp.concatenate(lats, axis=1)
        b_ref[step] = jnp.concatenate(parts, axis=0)

        @pl.when(step == shards - 1)
        def _():
            lat = lat_ref[...].astype(BF16)
            final = acc_ref[...] + nn(lat, a_ref[first * rank :])
            out_ref[...] = final.astype(out_ref.dtype)
            part = jnp.concatenate([b_ref[t] for t in range(shards)], axis=1)
            part = jnp.concatenate([part, tn(lat, x_ref[...])], axis=0)
            if added:
                other = before_ref[...]
                none = jnp.zeros((rank, width), F32)
                size = depth - rank
                part = part + jnp.concatenate([none, other[:size], none, other[size:]], axis=0)
            part_ref[...] = part.astype(part_ref.dtype)

    whole = lambda array: pl.BlockSpec(array.shape, lambda i, s: (0,) * array.ndim)
    chosen = lambda array: pl.BlockSpec((count, array.shape[1]), lambda i, s: (s[0], 0))
    columns = lambda size: pl.BlockSpec((size, local), lambda i, s: (0, i))
    fixed = lambda size: pl.BlockSpec((size, width), lambda i, s: (0, 0))
    operands = [weights, factors, outer, latent, rows, *grads]
    specs = [
        pl.BlockSpec((1, 3, width, local), lambda i, s: (i, 0, 0, 0)),
        columns(3 * rank),
        whole(outer),
        chosen(latent),
        chosen(rows),
        *[columns(count) for _ in grads],
    ]
    if based:
        operands.append(base)
        specs.append(fixed(count))
    if added:
        operands.append(before)
        specs.append(whole(before))
    return pl.pallas_call(
        kernel,
        grid_spec=pltpu.PrefetchScalarGridSpec(
            num_scalar_prefetch=1,
            grid=(shards,),
            in_specs=specs,
            out_specs=[fixed(count), fixed(2 * depth)],
            scratch_shapes=[
                pltpu.VMEM((count, width), F32),
                pltpu.VMEM((count, depth), F32),
                pltpu.VMEM((shards, depth, local), F32),
            ],
        ),
        out_shape=[
            jax.ShapeDtypeStruct((count, width), F32 if based else BF16),
            jax.ShapeDtypeStruct((2 * depth, width), BF16 if based else F32),
        ],
        cost_estimate=pl.CostEstimate(
            flops=2 * number * count * width * width,
            bytes_accessed=6 * width * width + 2 * (number + 4) * count * width,
            transcendentals=0,
        ),
        name="project_back",
    )(jnp.reshape(block, (1,)), *operands)


def out_forward(mixed, weights, outer, factors, rows, gain, shift, next_factors):
    count, width = mixed.shape
    rank = factors.shape[0]

    def kernel(m_ref, w_ref, a_ref, b_ref, x_ref, g_ref, s_ref, f_ref, hid_ref, hidb_ref, n_ref, i_ref, lo_ref, lf_ref):
        m = m_ref[...]
        latent = nt(m, a_ref[...]).astype(BF16)
        total = x_ref[...].astype(F32) + nn(m, w_ref[...]) + nn(latent, b_ref[...])
        hidden, normed, inverse = norm_forward(total, g_ref[...], s_ref[...])
        hid_ref[...] = hidden
        hidden_b = hidden.astype(BF16)
        hidb_ref[...] = hidden_b
        n_ref[...] = normed
        i_ref[...] = inverse
        lo_ref[...] = latent
        lf_ref[...] = nt(hidden_b, f_ref[...]).astype(BF16)

    full = lambda array: pl.BlockSpec(array.shape, lambda i: (0,) * array.ndim)
    block = min(256, count)
    part = lambda size: pl.BlockSpec((block, size), lambda i: (i, 0))
    operands = [mixed, weights, outer, factors, rows, gain, shift, next_factors]
    return pl.pallas_call(
        kernel,
        grid=(count // block,),
        in_specs=[
            part(width),
            full(weights),
            full(outer),
            full(factors),
            part(width),
            full(gain),
            full(shift),
            full(next_factors),
        ],
        out_specs=[part(width), part(width), part(width), part(1), part(rank), part(2 * rank)],
        out_shape=[
            jax.ShapeDtypeStruct((count, width), F32),
            jax.ShapeDtypeStruct((count, width), BF16),
            jax.ShapeDtypeStruct((count, width), F32),
            jax.ShapeDtypeStruct((count, 1), F32),
            jax.ShapeDtypeStruct((count, rank), BF16),
            jax.ShapeDtypeStruct((count, 2 * rank), BF16),
        ],
        cost_estimate=pl.CostEstimate(
            flops=2 * count * width * width,
            bytes_accessed=2 * width * width + 14 * count * width,
            transcendentals=count,
        ),
        name="out_forward",
    )(*operands)


def ffn_views(weights, width, sub):
    if len(weights) == 1:
        (packed,) = weights
        _, parts, rows, units = packed.shape
        low = units // parts
        high = rows - low
        specs = [
            pl.BlockSpec((1, parts, high, sub), lambda t, b: (t, 0, 0, b)),
            pl.BlockSpec((1, sub // low, low, width), lambda t, b: (t, b, high // low, 0)),
        ]
        upper = lambda ref, i: ref[0, i * parts // 2 : (i + 1) * parts // 2].reshape(width, sub)
        lower = lambda ref: ref[0].reshape(sub, width)
        return [packed, packed], specs, upper, lower
    specs = [
        pl.BlockSpec((1, 2, width, sub), lambda t, b: (t, 0, 0, b)),
        pl.BlockSpec((1, sub, width), lambda t, b: (t, b, 0)),
    ]
    return list(weights), specs, lambda ref, i: ref[0, i], lambda ref: ref[0]


def ffn_forward(hidden, hidden_b, latent, weights, fb, da, db, gain, shift, cotangent):
    count, width = hidden.shape
    shards, _, units = fb.shape
    rank = db.shape[0]
    sub = min(512, units)
    arrays, views, upper, lower = ffn_views(weights, width, sub)
    inner = units // sub
    steps = shards * inner

    def kernel(h_ref, hb_ref, l_ref, w_ref, wd_ref, fb_ref, da_ref, db_ref, g_ref, s_ref, c_ref,
               pre_ref, res_ref, mid_ref, midb_ref, ld_ref, ldg_ref, acc_ref, lat_ref):
        step = pl.program_id(0) * inner + pl.program_id(1)

        @pl.when(step == 0)
        def _():
            acc_ref[...] = h_ref[...]
            lat_ref[...] = jnp.zeros_like(lat_ref)

        h = hb_ref[...]
        lat = l_ref[...]
        gate = nn(h, upper(w_ref, 0)) + nn(lat[:, :rank], fb_ref[0, :rank])
        up = nn(h, upper(w_ref, 1)) + nn(lat[:, rank:], fb_ref[0, rank:])
        pre_ref[0] = gate.astype(BF16)
        pre_ref[1] = up.astype(BF16)
        active = (gate * jax.nn.sigmoid(gate) * up).astype(BF16)
        acc_ref[...] += nn(active, lower(wd_ref))
        lat_ref[...] += nt(active, da_ref[0])

        @pl.when(step == steps - 1)
        def _():
            latent_down = lat_ref[...].astype(BF16)
            total = acc_ref[...] + nn(latent_down, db_ref[...])
            result, normed, inverse = norm_forward(total, g_ref[...], s_ref[...])
            res_ref[...] = result.astype(BF16)
            grad = norm_backward(c_ref[...], normed, inverse, g_ref[...])
            mid_ref[...] = grad
            grad_b = grad.astype(BF16)
            midb_ref[...] = grad_b
            ld_ref[...] = latent_down
            ldg_ref[...] = nt(grad_b, db_ref[...]).astype(BF16)

    full = lambda array: pl.BlockSpec(array.shape, lambda t, b: (0,) * array.ndim)
    fixed = lambda rows, size: pl.BlockSpec((rows, size), lambda t, b: (0, 0))
    operands = [hidden, hidden_b, latent, *arrays, fb, da, db, gain, shift, cotangent]
    return pl.pallas_call(
        kernel,
        grid=(shards, inner),
        in_specs=[
            full(hidden),
            full(hidden_b),
            full(latent),
            *views,
            pl.BlockSpec((1, 2 * rank, sub), lambda t, b: (t, 0, b)),
            pl.BlockSpec((1, rank, sub), lambda t, b: (t, 0, b)),
            full(db),
            full(gain),
            full(shift),
            full(cotangent),
        ],
        out_specs=[
            pl.BlockSpec((2, count, sub), lambda t, b: (0, 0, t * inner + b)),
            fixed(count, width),
            fixed(count, width),
            fixed(count, width),
            fixed(count, rank),
            fixed(count, rank),
        ],
        out_shape=[
            jax.ShapeDtypeStruct((2, count, shards * units), BF16),
            jax.ShapeDtypeStruct((count, width), BF16),
            jax.ShapeDtypeStruct((count, width), F32),
            jax.ShapeDtypeStruct((count, width), BF16),
            jax.ShapeDtypeStruct((count, rank), BF16),
            jax.ShapeDtypeStruct((count, rank), BF16),
        ],
        scratch_shapes=[pltpu.VMEM((count, width), F32), pltpu.VMEM((count, rank), F32)],
        cost_estimate=pl.CostEstimate(
            flops=6 * count * width * shards * units,
            bytes_accessed=6 * width * shards * units + 4 * count * shards * units,
            transcendentals=count * shards * units,
        ),
        name="ffn_forward",
    )(*operands)


def ffn_backward(
    grad_b, grad, pre, latent_down, latent_down_grad, latent_ffn, weights, fb, da, fa, hidden_b,
    normed, inverse, gain, latent_out, ob, oa, mixed, out_all,
):
    count, width = grad.shape
    shards, _, units = fb.shape
    rank = ob.shape[0]
    sub = min(512, units)
    inner = units // sub
    steps = shards * inner
    arrays, views, upper, lower = ffn_views(weights, width, sub)

    def kernel(gb_ref, g_ref, pre_ref, ld_ref, ldg_ref, lf_ref, w_ref, wd_ref, fb_ref, da_ref, fa_ref,
               hb_ref, n_ref, i_ref, gain_ref, lo_ref, ob_ref, oa_ref, m_ref, wo_ref,
               first_ref, mixed_ref, split_ref, common_ref, acc_ref, lat_ref):
        step = pl.program_id(0) * inner + pl.program_id(1)

        @pl.when(step == 0)
        def _():
            acc_ref[...] = g_ref[...]
            lat_ref[...] = jnp.zeros_like(lat_ref)

        ldg = ldg_ref[...]
        lf = lf_ref[...]
        grad_active = nt(gb_ref[...], lower(wd_ref)) + nn(ldg, da_ref[0])
        gate = pre_ref[0].astype(F32)
        up = pre_ref[1].astype(F32)
        sigma = jax.nn.sigmoid(gate)
        swish = gate * sigma
        active = (swish * up).astype(BF16)
        grad_gate = (grad_active * up * (sigma + swish * (1.0 - sigma))).astype(BF16)
        grad_up = (grad_active * swish).astype(BF16)
        split_ref[0] = jnp.concatenate(
            [tn(ldg, active), tn(lf[:, :rank], grad_gate), tn(lf[:, rank:], grad_up)], axis=0
        ).astype(BF16)
        acc_ref[...] += nt(grad_gate, upper(w_ref, 0)) + nt(grad_up, upper(w_ref, 1))
        lat_ref[...] += jnp.concatenate(
            [nt(grad_gate, fb_ref[0, :rank]), nt(grad_up, fb_ref[0, rank:])], axis=1
        )

        @pl.when(step == steps - 1)
        def _():
            lat = lat_ref[...].astype(BF16)
            total = acc_ref[...] + nn(lat, fa_ref[...])
            first = norm_backward(total, n_ref[...], i_ref[...], gain_ref[...])
            first_ref[...] = first
            branch = first.astype(BF16)
            log = nt(branch, ob_ref[...]).astype(BF16)
            common_ref[...] = jnp.concatenate(
                [
                    tn(ld_ref[...], gb_ref[...]),
                    tn(lat, hb_ref[...]),
                    tn(lo_ref[...], branch),
                    tn(log, m_ref[...]),
                ],
                axis=0,
            ).astype(BF16)
            mixed_ref[...] = (nt(branch, wo_ref[...]) + nn(log, oa_ref[...])).astype(BF16)

    full = lambda array: pl.BlockSpec(array.shape, lambda t, b: (0,) * array.ndim)
    fixed = lambda rows, size: pl.BlockSpec((rows, size), lambda t, b: (0, 0))
    head = [grad_b, grad, pre, latent_down, latent_down_grad, latent_ffn]
    rest = [fa, hidden_b, normed, inverse, gain, latent_out, ob, oa, mixed, out_all]
    specs = [full(array) for array in head]
    specs[2] = pl.BlockSpec((2, count, sub), lambda t, b: (0, 0, t * inner + b))
    specs += views
    specs += [
        pl.BlockSpec((1, 2 * rank, sub), lambda t, b: (t, 0, b)),
        pl.BlockSpec((1, rank, sub), lambda t, b: (t, 0, b)),
    ]
    specs += [full(array) for array in rest]
    return pl.pallas_call(
        kernel,
        grid=(shards, inner),
        in_specs=specs,
        out_specs=[
            fixed(count, width),
            fixed(count, width),
            pl.BlockSpec((1, 3 * rank, sub), lambda t, b: (t, 0, b)),
            fixed(5 * rank, width),
        ],
        out_shape=[
            jax.ShapeDtypeStruct((count, width), F32),
            jax.ShapeDtypeStruct((count, width), BF16),
            jax.ShapeDtypeStruct((shards, 3 * rank, units), BF16),
            jax.ShapeDtypeStruct((5 * rank, width), BF16),
        ],
        scratch_shapes=[pltpu.VMEM((count, width), F32), pltpu.VMEM((count, 2 * rank), F32)],
        cost_estimate=pl.CostEstimate(
            flops=6 * count * width * shards * units,
            bytes_accessed=6 * width * shards * units + 4 * count * shards * units,
            transcendentals=count * shards * units,
        ),
        name="ffn_backward",
    )(*head, *arrays, fb, da, *rest)


def norm_forward(rows, gain, shift):
    centre = jnp.mean(rows, axis=-1, keepdims=True)
    centred = rows - centre
    spread = jnp.mean(centred * centred, axis=-1, keepdims=True)
    inverse = lax.rsqrt(spread + 1e-12)
    normed = centred * inverse
    return (normed * gain + shift, normed, inverse)


def norm_backward(grads, normed, inverse, gain):
    scaled = grads * gain
    first_mean = jnp.mean(scaled, axis=-1, keepdims=True)
    second_mean = jnp.mean(scaled * normed, axis=-1, keepdims=True)
    return inverse * (scaled - first_mean - normed * second_mean)


def rope_tables(length, extra):
    half = HEAD_DIM // 2
    step = 64
    freq = 10000.0 ** (-(2.0 * np.arange(half)) / HEAD_DIM)
    freq = np.tile(freq, LANES // half)
    sign = np.where(np.arange(LANES) % HEAD_DIM < half, -1.0, 1.0)
    coarse = ((np.arange(length + extra) % length)[::step, None] * freq).astype(np.float64)
    fine = np.arange(step)[:, None] * freq
    f = lambda array: jnp.asarray(array, F32)
    cos_c, sin_c = f(np.cos(coarse))[:, None], f(np.sin(coarse))[:, None]
    cos_f, sin_f = f(np.cos(fine))[None], f(np.sin(fine))[None]
    cosine = (cos_c * cos_f - sin_c * sin_f).reshape(-1, LANES)
    sine = ((sin_c * cos_f + cos_c * sin_f) * f(sign)).reshape(-1, LANES)
    return cosine, sine


def window(array, start, count):
    return lax.dynamic_slice_in_dim(array, start, count, 0)


def gather_weight(local, parts, part):
    rows = local.shape[0] // parts
    piece = window(local, part * rows, rows)
    return lax.all_gather(piece, ALL, axis=0, tiled=True)


def gather_ffn(w_gate_up, w_down, parts, part):
    _, width, units = w_gate_up.shape
    upper = w_gate_up.reshape(2 * width, units)
    if units == width and width % (128 * parts // 8) == 0 and parts == 8:
        high, low = 2 * width // parts, units // parts
        piece = jnp.concatenate(
            [window(upper, part * high, high), window(w_down, part * low, low)], axis=0
        )
        whole = lax.all_gather(piece, ALL, axis=0, tiled=True)
        return (whole.reshape(-1, parts, high + low, units),)
    return (
        gather_weight(upper, parts, part).reshape(-1, 2, width, units),
        gather_weight(w_down, parts, part).reshape(-1, units, width),
    )


def flip(bit):
    return [(i, i ^ bit) for i in range(4)]


def send_round(piece):
    shards = lax.axis_size("tensor")
    return [lax.ppermute(piece, "tensor", cyclic(shards, k)) for k in range(1, shards)]


def spread_first(stack):
    return lax.ppermute(stack, "yx", flip(1)), lax.ppermute(stack, "yx", flip(2))


def spread_second(across, along):
    half = across.shape[0] // 2
    return (
        lax.ppermute(across[:half], "yx", flip(2)),
        lax.ppermute(along[half:], "yx", flip(1)),
    )


def swap_core(near):
    return lax.ppermute(near, "core", [(0, 1), (1, 0)])


def assemble(own, near, far, outs, store):
    shards = near.shape[1] + 1
    rows, cols = own.shape[1:]
    scalars = jnp.stack(
        [lax.axis_index("tensor"), lax.axis_index("yx"), lax.axis_index("core")]
    ).astype(jnp.int32)

    def behind(t, s):
        return lax.rem(s[0] - t + shards, shards)

    def kernel(scalar_ref, own_ref, near_ref, far_ref, *out_refs):
        mine = behind(pl.program_id(0), scalar_ref) == 0
        first = scalar_ref[2] == 0

        @pl.when(mine)
        def _():
            for j in range(8):
                store(own_ref[j], j, out_refs)

        for low_ref, high_ref, here in ((near_ref, far_ref, first), (far_ref, near_ref, jnp.logical_not(first))):

            @pl.when(jnp.logical_and(jnp.logical_not(mine), here))
            def _():
                for i in range(4):
                    side = lax.bitwise_xor(scalar_ref[1], i)
                    store(low_ref[side, 0], 2 * i, out_refs)
                    store(high_ref[side, 0], 2 * i + 1, out_refs)

    other = pl.BlockSpec(
        (4, 1, rows, cols), lambda t, s: (0, jnp.maximum(behind(t, s) - 1, 0), 0, 0)
    )
    return pl.pallas_call(
        kernel,
        grid_spec=pltpu.PrefetchScalarGridSpec(
            num_scalar_prefetch=1,
            grid=(shards,),
            in_specs=[pl.BlockSpec((8, rows, cols), lambda t, s: (0, 0, 0)), other, other],
            out_specs=[spec for _, spec in outs],
        ),
        out_shape=[jax.ShapeDtypeStruct(shape, BF16) for shape, _ in outs],
        cost_estimate=pl.CostEstimate(
            flops=0, bytes_accessed=32 * shards * rows * cols, transcendentals=0
        ),
    )(scalars, own, near, far)


def assemble_qkv(own, near, far, width, local):
    shards = near.shape[1] + 1
    size = width // 8
    short = local // 8
    head = 3 * size

    def store(piece, j, outs):
        for p in range(3):
            outs[0][0, p, j * size : (j + 1) * size] = piece[p * size : (p + 1) * size]
        for c in range(width // local):
            outs[1][j * short : (j + 1) * short, c * local : (c + 1) * local] = piece[
                head + c * short : head + (c + 1) * short
            ]

    outs = [
        (
            (shards, 3, width, local),
            pl.BlockSpec((1, 3, width, local), lambda t, s: (t, 0, 0, 0)),
        ),
        ((shards * local, width), pl.BlockSpec((local, width), lambda t, s: (t, 0))),
    ]
    return assemble(own, near, far, outs, store)


def in_order(blocks, place):
    shards = len(blocks)
    stack = jnp.stack(blocks)
    return jnp.stack(
        [
            lax.dynamic_index_in_dim(stack, lax.rem(place - t + shards, shards), 0, keepdims=False)
            for t in range(shards)
        ]
    )


def cyclic(size, step):
    return [(i, (i + step) % size) for i in range(size)]


def send_grads(share):
    shards = lax.axis_size("tensor")
    place = lax.axis_index("tensor")
    received = [share(place)]
    for step in range(1, shards):
        sent = share(lax.rem(place + step, shards))
        received.append(lax.ppermute(sent, "tensor", cyclic(shards, step)))
    return received


def add_all(blocks):
    total = blocks[0].astype(F32)
    for block in blocks[1:]:
        total = total + block.astype(F32)
    return total


def after(array, *marks):
    return lax.optimization_barrier((array, *marks))[0]


def layer(
    layer_input,
    output_grad,
    segments,
    adapter_ids,
    ln_gain,
    ln_bias,
    w_qkv,
    w_out,
    w_gate_up,
    w_down,
    qkv_a,
    qkv_b,
    out_a,
    out_b,
    ffn_a,
    ffn_b,
    down_a,
    down_b,
):
    seq_count, length = segments.shape
    assert seq_count == 1
    width = layer_input.shape[1]
    shards = lax.axis_size("tensor")
    parts = lax.axis_size(DP)
    place = lax.axis_index("tensor")
    part = lax.axis_index(DP)
    members = shards // 2
    half = length // 2
    count = length // shards
    group = place // members
    member = lax.rem(place, members)
    local = w_qkv.shape[2]
    units = w_down.shape[0]
    rank = out_b.shape[1]

    adapter = adapter_ids[0, 0]
    pick = lambda stack: lax.dynamic_index_in_dim(stack, adapter, 0, keepdims=False)
    qa, ob, fa, db = pick(qkv_a), pick(out_b), pick(ffn_a), pick(down_b)
    small = jnp.concatenate(
        [
            pick(qkv_b),
            pick(out_a),
            pick(ffn_b).reshape(-1, local),
            pick(down_a).reshape(-1, local),
        ],
        axis=0,
    )
    labels = segments[0]
    long = labels[: length - half + 1] == labels[half - 1 :]
    start = jnp.sum(jnp.where(long, jnp.arange(length - half + 1, dtype=jnp.int32), 0))
    group_start = start + group * half
    own_start = start + place * count
    x_group = roll_rows([layer_input], place, group_start, half, BF16)
    x_own_b = window(x_group, member * count, count)
    cotangent = roll_rows([output_grad], place, own_start, count, F32)
    labels_twice = jnp.concatenate([labels, labels[:half]])
    labels_group = window(labels_twice, group_start, half)
    labels_own = window(labels_group, member * count, count)
    cosine, sine = rope_tables(length, half)
    tables = (window(cosine, group_start, half), window(sine, group_start, half))
    tables_own = tuple(window(table, member * count, count) for table in tables)

    ffn_all = gather_ffn(w_gate_up, w_down, parts, part)
    if parts == 8:
        qkv_pieces = w_qkv.reshape(3, 8, width // 8, local).transpose(1, 0, 2, 3)
        out_pieces = w_out.reshape(8, local // 8, width // local, local).transpose(0, 2, 1, 3)
        pieces = jnp.concatenate(
            [
                qkv_pieces.reshape(8, 3 * width // 8, local),
                out_pieces.reshape(8, width // 8, local),
            ],
            axis=1,
        )
        piece = lax.dynamic_index_in_dim(pieces, part, 0, keepdims=False)
        joined = send_round(jnp.concatenate([piece, small], axis=0))
        size = piece.shape[0]
        small = in_order([small] + [block[size:] for block in joined], place)
        stack = jnp.concatenate([block[:size] for block in joined], axis=0)
        stack = after(stack, x_group, cotangent)
        across, along = spread_first(stack)
        corner = jnp.concatenate(spread_second(across, along), axis=0)
        near = jnp.stack([stack, across, along, corner]).reshape(4, shards - 1, size, local)
        far = swap_core(near)
        qkv_all, out_all = assemble_qkv(pieces, near, far, width, local)
    else:
        qkv_all = gather_weight(w_qkv.reshape(3 * width, local), parts, part)
        qkv_all = qkv_all.reshape(shards, 3, width, local)
        out_all = gather_weight(w_out, parts, part)
        small = lax.all_gather(small, "tensor", axis=0)
    cuts = np.cumsum([3 * rank, rank, 2 * rank * (units // local)])
    rejoin = lambda piece: piece.transpose(1, 0, 2).reshape(piece.shape[1], -1)
    qb = rejoin(small[:, : cuts[0]])
    oa = rejoin(small[:, cuts[0] : cuts[1]])
    fb = small[:, cuts[1] : cuts[2]].reshape(shards, 2 * rank, units)
    da = small[:, cuts[2] :].reshape(shards, rank, units)

    latent_qkv = nt(x_group, qa).astype(BF16)
    latent_own = window(latent_qkv, member * count, count)
    query, keys, values = project_qkv(
        x_group, x_own_b, qkv_all, latent_qkv, latent_own, qb, tables, tables_own
    )
    mixed, logs = attend(query, keys, values, labels_own, labels_group)
    hidden, hidden_b, normed, inverse, latent_out, latent_ffn = out_forward(
        mixed, out_all, oa, ob, x_own_b, ln_gain[:1], ln_bias[:1], fa
    )

    pre, result, grad_mid, grad_ffn, latent_down, latent_down_grad = ffn_forward(
        hidden, hidden_b, latent_ffn, ffn_all, fb, da, db, ln_gain[1:], ln_bias[1:], cotangent
    )
    rolled = lax.all_gather(result, "tensor", axis=0, tiled=True)

    grad_first, grad_mixed, split, common = ffn_backward(
        grad_ffn, grad_mid, pre, latent_down, latent_down_grad, latent_ffn, ffn_all, fb, da, fa,
        hidden_b, normed, inverse, ln_gain[:1], latent_out, ob, oa, mixed, out_all,
    )

    dq = None
    received = []
    before = None
    for d in range(1, members):
        target = lax.rem(member + d, members)
        dq, dk, dv = attend_back(
            query, keys, values, mixed, grad_mixed, logs, labels_own, labels_group, tables,
            tables_own, target, dq, False,
        )
        sent, part_of = project_back(
            [dk, dv], 1, qkv_all, qb, qa, latent_qkv, x_group, target, None, None
        )
        before = part_of if before is None else before + part_of
        links = [
            (g * members + i, g * members + (i + d) % members)
            for g in range(2)
            for i in range(members)
        ]
        received.append(lax.ppermute(sent, "tensor", links))

    def early_share(target):
        mine = lax.dynamic_index_in_dim(split, target, 0, keepdims=False)
        return jnp.concatenate([common, mine.reshape(-1, width)], axis=0)

    common = after(common, sent)
    early = send_grads(early_share)
    dq, dk, dv = attend_back(
        query, keys, values, mixed, grad_mixed, logs, labels_own, labels_group, tables, tables_own,
        member, dq, True,
    )
    back, qkv_part = project_back(
        [dq, dk, dv], 0, qkv_all, qb, qa, latent_qkv, x_group, member, grad_first, before
    )
    for piece in received:
        back = back + after(piece, back).astype(F32)
    back = back.astype(BF16)
    blocks = [back] + send_round(back)
    qkv_part = after(qkv_part, back)
    late = send_grads(lambda target: qkv_part)

    adapters = qkv_a.shape[0]
    hot = (adapter == jnp.arange(adapters, dtype=jnp.int32)).astype(BF16)
    flag = jnp.zeros((16, width), BF16).at[0, :adapters].set(hot)
    early = [after(piece, back) for piece in early]
    sums = jnp.concatenate([add_all(early).astype(BF16), add_all(late).astype(BF16), flag], axis=0)
    every = lax.all_gather(sums, DP, axis=0)
    placed = jnp.einsum(
        "sj,srn->jrn", every[:, -16, :adapters], every[:, :-16], preferred_element_type=F32
    )
    own_columns = lambda rows: lax.dynamic_slice_in_dim(rows, place * local, local, 2)
    mark = 5 * rank
    down_b_grad = placed[:, :rank]
    ffn_a_grad = placed[:, rank : 3 * rank]
    out_b_grad = placed[:, 3 * rank : 4 * rank]
    out_a_grad = own_columns(placed[:, 4 * rank : mark])
    extent = 3 * rank * units // width
    own_split = placed[:, mark : mark + extent].reshape(adapters, 3 * rank, units)
    down_a_grad = own_split[:, :rank]
    ffn_b_grad = own_split[:, rank:]
    mark += extent
    qkv_b_grad = own_columns(placed[:, mark : mark + 3 * rank])
    qkv_a_grad = placed[:, mark + 3 * rank : mark + 6 * rank]

    output = roll_rows([after(rolled, back)], place, -start, length, BF16)
    blocks = [after(block, output, qkv_a_grad) for block in blocks]
    grad_whole = roll_rows(blocks, place, -start, length, F32)
    return (
        output,
        grad_whole,
        qkv_a_grad,
        qkv_b_grad,
        out_a_grad,
        out_b_grad,
        ffn_a_grad,
        ffn_b_grad,
        down_a_grad,
        down_b_grad,
    )


def solution(mesh):
    devices = mesh.devices
    mesh = Mesh(
        devices.reshape(devices.shape[0] // 2, 2, devices.shape[1]), ("yx", "core", "tensor")
    )
    in_specs = (
        P(DP, None),
        P(DP, None),
        P(DP, None),
        P(DP, None),
        P(),
        P(),
        P(None, None, "tensor"),
        P("tensor", None),
        P(None, None, "tensor"),
        P("tensor", None),
        P(),
        P(None, None, "tensor"),
        P(None, None, "tensor"),
        P(),
        P(),
        P(None, None, "tensor"),
        P(None, None, "tensor"),
        P(),
    )
    out_specs = (
        P(DP, None),
        P(DP, None),
        P(),
        P(None, None, "tensor"),
        P(None, None, "tensor"),
        P(),
        P(),
        P(None, None, "tensor"),
        P(None, None, "tensor"),
        P(),
    )
    return jax.shard_map(layer, mesh=mesh, in_specs=in_specs, out_specs=out_specs, check_vma=False)
```

```python
import jax
import jax.numpy as jnp
import numpy as np
from jax import lax
from jax.experimental import pallas as pl
from jax.experimental.pallas import tpu as pltpu
from jax.sharding import Mesh
from jax.sharding import PartitionSpec as P


HEAD_DIM = 64
LANES = 128
DP = ("yx", "core")
ALL = ("tensor", "yx", "core")
F32 = jnp.float32
BF16 = jnp.bfloat16


def nt(left, right):
    return lax.dot_general(left, right, (((1,), (1,)), ((), ())), preferred_element_type=F32)


def tn(left, right):
    return lax.dot_general(left, right, (((0,), (0,)), ((), ())), preferred_element_type=F32)


def nn(left, right):
    return jnp.dot(left, right, preferred_element_type=F32)


def roll_rows(pieces, place, shift, count, dtype):
    pieces, offsets = zip(*pieces)
    number = len(pieces)
    size, width = pieces[0].shape
    group = lax.axis_size("tensor") if number > 1 else 1
    length = group * size
    unit = LANES
    units = length // unit
    block = min(512, count)
    shift = lax.rem(shift + length, length)
    first = shift // unit
    scalars = jnp.stack([first, shift - first * unit, place]).astype(jnp.int32)

    def kernel(scalar_ref, *refs):
        out_ref = refs[number]
        step = pl.program_id(0)
        if number > 1:
            rows_ref = refs[number + 1]

            @pl.when(step == 0)
            def _():
                for k in range(number):
                    member = scalar_ref[2] + offsets[k]

                    @pl.when(jnp.logical_and(member >= 0, member < group))
                    def _():
                        rows_ref[pl.ds(pl.multiple_of(member * size, size), size)] = refs[k][...]
        else:
            rows_ref = refs[0]
        offset = scalar_ref[1]
        row = lax.broadcasted_iota(jnp.int32, (unit, 2 * unit), 0)
        column = lax.broadcasted_iota(jnp.int32, (unit, 2 * unit), 1)
        move = jnp.where(column == row + offset, 1.0, 0.0).astype(BF16)
        for s in range(block // unit):
            base = scalar_ref[0] + step * (block // unit) + s
            low = rows_ref[pl.ds(pl.multiple_of(lax.rem(base, units) * unit, unit), unit)]
            high = rows_ref[pl.ds(pl.multiple_of(lax.rem(base + 1, units) * unit, unit), unit)]
            pair = jnp.concatenate([low, high], axis=0)
            out_ref[s * unit : (s + 1) * unit] = nn(move, pair).astype(dtype)

    return pl.pallas_call(
        kernel,
        grid_spec=pltpu.PrefetchScalarGridSpec(
            num_scalar_prefetch=1,
            grid=(count // block,),
            in_specs=[pl.BlockSpec((size, width), lambda i, s: (0, 0))] * number,
            out_specs=pl.BlockSpec((block, width), lambda i, s: (i, 0)),
            scratch_shapes=[pltpu.VMEM((length, width), BF16)] if number > 1 else [],
        ),
        out_shape=jax.ShapeDtypeStruct((count, width), dtype),
        cost_estimate=pl.CostEstimate(
            flops=4 * count * unit * width,
            bytes_accessed=2 * length * width + 4 * count * width,
            transcendentals=0,
        ),
        name="roll_rows",
    )(scalars, *pieces)


def spin(values, cosine, sine):
    lane = lax.broadcasted_iota(jnp.int32, (1, LANES), 1)
    first = lax.rem(lane, HEAD_DIM) < HEAD_DIM // 2
    parts = []
    for start in range(0, values.shape[1], LANES):
        piece = values[:, start : start + LANES]
        ahead = pltpu.roll(piece, LANES - HEAD_DIM // 2, 1)
        behind = pltpu.roll(piece, HEAD_DIM // 2, 1)
        parts.append(piece * cosine + jnp.where(first, ahead, behind) * sine)
    return parts[0] if len(parts) == 1 else jnp.concatenate(parts, axis=1)


def project_qkv(group, own, weights, latent, latent_own, factors, tables, tables_own):
    shards, _, width, local = weights.shape
    count, total = own.shape[0], group.shape[0]
    rank = latent.shape[1] // 3
    scale = HEAD_DIM ** (-0.5)

    def kernel(x_ref, o_ref, w_ref, l_ref, lo_ref, f_ref, c_ref, s_ref, co_ref, so_ref, q_ref, k_ref, v_ref):
        x = x_ref[...]
        lat = l_ref[...]
        factor = f_ref[...]
        query = nn(o_ref[...], w_ref[0, 0]) + nn(lo_ref[...][:, :rank], factor[:rank])
        q_ref[...] = (spin(query, co_ref[...], so_ref[...]).astype(BF16) * scale).astype(BF16)
        key = nn(x, w_ref[0, 1]) + nn(lat[:, rank : 2 * rank], factor[rank : 2 * rank])
        k_ref[...] = spin(key, c_ref[...], s_ref[...]).astype(BF16)
        value = nn(x, w_ref[0, 2]) + nn(lat[:, 2 * rank :], factor[2 * rank :])
        v_ref[...] = value.astype(BF16)

    def whole(array):
        return pl.BlockSpec(array.shape, lambda i: (0,) * array.ndim)

    def columns(rows):
        return pl.BlockSpec((rows, local), lambda i: (0, i))

    cosine, sine = tables
    cosine_own, sine_own = tables_own
    return pl.pallas_call(
        kernel,
        grid=(shards,),
        in_specs=[
            whole(group),
            whole(own),
            pl.BlockSpec((1, 3, width, local), lambda i: (i, 0, 0, 0)),
            whole(latent),
            whole(latent_own),
            columns(factors.shape[0]),
            whole(cosine),
            whole(sine),
            whole(cosine_own),
            whole(sine_own),
        ],
        out_specs=[columns(count), columns(total), columns(total)],
        out_shape=[
            jax.ShapeDtypeStruct((count, width), BF16),
            jax.ShapeDtypeStruct((total, width), BF16),
            jax.ShapeDtypeStruct((total, width), BF16),
        ],
        cost_estimate=pl.CostEstimate(
            flops=2 * width * width * (count + 2 * total),
            bytes_accessed=2 * (4 * width * width + 6 * total * width),
            transcendentals=0,
        ),
        name="project_qkv",
    )(group, own, weights, latent, latent_own, factors, cosine, sine, cosine_own, sine_own)


def head_lanes():
    return lax.broadcasted_iota(jnp.int32, (1, LANES), 1) // HEAD_DIM


def attend(query, keys, values, labels_own, labels):
    count, width = query.shape
    total = keys.shape[0]
    pairs = width // LANES

    def kernel(q_ref, k_ref, v_ref, own_ref, all_ref, out_ref, log_ref):
        q = q_ref[...]
        k = k_ref[...]
        flipped = v_ref[...].astype(F32).T
        same = all_ref[...] == own_ref[...]
        lanes = head_lanes()
        sides = lax.broadcasted_iota(jnp.int32, (LANES, 1), 0) // HEAD_DIM
        outs = []
        logs = []
        for head in range(2):
            masked = jnp.where(lanes == head, q, jnp.zeros_like(q))
            scores = jnp.where(same, nt(k, masked), -1e30)
            top = jnp.max(scores, axis=0, keepdims=True)
            expo = jnp.exp(scores - top).astype(BF16)
            stacked = jnp.where(sides == head, flipped, 1.0).astype(BF16)
            product = nn(stacked, expo)
            other = (1 - head) * HEAD_DIM
            weight_sum = product[other : other + 1]
            outs.append(product[head * HEAD_DIM : (head + 1) * HEAD_DIM] / weight_sum)
            logs.append(top + jnp.log(weight_sum))
        out_ref[...] = jnp.concatenate(outs, axis=0).T.astype(BF16)
        log_ref[0, 0:1] = logs[0]
        log_ref[0, 1:2] = logs[1]

    pair = lambda rows: pl.BlockSpec((rows, LANES), lambda i: (0, i))
    return pl.pallas_call(
        kernel,
        grid=(pairs,),
        in_specs=[
            pair(count),
            pair(total),
            pair(total),
            pl.BlockSpec((1, count), lambda i: (0, 0)),
            pl.BlockSpec((total, 1), lambda i: (0, 0)),
        ],
        out_specs=[pair(count), pl.BlockSpec((1, 8, count), lambda i: (i, 0, 0))],
        out_shape=[
            jax.ShapeDtypeStruct((count, width), BF16),
            jax.ShapeDtypeStruct((pairs, 8, count), F32),
        ],
        cost_estimate=pl.CostEstimate(
            flops=16 * count * total * width,
            bytes_accessed=4 * (count + total) * width,
            transcendentals=2 * pairs * count * total,
        ),
        name="attend",
    )(query, keys, values, labels_own[None, :], labels[:, None])


def attend_back(query, keys, values, mixed, grads, logs, labels_own, labels, tables, tables_own, block, before, last):
    count, width = query.shape
    pairs = width // LANES
    scale = HEAD_DIM ** (-0.5)
    cosine, sine = tables
    cosine_own, sine_own = tables_own
    chained = before is not None

    def kernel(block_ref, q_ref, k_ref, v_ref, m_ref, g_ref, log_ref, own_ref, all_ref, c_ref, s_ref, co_ref, so_ref, *rest):
        before_ref = rest[0] if chained else None
        dq_ref, dk_ref, dv_ref = rest[-3:]
        q = q_ref[...]
        k = k_ref[...]
        v = v_ref[...]
        g = g_ref[...]
        same = all_ref[...] == own_ref[...]
        lanes = head_lanes()
        sides = lax.broadcasted_iota(jnp.int32, (LANES, 1), 0) // HEAD_DIM
        k_flipped = k.astype(F32).T
        product = g.astype(F32) * m_ref[...].astype(F32)
        high = product.astype(BF16)
        low = (product - high.astype(F32)).astype(BF16)
        picks = (
            lax.broadcasted_iota(jnp.int32, (8, LANES), 1) // HEAD_DIM
            == lax.broadcasted_iota(jnp.int32, (8, LANES), 0)
        ).astype(F32).astype(BF16)
        delta = nt(picks, high) + nt(picks, low)
        dq = jnp.zeros((LANES, count), F32)
        dk = jnp.zeros((count, LANES), F32)
        dv = jnp.zeros((count, LANES), F32)
        for head in range(2):
            q_masked = jnp.where(lanes == head, q, jnp.zeros_like(q))
            g_masked = jnp.where(lanes == head, g, jnp.zeros_like(g))
            scores = jnp.where(same, nt(k, q_masked), -1e30)
            prob = jnp.exp(scores - log_ref[0, head : head + 1])
            grad_prob = nt(v, g_masked)
            grad_score = (prob * (grad_prob - delta[head : head + 1])).astype(BF16)
            dv = dv + nn(prob.astype(BF16), g_masked)
            dk = dk + nn(grad_score, q_masked)
            k_side = jnp.where(sides == head, k_flipped, 0.0).astype(BF16)
            dq = dq + nn(k_side, grad_score)
        dq = dq.T * scale
        if chained:
            dq = dq + before_ref[...]
        dq_ref[...] = spin(dq, co_ref[...], -so_ref[...]).astype(BF16) if last else dq
        dk_ref[...] = spin(dk, c_ref[...], -s_ref[...]).astype(BF16)
        dv_ref[...] = dv.astype(BF16)

    pair = pl.BlockSpec((count, LANES), lambda i, s: (0, i))
    chosen = pl.BlockSpec((count, LANES), lambda i, s: (s[0], i))
    rows = lambda array: pl.BlockSpec((count, array.shape[1]), lambda i, s: (s[0], 0))
    whole = lambda array: pl.BlockSpec(array.shape, lambda i, s: (0,) * array.ndim)
    labels_own = labels_own[None, :]
    labels = labels[:, None]
    operands = [query, keys, values, mixed, grads, logs, labels_own, labels, cosine, sine, cosine_own, sine_own]
    specs = [
        pair,
        chosen,
        chosen,
        pair,
        pair,
        pl.BlockSpec((1, 8, count), lambda i, s: (i, 0, 0)),
        whole(labels_own),
        rows(labels),
        rows(cosine),
        rows(sine),
        whole(cosine_own),
        whole(sine_own),
    ]
    if chained:
        operands.append(before)
        specs.append(pair)
    return pl.pallas_call(
        kernel,
        grid_spec=pltpu.PrefetchScalarGridSpec(
            num_scalar_prefetch=1, grid=(pairs,), in_specs=specs, out_specs=[pair] * 3
        ),
        out_shape=[
            jax.ShapeDtypeStruct((count, width), BF16 if last else F32),
            jax.ShapeDtypeStruct((count, width), BF16),
            jax.ShapeDtypeStruct((count, width), BF16),
        ],
        cost_estimate=pl.CostEstimate(
            flops=40 * count * count * width,
            bytes_accessed=2 * 9 * count * width,
            transcendentals=2 * pairs * count * count,
        ),
        name="attend_back",
    )(jnp.reshape(block, (1,)), *operands)


def project_back(grads, first, weights, factors, outer, latent, rows, block, base, before):
    shards, _, width, local = weights.shape
    count = grads[0].shape[0]
    rank = factors.shape[0] // 3
    number = len(grads)
    based = base is not None
    added = before is not None
    depth = number * rank

    def kernel(block_ref, w_ref, f_ref, a_ref, l_ref, x_ref, *rest):
        g_refs = rest[:number]
        base_ref = rest[number] if based else None
        before_refs = rest[number + based : number + based + 2] if added else None
        out_ref, part_ref, b_ref, acc_ref, lat_ref = rest[-5:]
        step = pl.program_id(0)

        @pl.when(step == 0)
        def _():
            acc_ref[...] = base_ref[...] if based else jnp.zeros_like(acc_ref)
            lat_ref[...] = jnp.zeros_like(lat_ref)

        total = acc_ref[...]
        lats = []
        parts = []
        for j in range(number):
            p = first + j
            g = g_refs[j][...]
            total = total + nt(g, w_ref[0, p])
            lats.append(nt(g, f_ref[p * rank : (p + 1) * rank]))
            parts.append(tn(l_ref[:, p * rank : (p + 1) * rank], g))
        acc_ref[...] = total
        lat_ref[...] += jnp.concatenate(lats, axis=1)
        if added:
            parts = parts[:1] + [
                part + before_refs[1][step, j * rank : (j + 1) * rank]
                for j, part in enumerate(parts[1:])
            ]
        b_ref[step] = jnp.concatenate(parts, axis=0).astype(b_ref.dtype)

        @pl.when(step == shards - 1)
        def _():
            lat = lat_ref[...].astype(BF16)
            final = acc_ref[...] + nn(lat, a_ref[first * rank :])
            out_ref[...] = final.astype(out_ref.dtype)
            part = tn(lat, x_ref[...])
            if added:
                none = jnp.zeros((rank, width), F32)
                part = part + jnp.concatenate([none, before_refs[0][...]], axis=0)
            part_ref[...] = part.astype(part_ref.dtype)

    whole = lambda array: pl.BlockSpec(array.shape, lambda i, s: (0,) * array.ndim)
    chosen = lambda array: pl.BlockSpec((count, array.shape[1]), lambda i, s: (s[0], 0))
    columns = lambda size: pl.BlockSpec((size, local), lambda i, s: (0, i))
    fixed = lambda size: pl.BlockSpec((size, width), lambda i, s: (0, 0))
    operands = [weights, factors, outer, latent, rows, *grads]
    specs = [
        pl.BlockSpec((1, 3, width, local), lambda i, s: (i, 0, 0, 0)),
        columns(3 * rank),
        whole(outer),
        chosen(latent),
        chosen(rows),
        *[columns(count) for _ in grads],
    ]
    if based:
        operands.append(base)
        specs.append(fixed(count))
    if added:
        operands += list(before)
        specs += [whole(array) for array in before]
    return pl.pallas_call(
        kernel,
        grid_spec=pltpu.PrefetchScalarGridSpec(
            num_scalar_prefetch=1,
            grid=(shards,),
            in_specs=specs,
            out_specs=[
                fixed(count),
                fixed(depth),
                pl.BlockSpec((shards, depth, local), lambda i, s: (0, 0, 0)),
            ],
            scratch_shapes=[
                pltpu.VMEM((count, width), F32),
                pltpu.VMEM((count, depth), F32),
            ],
        ),
        out_shape=[
            jax.ShapeDtypeStruct((count, width), F32 if based else BF16),
            jax.ShapeDtypeStruct((depth, width), BF16 if based else F32),
            jax.ShapeDtypeStruct((shards, depth, local), BF16 if based else F32),
        ],
        cost_estimate=pl.CostEstimate(
            flops=2 * number * count * width * width,
            bytes_accessed=6 * width * width + 2 * (number + 4) * count * width,
            transcendentals=0,
        ),
        name="project_back",
    )(jnp.reshape(block, (1,)), *operands)


def out_forward(mixed, weights, outer, factors, rows, gain, shift, next_factors):
    count, width = mixed.shape
    rank = factors.shape[0]

    def kernel(m_ref, w_ref, a_ref, b_ref, x_ref, g_ref, s_ref, f_ref, hid_ref, hidb_ref, n_ref, i_ref, lo_ref, lf_ref):
        m = m_ref[...]
        latent = nt(m, a_ref[...]).astype(BF16)
        total = x_ref[...].astype(F32) + nn(m, w_ref[...]) + nn(latent, b_ref[...])
        hidden, normed, inverse = norm_forward(total, g_ref[...], s_ref[...])
        hid_ref[...] = hidden
        hidden_b = hidden.astype(BF16)
        hidb_ref[...] = hidden_b
        n_ref[...] = normed
        i_ref[...] = inverse
        lo_ref[...] = latent
        lf_ref[...] = nt(hidden_b, f_ref[...]).astype(BF16)

    full = lambda array: pl.BlockSpec(array.shape, lambda i: (0,) * array.ndim)
    block = min(256, count)
    part = lambda size: pl.BlockSpec((block, size), lambda i: (i, 0))
    operands = [mixed, weights, outer, factors, rows, gain, shift, next_factors]
    return pl.pallas_call(
        kernel,
        grid=(count // block,),
        in_specs=[
            part(width),
            full(weights),
            full(outer),
            full(factors),
            part(width),
            full(gain),
            full(shift),
            full(next_factors),
        ],
        out_specs=[part(width), part(width), part(width), part(1), part(rank), part(2 * rank)],
        out_shape=[
            jax.ShapeDtypeStruct((count, width), F32),
            jax.ShapeDtypeStruct((count, width), BF16),
            jax.ShapeDtypeStruct((count, width), F32),
            jax.ShapeDtypeStruct((count, 1), F32),
            jax.ShapeDtypeStruct((count, rank), BF16),
            jax.ShapeDtypeStruct((count, 2 * rank), BF16),
        ],
        cost_estimate=pl.CostEstimate(
            flops=2 * count * width * width,
            bytes_accessed=2 * width * width + 14 * count * width,
            transcendentals=count,
        ),
        name="out_forward",
    )(*operands)


def ffn_views(weights, width, sub):
    if len(weights) == 1:
        (packed,) = weights
        _, parts, rows, units = packed.shape
        low = units // parts
        high = rows - low
        specs = [
            pl.BlockSpec((1, parts, high, sub), lambda t, b: (t, 0, 0, b)),
            pl.BlockSpec((1, sub // low, low, width), lambda t, b: (t, b, high // low, 0)),
        ]
        upper = lambda ref, i: ref[0, i * parts // 2 : (i + 1) * parts // 2].reshape(width, sub)
        lower = lambda ref: ref[0].reshape(sub, width)
        return [packed, packed], specs, upper, lower
    specs = [
        pl.BlockSpec((1, 2, width, sub), lambda t, b: (t, 0, 0, b)),
        pl.BlockSpec((1, sub, width), lambda t, b: (t, b, 0)),
    ]
    return list(weights), specs, lambda ref, i: ref[0, i], lambda ref: ref[0]


def ffn_forward(hidden, hidden_b, latent, weights, fb, da, db, gain, shift, cotangent):
    count, width = hidden.shape
    shards, _, units = fb.shape
    rank = db.shape[0]
    sub = min(1024, units)
    arrays, views, upper, lower = ffn_views(weights, width, sub)
    inner = units // sub
    steps = shards * inner

    def kernel(h_ref, hb_ref, l_ref, w_ref, wd_ref, fb_ref, da_ref, db_ref, g_ref, s_ref, c_ref,
               pre_ref, res_ref, mid_ref, midb_ref, ld_ref, ldg_ref, acc_ref, lat_ref):
        step = pl.program_id(0) * inner + pl.program_id(1)

        @pl.when(step == 0)
        def _():
            acc_ref[...] = h_ref[...]
            lat_ref[...] = jnp.zeros_like(lat_ref)

        h = hb_ref[...]
        lat = l_ref[...]
        gate = nn(h, upper(w_ref, 0)) + nn(lat[:, :rank], fb_ref[0, :rank])
        up = nn(h, upper(w_ref, 1)) + nn(lat[:, rank:], fb_ref[0, rank:])
        pre_ref[0] = gate.astype(BF16)
        pre_ref[1] = up.astype(BF16)
        active = (gate * jax.nn.sigmoid(gate) * up).astype(BF16)
        acc_ref[...] += nn(active, lower(wd_ref))
        lat_ref[...] += nt(active, da_ref[0])

        @pl.when(step == steps - 1)
        def _():
            latent_down = lat_ref[...].astype(BF16)
            total = acc_ref[...] + nn(latent_down, db_ref[...])
            result, normed, inverse = norm_forward(total, g_ref[...], s_ref[...])
            res_ref[...] = result.astype(BF16)
            grad = norm_backward(c_ref[...], normed, inverse, g_ref[...])
            mid_ref[...] = grad
            grad_b = grad.astype(BF16)
            midb_ref[...] = grad_b
            ld_ref[...] = latent_down
            ldg_ref[...] = nt(grad_b, db_ref[...]).astype(BF16)

    full = lambda array: pl.BlockSpec(array.shape, lambda t, b: (0,) * array.ndim)
    fixed = lambda rows, size: pl.BlockSpec((rows, size), lambda t, b: (0, 0))
    operands = [hidden, hidden_b, latent, *arrays, fb, da, db, gain, shift, cotangent]
    return pl.pallas_call(
        kernel,
        grid=(shards, inner),
        in_specs=[
            full(hidden),
            full(hidden_b),
            full(latent),
            *views,
            pl.BlockSpec((1, 2 * rank, sub), lambda t, b: (t, 0, b)),
            pl.BlockSpec((1, rank, sub), lambda t, b: (t, 0, b)),
            full(db),
            full(gain),
            full(shift),
            full(cotangent),
        ],
        out_specs=[
            pl.BlockSpec((2, count, sub), lambda t, b: (0, 0, t * inner + b)),
            fixed(count, width),
            fixed(count, width),
            fixed(count, width),
            fixed(count, rank),
            fixed(count, rank),
        ],
        out_shape=[
            jax.ShapeDtypeStruct((2, count, shards * units), BF16),
            jax.ShapeDtypeStruct((count, width), BF16),
            jax.ShapeDtypeStruct((count, width), F32),
            jax.ShapeDtypeStruct((count, width), BF16),
            jax.ShapeDtypeStruct((count, rank), BF16),
            jax.ShapeDtypeStruct((count, rank), BF16),
        ],
        scratch_shapes=[pltpu.VMEM((count, width), F32), pltpu.VMEM((count, rank), F32)],
        cost_estimate=pl.CostEstimate(
            flops=6 * count * width * shards * units,
            bytes_accessed=6 * width * shards * units + 4 * count * shards * units,
            transcendentals=count * shards * units,
        ),
        name="ffn_forward",
    )(*operands)


def ffn_backward(
    grad_b, grad, pre, latent_down, latent_down_grad, latent_ffn, weights, fb, da, fa, hidden_b,
    normed, inverse, gain, latent_out, ob, oa, mixed, out_all,
):
    count, width = grad.shape
    shards, _, units = fb.shape
    rank = ob.shape[0]
    sub = min(1024, units)
    inner = units // sub
    steps = shards * inner
    arrays, views, upper, lower = ffn_views(weights, width, sub)

    def kernel(gb_ref, g_ref, pre_ref, ld_ref, ldg_ref, lf_ref, w_ref, wd_ref, fb_ref, da_ref, fa_ref,
               hb_ref, n_ref, i_ref, gain_ref, lo_ref, ob_ref, oa_ref, m_ref, wo_ref,
               first_ref, mixed_ref, split_ref, common_ref, acc_ref, lat_ref):
        step = pl.program_id(0) * inner + pl.program_id(1)

        @pl.when(step == 0)
        def _():
            acc_ref[...] = g_ref[...]
            lat_ref[...] = jnp.zeros_like(lat_ref)

        ldg = ldg_ref[...]
        lf = lf_ref[...]
        grad_active = nt(gb_ref[...], lower(wd_ref)) + nn(ldg, da_ref[0])
        gate = pre_ref[0].astype(F32)
        up = pre_ref[1].astype(F32)
        sigma = jax.nn.sigmoid(gate)
        swish = gate * sigma
        active = (swish * up).astype(BF16)
        grad_gate = (grad_active * up * (sigma + swish * (1.0 - sigma))).astype(BF16)
        grad_up = (grad_active * swish).astype(BF16)
        split_ref[0] = jnp.concatenate(
            [tn(ldg, active), tn(lf[:, :rank], grad_gate), tn(lf[:, rank:], grad_up)], axis=0
        ).astype(BF16)
        acc_ref[...] += nt(grad_gate, upper(w_ref, 0)) + nt(grad_up, upper(w_ref, 1))
        lat_ref[...] += jnp.concatenate(
            [nt(grad_gate, fb_ref[0, :rank]), nt(grad_up, fb_ref[0, rank:])], axis=1
        )

        @pl.when(step == steps - 1)
        def _():
            lat = lat_ref[...].astype(BF16)
            total = acc_ref[...] + nn(lat, fa_ref[...])
            first = norm_backward(total, n_ref[...], i_ref[...], gain_ref[...])
            first_ref[...] = first
            branch = first.astype(BF16)
            log = nt(branch, ob_ref[...]).astype(BF16)
            common_ref[...] = jnp.concatenate(
                [
                    tn(ld_ref[...], gb_ref[...]),
                    tn(lat, hb_ref[...]),
                    tn(lo_ref[...], branch),
                    tn(log, m_ref[...]),
                ],
                axis=0,
            ).astype(BF16)
            mixed_ref[...] = (nt(branch, wo_ref[...]) + nn(log, oa_ref[...])).astype(BF16)

    full = lambda array: pl.BlockSpec(array.shape, lambda t, b: (0,) * array.ndim)
    fixed = lambda rows, size: pl.BlockSpec((rows, size), lambda t, b: (0, 0))
    head = [grad_b, grad, pre, latent_down, latent_down_grad, latent_ffn]
    rest = [fa, hidden_b, normed, inverse, gain, latent_out, ob, oa, mixed, out_all]
    specs = [full(array) for array in head]
    specs[2] = pl.BlockSpec((2, count, sub), lambda t, b: (0, 0, t * inner + b))
    specs += views
    specs += [
        pl.BlockSpec((1, 2 * rank, sub), lambda t, b: (t, 0, b)),
        pl.BlockSpec((1, rank, sub), lambda t, b: (t, 0, b)),
    ]
    specs += [full(array) for array in rest]
    return pl.pallas_call(
        kernel,
        grid=(shards, inner),
        in_specs=specs,
        out_specs=[
            fixed(count, width),
            fixed(count, width),
            pl.BlockSpec((1, 3 * rank, sub), lambda t, b: (t, 0, b)),
            fixed(5 * rank, width),
        ],
        out_shape=[
            jax.ShapeDtypeStruct((count, width), F32),
            jax.ShapeDtypeStruct((count, width), BF16),
            jax.ShapeDtypeStruct((shards, 3 * rank, units), BF16),
            jax.ShapeDtypeStruct((5 * rank, width), BF16),
        ],
        scratch_shapes=[pltpu.VMEM((count, width), F32), pltpu.VMEM((count, 2 * rank), F32)],
        cost_estimate=pl.CostEstimate(
            flops=6 * count * width * shards * units,
            bytes_accessed=6 * width * shards * units + 4 * count * shards * units,
            transcendentals=count * shards * units,
        ),
        name="ffn_backward",
    )(*head, *arrays, fb, da, *rest)


def norm_forward(rows, gain, shift):
    centre = jnp.mean(rows, axis=-1, keepdims=True)
    centred = rows - centre
    spread = jnp.mean(centred * centred, axis=-1, keepdims=True)
    inverse = lax.rsqrt(spread + 1e-12)
    normed = centred * inverse
    return (normed * gain + shift, normed, inverse)


def norm_backward(grads, normed, inverse, gain):
    scaled = grads * gain
    first_mean = jnp.mean(scaled, axis=-1, keepdims=True)
    second_mean = jnp.mean(scaled * normed, axis=-1, keepdims=True)
    return inverse * (scaled - first_mean - normed * second_mean)


def rope_tables(length, extra):
    half = HEAD_DIM // 2
    step = 64
    freq = 10000.0 ** (-(2.0 * np.arange(half)) / HEAD_DIM)
    freq = np.tile(freq, LANES // half)
    sign = np.where(np.arange(LANES) % HEAD_DIM < half, -1.0, 1.0)
    coarse = ((np.arange(length + extra) % length)[::step, None] * freq).astype(np.float64)
    fine = np.arange(step)[:, None] * freq
    f = lambda array: jnp.asarray(array, F32)
    cos_c, sin_c = f(np.cos(coarse))[:, None], f(np.sin(coarse))[:, None]
    cos_f, sin_f = f(np.cos(fine))[None], f(np.sin(fine))[None]
    cosine = (cos_c * cos_f - sin_c * sin_f).reshape(-1, LANES)
    sine = ((sin_c * cos_f + cos_c * sin_f) * f(sign)).reshape(-1, LANES)
    return cosine, sine


def window(array, start, count):
    return lax.dynamic_slice_in_dim(array, start, count, 0)


def gather_weight(local, parts, part):
    rows = local.shape[0] // parts
    piece = window(local, part * rows, rows)
    return lax.all_gather(piece, ALL, axis=0, tiled=True)


def gather_ffn(w_gate_up, w_down, parts, part):
    _, width, units = w_gate_up.shape
    upper = w_gate_up.reshape(2 * width, units)
    if units == width and width % (128 * parts // 8) == 0 and parts == 8:
        high, low = 2 * width // parts, units // parts
        piece = jnp.concatenate(
            [window(upper, part * high, high), window(w_down, part * low, low)], axis=0
        )
        whole = lax.all_gather(piece, ALL, axis=0, tiled=True)
        return (whole.reshape(-1, parts, high + low, units),)
    return (
        gather_weight(upper, parts, part).reshape(-1, 2, width, units),
        gather_weight(w_down, parts, part).reshape(-1, units, width),
    )


def flip(bit):
    return [(i, i ^ bit) for i in range(4)]


def send_round(piece):
    shards = lax.axis_size("tensor")
    return [lax.ppermute(piece, "tensor", cyclic(shards, k)) for k in range(1, shards)]


def spread_first(stack):
    return lax.ppermute(stack, "yx", flip(1)), lax.ppermute(stack, "yx", flip(2))


def spread_second(across, along):
    half = across.shape[0] // 2
    return (
        lax.ppermute(across[:half], "yx", flip(2)),
        lax.ppermute(along[half:], "yx", flip(1)),
    )


def swap_core(near):
    return lax.ppermute(near, "core", [(0, 1), (1, 0)])


def assemble(own, near, far, outs, store):
    shards = near.shape[1] + 1
    rows, cols = own.shape[1:]
    scalars = jnp.stack(
        [lax.axis_index("tensor"), lax.axis_index("yx"), lax.axis_index("core")]
    ).astype(jnp.int32)

    def behind(t, s):
        return lax.rem(s[0] - t + shards, shards)

    def kernel(scalar_ref, own_ref, near_ref, far_ref, *out_refs):
        mine = behind(pl.program_id(0), scalar_ref) == 0
        first = scalar_ref[2] == 0

        @pl.when(mine)
        def _():
            for j in range(8):
                store(own_ref[j], j, out_refs)

        for low_ref, high_ref, here in ((near_ref, far_ref, first), (far_ref, near_ref, jnp.logical_not(first))):

            @pl.when(jnp.logical_and(jnp.logical_not(mine), here))
            def _():
                for i in range(4):
                    side = lax.bitwise_xor(scalar_ref[1], i)
                    store(low_ref[side, 0], 2 * i, out_refs)
                    store(high_ref[side, 0], 2 * i + 1, out_refs)

    other = pl.BlockSpec(
        (4, 1, rows, cols), lambda t, s: (0, jnp.maximum(behind(t, s) - 1, 0), 0, 0)
    )
    return pl.pallas_call(
        kernel,
        grid_spec=pltpu.PrefetchScalarGridSpec(
            num_scalar_prefetch=1,
            grid=(shards,),
            in_specs=[pl.BlockSpec((8, rows, cols), lambda t, s: (0, 0, 0)), other, other],
            out_specs=[spec for _, spec in outs],
        ),
        out_shape=[jax.ShapeDtypeStruct(shape, BF16) for shape, _ in outs],
        cost_estimate=pl.CostEstimate(
            flops=0, bytes_accessed=32 * shards * rows * cols, transcendentals=0
        ),
    )(scalars, own, near, far)


def assemble_qkv(own, near, far, width, local):
    shards = near.shape[1] + 1
    size = width // 8
    short = local // 8
    head = 3 * size

    def store(piece, j, outs):
        for p in range(3):
            outs[0][0, p, j * size : (j + 1) * size] = piece[p * size : (p + 1) * size]
        for c in range(width // local):
            outs[1][j * short : (j + 1) * short, c * local : (c + 1) * local] = piece[
                head + c * short : head + (c + 1) * short
            ]

    outs = [
        (
            (shards, 3, width, local),
            pl.BlockSpec((1, 3, width, local), lambda t, s: (t, 0, 0, 0)),
        ),
        ((shards * local, width), pl.BlockSpec((local, width), lambda t, s: (t, 0))),
    ]
    return assemble(own, near, far, outs, store)


def in_order(blocks, place):
    shards = len(blocks)
    stack = jnp.stack(blocks)
    return jnp.stack(
        [
            lax.dynamic_index_in_dim(stack, lax.rem(place - t + shards, shards), 0, keepdims=False)
            for t in range(shards)
        ]
    )


def cyclic(size, step):
    return [(i, (i + step) % size) for i in range(size)]


def send_grads(share):
    shards = lax.axis_size("tensor")
    place = lax.axis_index("tensor")
    received = [share(place)]
    for step in range(1, shards):
        sent = share(lax.rem(place + step, shards))
        received.append(lax.ppermute(sent, "tensor", cyclic(shards, step)))
    return received


def add_all(blocks):
    total = blocks[0].astype(F32)
    for block in blocks[1:]:
        total = total + block.astype(F32)
    return total


def line_gather(block):
    shards = lax.axis_size("tensor")
    blocks = [(block, 0)]
    up = down = block
    for step in range(1, shards):
        links = [(i, i + 1) for i in range(step - 1, shards - 1)]
        up = lax.ppermute(up, "tensor", links)
        down = lax.ppermute(down, "tensor", [(shards - 1 - i, shards - 1 - j) for i, j in links])
        blocks += [(up, -step), (down, step)]
    return blocks


def after(array, *marks):
    return lax.optimization_barrier((array, *marks))[0]


def place_sums(every, plan, adapters, place):
    count, rows, width = every.shape
    rows -= 16
    owners = jnp.sum(
        every[:, rows, :adapters].astype(jnp.int32) * jnp.arange(adapters, dtype=jnp.int32), axis=1
    )
    scalars = jnp.concatenate([jnp.reshape(place, (1,)), owners]).astype(jnp.int32)

    def kernel(scalar_ref, every_ref, *refs):
        outs, total_ref = refs[:-1], refs[-1]
        adapter = pl.program_id(0)
        total_ref[...] = jnp.zeros_like(total_ref)
        for s in range(count):

            @pl.when(scalar_ref[1 + s] == adapter)
            def _():
                total_ref[...] += every_ref[s, :rows].astype(F32)

        for (first, size, columns), out in zip(plan, outs):
            if columns is None:
                out[0] = total_ref[first : first + size]
            else:
                start = pl.multiple_of(scalar_ref[0] * columns, LANES)
                out[0] = total_ref[first : first + size, pl.ds(start, columns)]

    shapes = [(adapters, size, width if columns is None else columns) for _, size, columns in plan]
    return pl.pallas_call(
        kernel,
        grid_spec=pltpu.PrefetchScalarGridSpec(
            num_scalar_prefetch=1,
            grid=(adapters,),
            in_specs=[pl.BlockSpec(every.shape, lambda i, s: (0, 0, 0))],
            out_specs=[pl.BlockSpec((1,) + shape[1:], lambda i, s: (i, 0, 0)) for shape in shapes],
            scratch_shapes=[pltpu.VMEM((rows, width), F32)],
        ),
        out_shape=[jax.ShapeDtypeStruct(shape, F32) for shape in shapes],
        cost_estimate=pl.CostEstimate(
            flops=count * rows * width,
            bytes_accessed=(2 * count + 4 * adapters) * rows * width,
            transcendentals=0,
        ),
        name="place_sums",
    )(scalars, every)


def after(array, *marks):
    return lax.optimization_barrier((array, *marks))[0]


def layer(
    layer_input,
    output_grad,
    segments,
    adapter_ids,
    ln_gain,
    ln_bias,
    w_qkv,
    w_out,
    w_gate_up,
    w_down,
    qkv_a,
    qkv_b,
    out_a,
    out_b,
    ffn_a,
    ffn_b,
    down_a,
    down_b,
):
    seq_count, length = segments.shape
    assert seq_count == 1
    width = layer_input.shape[1]
    shards = lax.axis_size("tensor")
    parts = lax.axis_size(DP)
    place = lax.axis_index("tensor")
    part = lax.axis_index(DP)
    members = shards // 2
    half = length // 2
    count = length // shards
    group = place // members
    member = lax.rem(place, members)
    local = w_qkv.shape[2]
    units = w_down.shape[0]
    rank = out_b.shape[1]

    adapter = adapter_ids[0, 0]
    pick = lambda stack: lax.dynamic_index_in_dim(stack, adapter, 0, keepdims=False)
    qa, ob, fa, db = pick(qkv_a), pick(out_b), pick(ffn_a), pick(down_b)
    small = jnp.concatenate(
        [
            pick(qkv_b),
            pick(out_a),
            pick(ffn_b).reshape(-1, local),
            pick(down_a).reshape(-1, local),
        ],
        axis=0,
    )
    labels = segments[0]
    long = labels[: length - half + 1] == labels[half - 1 :]
    start = jnp.sum(jnp.where(long, jnp.arange(length - half + 1, dtype=jnp.int32), 0))
    group_start = start + group * half
    own_start = start + place * count
    x_group = roll_rows([(layer_input, 0)], place, group_start, half, BF16)
    x_own_b = window(x_group, member * count, count)
    cotangent = roll_rows([(output_grad, 0)], place, own_start, count, F32)
    labels_twice = jnp.concatenate([labels, labels[:half]])
    labels_group = window(labels_twice, group_start, half)
    labels_own = window(labels_group, member * count, count)
    cosine, sine = rope_tables(length, half)
    tables = (window(cosine, group_start, half), window(sine, group_start, half))
    tables_own = tuple(window(table, member * count, count) for table in tables)

    ffn_all = gather_ffn(w_gate_up, w_down, parts, part)
    if parts == 8:
        qkv_pieces = w_qkv.reshape(3, 8, width // 8, local).transpose(1, 0, 2, 3)
        out_pieces = w_out.reshape(8, local // 8, width // local, local).transpose(0, 2, 1, 3)
        pieces = jnp.concatenate(
            [
                qkv_pieces.reshape(8, 3 * width // 8, local),
                out_pieces.reshape(8, width // 8, local),
            ],
            axis=1,
        )
        piece = lax.dynamic_index_in_dim(pieces, part, 0, keepdims=False)
        joined = send_round(jnp.concatenate([piece, small], axis=0))
        size = piece.shape[0]
        small = in_order([small] + [block[size:] for block in joined], place)
        stack = jnp.concatenate([block[:size] for block in joined], axis=0)
        stack = after(stack, x_group, cotangent)
        across, along = spread_first(stack)
        corner = jnp.concatenate(spread_second(across, along), axis=0)
        near = jnp.stack([stack, across, along, corner]).reshape(4, shards - 1, size, local)
        far = swap_core(near)
        qkv_all, out_all = assemble_qkv(pieces, near, far, width, local)
    else:
        qkv_all = gather_weight(w_qkv.reshape(3 * width, local), parts, part)
        qkv_all = qkv_all.reshape(shards, 3, width, local)
        out_all = gather_weight(w_out, parts, part)
        small = lax.all_gather(small, "tensor", axis=0)
    cuts = np.cumsum([3 * rank, rank, 2 * rank * (units // local)])
    rejoin = lambda piece: piece.transpose(1, 0, 2).reshape(piece.shape[1], -1)
    qb = rejoin(small[:, : cuts[0]])
    oa = rejoin(small[:, cuts[0] : cuts[1]])
    fb = small[:, cuts[1] : cuts[2]].reshape(shards, 2 * rank, units)
    da = small[:, cuts[2] :].reshape(shards, rank, units)

    latent_qkv = nt(x_group, qa).astype(BF16)
    latent_own = window(latent_qkv, member * count, count)
    query, keys, values = project_qkv(
        x_group, x_own_b, qkv_all, latent_qkv, latent_own, qb, tables, tables_own
    )
    mixed, logs = attend(query, keys, values, labels_own, labels_group)
    hidden, hidden_b, normed, inverse, latent_out, latent_ffn = out_forward(
        mixed, out_all, oa, ob, x_own_b, ln_gain[:1], ln_bias[:1], fa
    )

    pre, result, grad_mid, grad_ffn, latent_down, latent_down_grad = ffn_forward(
        hidden, hidden_b, latent_ffn, ffn_all, fb, da, db, ln_gain[1:], ln_bias[1:], cotangent
    )
    rolled = lax.all_gather(result, "tensor", axis=0, tiled=True)

    grad_first, grad_mixed, split, common = ffn_backward(
        grad_ffn, grad_mid, pre, latent_down, latent_down_grad, latent_ffn, ffn_all, fb, da, fa,
        hidden_b, normed, inverse, ln_gain[:1], latent_out, ob, oa, mixed, out_all,
    )

    dq = None
    received = []
    before = None
    for d in range(1, members):
        target = lax.rem(member + d, members)
        dq, dk, dv = attend_back(
            query, keys, values, mixed, grad_mixed, logs, labels_own, labels_group, tables,
            tables_own, target, dq, False,
        )
        sent, *part_of = project_back(
            [dk, dv], 1, qkv_all, qb, qa, latent_qkv, x_group, target, None, None
        )
        before = part_of if before is None else [a + b for a, b in zip(before, part_of)]
        links = [
            (g * members + i, g * members + (i + d) % members)
            for g in range(2)
            for i in range(members)
        ]
        received.append(lax.ppermute(sent, "tensor", links))

    def early_share(target):
        mine = lax.dynamic_index_in_dim(split, target, 0, keepdims=False)
        return jnp.concatenate([common, mine.reshape(-1, width)], axis=0)

    def late_share(target):
        mine = lax.dynamic_index_in_dim(qkv_b_part, target, 0, keepdims=False)
        return jnp.concatenate([qkv_a_part, mine.reshape(-1, width)], axis=0)

    common = after(common, sent)
    early = send_grads(early_share)
    dq, dk, dv = attend_back(
        query, keys, values, mixed, grad_mixed, logs, labels_own, labels_group, tables, tables_own,
        member, dq, True,
    )
    back, qkv_a_part, qkv_b_part = project_back(
        [dq, dk, dv], 0, qkv_all, qb, qa, latent_qkv, x_group, member, grad_first, before
    )
    late = send_grads(late_share)

    adapters = qkv_a.shape[0]
    hot = (adapter == jnp.arange(adapters, dtype=jnp.int32)).astype(BF16)
    flag = jnp.zeros((16, width), BF16).at[0, :adapters].set(hot)
    early_sum = add_all([early[0]] + [after(piece, qkv_a_part) for piece in early[1:]]).astype(BF16)
    early_every = lax.all_gather(jnp.concatenate([early_sum, flag], axis=0), DP, axis=0)
    for piece in received:
        back = back + after(piece, back, early_sum).astype(F32)
    back = back.astype(BF16)
    blocks = line_gather(back)
    late_sum = add_all([late[0]] + [after(piece, back) for piece in late[1:]]).astype(BF16)
    late_every = lax.all_gather(jnp.concatenate([late_sum, flag], axis=0), DP, axis=0)
    plan = [
        (0, rank, None),
        (rank, 2 * rank, None),
        (3 * rank, rank, None),
        (4 * rank, rank, local),
    ]
    straight = units == width
    if straight:
        plan += [(5 * rank, rank, None), (6 * rank, 2 * rank, None)]
    else:
        plan += [(5 * rank, 3 * rank * units // width, None)]
    early_grads = place_sums(early_every, plan, adapters, place)
    down_b_grad, ffn_a_grad, out_b_grad, out_a_grad = early_grads[:4]
    if straight:
        down_a_grad, ffn_b_grad = early_grads[4:]
    else:
        own_split = early_grads[4].reshape(adapters, 3 * rank, units)
        down_a_grad, ffn_b_grad = own_split[:, :rank], own_split[:, rank:]
    qkv_a_grad, qkv_b_grad = place_sums(
        late_every,
        [(0, 3 * rank, None), (3 * rank, 3 * rank * local // width, None)],
        adapters,
        place,
    )
    qkv_b_grad = qkv_b_grad.reshape(adapters, 3 * rank, local)

    output = roll_rows([(after(rolled, back), 0)], place, -start, length, BF16)
    blocks = [(after(block, output, qkv_a_grad, out_b_grad), i) for block, i in blocks]
    grad_whole = roll_rows(blocks, place, -start, length, F32)
    return (
        output,
        grad_whole,
        qkv_a_grad,
        qkv_b_grad,
        out_a_grad,
        out_b_grad,
        ffn_a_grad,
        ffn_b_grad,
        down_a_grad,
        down_b_grad,
    )


def solution(mesh):
    devices = mesh.devices
    mesh = Mesh(
        devices.reshape(devices.shape[0] // 2, 2, devices.shape[1]), ("yx", "core", "tensor")
    )
    in_specs = (
        P(DP, None),
        P(DP, None),
        P(DP, None),
        P(DP, None),
        P(),
        P(),
        P(None, None, "tensor"),
        P("tensor", None),
        P(None, None, "tensor"),
        P("tensor", None),
        P(),
        P(None, None, "tensor"),
        P(None, None, "tensor"),
        P(),
        P(),
        P(None, None, "tensor"),
        P(None, None, "tensor"),
        P(),
    )
    out_specs = (
        P(DP, None),
        P(DP, None),
        P(),
        P(None, None, "tensor"),
        P(None, None, "tensor"),
        P(),
        P(),
        P(None, None, "tensor"),
        P(None, None, "tensor"),
        P(),
    )
    return jax.shard_map(layer, mesh=mesh, in_specs=in_specs, out_specs=out_specs, check_vma=False)
```

```python
import jax
import jax.numpy as jnp
import numpy as np
from jax import lax
from jax.experimental import pallas as pl
from jax.experimental.pallas import tpu as pltpu
from jax.sharding import Mesh
from jax.sharding import PartitionSpec as P


HEAD_DIM = 64
LANES = 128
DP = ("yx", "core")
ALL = ("tensor", "yx", "core")
F32 = jnp.float32
BF16 = jnp.bfloat16


def nt(left, right):
    return lax.dot_general(left, right, (((1,), (1,)), ((), ())), preferred_element_type=F32)


def tn(left, right):
    return lax.dot_general(left, right, (((0,), (0,)), ((), ())), preferred_element_type=F32)


def nn(left, right):
    return jnp.dot(left, right, preferred_element_type=F32)


def roll_rows(pieces, place, shift, count, dtype):
    pieces, offsets = zip(*pieces)
    number = len(pieces)
    size, width = pieces[0].shape
    group = lax.axis_size("tensor") if number > 1 else 1
    length = group * size
    unit = LANES
    units = length // unit
    block = min(1024, count)
    shift = lax.rem(shift + length, length)
    first = shift // unit
    scalars = jnp.stack([first, shift - first * unit, place]).astype(jnp.int32)

    def kernel(scalar_ref, *refs):
        out_ref = refs[number]
        step = pl.program_id(0)
        if number > 1:
            rows_ref = refs[number + 1]

            @pl.when(step == 0)
            def _():
                for k in range(number):
                    member = scalar_ref[2] + offsets[k]

                    @pl.when(jnp.logical_and(member >= 0, member < group))
                    def _():
                        rows_ref[pl.ds(pl.multiple_of(member * size, size), size)] = refs[k][...]
        else:
            rows_ref = refs[0]
        offset = scalar_ref[1]
        row = lax.broadcasted_iota(jnp.int32, (unit, 2 * unit), 0)
        column = lax.broadcasted_iota(jnp.int32, (unit, 2 * unit), 1)
        move = jnp.where(column == row + offset, 1.0, 0.0).astype(BF16)
        for s in range(block // unit):
            base = scalar_ref[0] + step * (block // unit) + s
            low = rows_ref[pl.ds(pl.multiple_of(lax.rem(base, units) * unit, unit), unit)]
            high = rows_ref[pl.ds(pl.multiple_of(lax.rem(base + 1, units) * unit, unit), unit)]
            pair = jnp.concatenate([low, high], axis=0)
            out_ref[s * unit : (s + 1) * unit] = nn(move, pair).astype(dtype)

    return pl.pallas_call(
        kernel,
        grid_spec=pltpu.PrefetchScalarGridSpec(
            num_scalar_prefetch=1,
            grid=(count // block,),
            in_specs=[pl.BlockSpec((size, width), lambda i, s: (0, 0))] * number,
            out_specs=pl.BlockSpec((block, width), lambda i, s: (i, 0)),
            scratch_shapes=[pltpu.VMEM((length, width), BF16)] if number > 1 else [],
        ),
        out_shape=jax.ShapeDtypeStruct((count, width), dtype),
        cost_estimate=pl.CostEstimate(
            flops=4 * count * unit * width,
            bytes_accessed=2 * length * width + 4 * count * width,
            transcendentals=0,
        ),
        name="roll_rows",
    )(scalars, *pieces)


def spin(values, cosine, sine):
    lane = lax.broadcasted_iota(jnp.int32, (1, LANES), 1)
    first = lax.rem(lane, HEAD_DIM) < HEAD_DIM // 2
    parts = []
    for start in range(0, values.shape[1], LANES):
        piece = values[:, start : start + LANES]
        ahead = pltpu.roll(piece, LANES - HEAD_DIM // 2, 1)
        behind = pltpu.roll(piece, HEAD_DIM // 2, 1)
        parts.append(piece * cosine + jnp.where(first, ahead, behind) * sine)
    return parts[0] if len(parts) == 1 else jnp.concatenate(parts, axis=1)


def project_qkv(group, own, weights, latent, latent_own, factors, tables, tables_own):
    shards, _, width, local = weights.shape
    count, total = own.shape[0], group.shape[0]
    rank = latent.shape[1] // 3
    scale = HEAD_DIM ** (-0.5)

    def kernel(x_ref, o_ref, w_ref, l_ref, lo_ref, f_ref, c_ref, s_ref, co_ref, so_ref, q_ref, k_ref, v_ref):
        x = x_ref[...]
        lat = l_ref[...]
        factor = f_ref[...]
        query = nn(o_ref[...], w_ref[0, 0]) + nn(lo_ref[...][:, :rank], factor[:rank])
        q_ref[...] = (spin(query, co_ref[...], so_ref[...]).astype(BF16) * scale).astype(BF16)
        key = nn(x, w_ref[0, 1]) + nn(lat[:, rank : 2 * rank], factor[rank : 2 * rank])
        k_ref[...] = spin(key, c_ref[...], s_ref[...]).astype(BF16)
        value = nn(x, w_ref[0, 2]) + nn(lat[:, 2 * rank :], factor[2 * rank :])
        v_ref[...] = value.astype(BF16)

    def whole(array):
        return pl.BlockSpec(array.shape, lambda i: (0,) * array.ndim)

    def columns(rows):
        return pl.BlockSpec((rows, local), lambda i: (0, i))

    cosine, sine = tables
    cosine_own, sine_own = tables_own
    return pl.pallas_call(
        kernel,
        grid=(shards,),
        in_specs=[
            whole(group),
            whole(own),
            pl.BlockSpec((1, 3, width, local), lambda i: (i, 0, 0, 0)),
            whole(latent),
            whole(latent_own),
            columns(factors.shape[0]),
            whole(cosine),
            whole(sine),
            whole(cosine_own),
            whole(sine_own),
        ],
        out_specs=[columns(count), columns(total), columns(total)],
        out_shape=[
            jax.ShapeDtypeStruct((count, width), BF16),
            jax.ShapeDtypeStruct((total, width), BF16),
            jax.ShapeDtypeStruct((total, width), BF16),
        ],
        cost_estimate=pl.CostEstimate(
            flops=2 * width * width * (count + 2 * total),
            bytes_accessed=2 * (4 * width * width + 6 * total * width),
            transcendentals=0,
        ),
        name="project_qkv",
    )(group, own, weights, latent, latent_own, factors, cosine, sine, cosine_own, sine_own)


def head_lanes():
    return lax.broadcasted_iota(jnp.int32, (1, LANES), 1) // HEAD_DIM


def attend(query, keys, values, labels_own, labels):
    count, width = query.shape
    total = keys.shape[0]
    pairs = width // LANES

    def kernel(q_ref, k_ref, v_ref, own_ref, all_ref, out_ref, log_ref):
        q = q_ref[...]
        k = k_ref[...]
        flipped = v_ref[...].astype(F32).T
        same = all_ref[...] == own_ref[...]
        lanes = head_lanes()
        sides = lax.broadcasted_iota(jnp.int32, (LANES, 1), 0) // HEAD_DIM
        outs = []
        logs = []
        for head in range(2):
            masked = jnp.where(lanes == head, q, jnp.zeros_like(q))
            scores = jnp.where(same, nt(k, masked), -1e30)
            top = jnp.max(scores, axis=0, keepdims=True)
            expo = jnp.exp(scores - top).astype(BF16)
            stacked = jnp.where(sides == head, flipped, 1.0).astype(BF16)
            product = nn(stacked, expo)
            other = (1 - head) * HEAD_DIM
            weight_sum = product[other : other + 1]
            outs.append(product[head * HEAD_DIM : (head + 1) * HEAD_DIM] / weight_sum)
            logs.append(top + jnp.log(weight_sum))
        out_ref[...] = jnp.concatenate(outs, axis=0).T.astype(BF16)
        log_ref[0, 0:1] = logs[0]
        log_ref[0, 1:2] = logs[1]

    pair = lambda rows: pl.BlockSpec((rows, LANES), lambda i: (0, i))
    return pl.pallas_call(
        kernel,
        grid=(pairs,),
        in_specs=[
            pair(count),
            pair(total),
            pair(total),
            pl.BlockSpec((1, count), lambda i: (0, 0)),
            pl.BlockSpec((total, 1), lambda i: (0, 0)),
        ],
        out_specs=[pair(count), pl.BlockSpec((1, 8, count), lambda i: (i, 0, 0))],
        out_shape=[
            jax.ShapeDtypeStruct((count, width), BF16),
            jax.ShapeDtypeStruct((pairs, 8, count), F32),
        ],
        cost_estimate=pl.CostEstimate(
            flops=16 * count * total * width,
            bytes_accessed=4 * (count + total) * width,
            transcendentals=2 * pairs * count * total,
        ),
        name="attend",
    )(query, keys, values, labels_own[None, :], labels[:, None])


def attend_back(query, keys, values, mixed, grads, logs, labels_own, labels, tables, tables_own, block, before, last):
    count, width = query.shape
    pairs = width // LANES
    scale = HEAD_DIM ** (-0.5)
    cosine, sine = tables
    cosine_own, sine_own = tables_own
    chained = before is not None

    def kernel(block_ref, q_ref, k_ref, v_ref, m_ref, g_ref, log_ref, own_ref, all_ref, c_ref, s_ref, co_ref, so_ref, *rest):
        before_ref = rest[0] if chained else None
        dq_ref, dk_ref, dv_ref = rest[-3:]
        q = q_ref[...]
        k = k_ref[...]
        v = v_ref[...]
        g = g_ref[...]
        same = all_ref[...] == own_ref[...]
        lanes = head_lanes()
        sides = lax.broadcasted_iota(jnp.int32, (LANES, 1), 0) // HEAD_DIM
        k_flipped = k.astype(F32).T
        product = g.astype(F32) * m_ref[...].astype(F32)
        high = product.astype(BF16)
        low = (product - high.astype(F32)).astype(BF16)
        picks = (
            lax.broadcasted_iota(jnp.int32, (8, LANES), 1) // HEAD_DIM
            == lax.broadcasted_iota(jnp.int32, (8, LANES), 0)
        ).astype(F32).astype(BF16)
        delta = nt(picks, high) + nt(picks, low)
        dq = jnp.zeros((LANES, count), F32)
        dk = jnp.zeros((count, LANES), F32)
        dv = jnp.zeros((count, LANES), F32)
        for head in range(2):
            q_masked = jnp.where(lanes == head, q, jnp.zeros_like(q))
            g_masked = jnp.where(lanes == head, g, jnp.zeros_like(g))
            scores = jnp.where(same, nt(k, q_masked), -1e30)
            prob = jnp.exp(scores - log_ref[0, head : head + 1])
            grad_prob = nt(v, g_masked)
            grad_score = (prob * (grad_prob - delta[head : head + 1])).astype(BF16)
            dv = dv + nn(prob.astype(BF16), g_masked)
            dk = dk + nn(grad_score, q_masked)
            k_side = jnp.where(sides == head, k_flipped, 0.0).astype(BF16)
            dq = dq + nn(k_side, grad_score)
        dq = dq.T * scale
        if chained:
            dq = dq + before_ref[...]
        dq_ref[...] = spin(dq, co_ref[...], -so_ref[...]).astype(BF16) if last else dq
        dk_ref[...] = spin(dk, c_ref[...], -s_ref[...]).astype(BF16)
        dv_ref[...] = dv.astype(BF16)

    pair = pl.BlockSpec((count, LANES), lambda i, s: (0, i))
    chosen = pl.BlockSpec((count, LANES), lambda i, s: (s[0], i))
    rows = lambda array: pl.BlockSpec((count, array.shape[1]), lambda i, s: (s[0], 0))
    whole = lambda array: pl.BlockSpec(array.shape, lambda i, s: (0,) * array.ndim)
    labels_own = labels_own[None, :]
    labels = labels[:, None]
    operands = [query, keys, values, mixed, grads, logs, labels_own, labels, cosine, sine, cosine_own, sine_own]
    specs = [
        pair,
        chosen,
        chosen,
        pair,
        pair,
        pl.BlockSpec((1, 8, count), lambda i, s: (i, 0, 0)),
        whole(labels_own),
        rows(labels),
        rows(cosine),
        rows(sine),
        whole(cosine_own),
        whole(sine_own),
    ]
    if chained:
        operands.append(before)
        specs.append(pair)
    return pl.pallas_call(
        kernel,
        grid_spec=pltpu.PrefetchScalarGridSpec(
            num_scalar_prefetch=1, grid=(pairs,), in_specs=specs, out_specs=[pair] * 3
        ),
        out_shape=[
            jax.ShapeDtypeStruct((count, width), BF16 if last else F32),
            jax.ShapeDtypeStruct((count, width), BF16),
            jax.ShapeDtypeStruct((count, width), BF16),
        ],
        cost_estimate=pl.CostEstimate(
            flops=40 * count * count * width,
            bytes_accessed=2 * 9 * count * width,
            transcendentals=2 * pairs * count * count,
        ),
        name="attend_back",
    )(jnp.reshape(block, (1,)), *operands)


def project_back(grads, first, weights, factors, outer, latent, rows, block, base, before):
    shards, _, width, local = weights.shape
    count = grads[0].shape[0]
    rank = factors.shape[0] // 3
    number = len(grads)
    based = base is not None
    added = before is not None
    depth = number * rank

    def kernel(block_ref, w_ref, f_ref, a_ref, l_ref, x_ref, *rest):
        g_refs = rest[:number]
        base_ref = rest[number] if based else None
        before_refs = rest[number + based : number + based + 2] if added else None
        out_ref, part_ref, b_ref, acc_ref, lat_ref = rest[-5:]
        step = pl.program_id(0)

        @pl.when(step == 0)
        def _():
            acc_ref[...] = base_ref[...] if based else jnp.zeros_like(acc_ref)
            lat_ref[...] = jnp.zeros_like(lat_ref)

        total = acc_ref[...]
        lats = []
        parts = []
        for j in range(number):
            p = first + j
            g = g_refs[j][...]
            total = total + nt(g, w_ref[0, p])
            lats.append(nt(g, f_ref[p * rank : (p + 1) * rank]))
            parts.append(tn(l_ref[:, p * rank : (p + 1) * rank], g))
        acc_ref[...] = total
        lat_ref[...] += jnp.concatenate(lats, axis=1)
        if added:
            parts = parts[:1] + [
                part + before_refs[1][step, j * rank : (j + 1) * rank]
                for j, part in enumerate(parts[1:])
            ]
        b_ref[step] = jnp.concatenate(parts, axis=0).astype(b_ref.dtype)

        @pl.when(step == shards - 1)
        def _():
            lat = lat_ref[...].astype(BF16)
            final = acc_ref[...] + nn(lat, a_ref[first * rank :])
            out_ref[...] = final.astype(out_ref.dtype)
            part = tn(lat, x_ref[...])
            if added:
                none = jnp.zeros((rank, width), F32)
                part = part + jnp.concatenate([none, before_refs[0][...]], axis=0)
            part_ref[...] = part.astype(part_ref.dtype)

    whole = lambda array: pl.BlockSpec(array.shape, lambda i, s: (0,) * array.ndim)
    chosen = lambda array: pl.BlockSpec((count, array.shape[1]), lambda i, s: (s[0], 0))
    columns = lambda size: pl.BlockSpec((size, local), lambda i, s: (0, i))
    fixed = lambda size: pl.BlockSpec((size, width), lambda i, s: (0, 0))
    operands = [weights, factors, outer, latent, rows, *grads]
    specs = [
        pl.BlockSpec((1, 3, width, local), lambda i, s: (i, 0, 0, 0)),
        columns(3 * rank),
        whole(outer),
        chosen(latent),
        chosen(rows),
        *[columns(count) for _ in grads],
    ]
    if based:
        operands.append(base)
        specs.append(fixed(count))
    if added:
        operands += list(before)
        specs += [whole(array) for array in before]
    return pl.pallas_call(
        kernel,
        grid_spec=pltpu.PrefetchScalarGridSpec(
            num_scalar_prefetch=1,
            grid=(shards,),
            in_specs=specs,
            out_specs=[
                fixed(count),
                fixed(depth),
                pl.BlockSpec((shards, depth, local), lambda i, s: (0, 0, 0)),
            ],
            scratch_shapes=[
                pltpu.VMEM((count, width), F32),
                pltpu.VMEM((count, depth), F32),
            ],
        ),
        out_shape=[
            jax.ShapeDtypeStruct((count, width), F32 if based else BF16),
            jax.ShapeDtypeStruct((depth, width), BF16 if based else F32),
            jax.ShapeDtypeStruct((shards, depth, local), BF16 if based else F32),
        ],
        cost_estimate=pl.CostEstimate(
            flops=2 * number * count * width * width,
            bytes_accessed=6 * width * width + 2 * (number + 4) * count * width,
            transcendentals=0,
        ),
        name="project_back",
    )(jnp.reshape(block, (1,)), *operands)


def out_forward(mixed, weights, outer, factors, rows, gain, shift, next_factors):
    count, width = mixed.shape
    rank = factors.shape[0]

    def kernel(m_ref, w_ref, a_ref, b_ref, x_ref, g_ref, s_ref, f_ref, hid_ref, hidb_ref, n_ref, i_ref, lo_ref, lf_ref):
        m = m_ref[...]
        latent = nt(m, a_ref[...]).astype(BF16)
        total = x_ref[...].astype(F32) + nn(m, w_ref[...]) + nn(latent, b_ref[...])
        hidden, normed, inverse = norm_forward(total, g_ref[...], s_ref[...])
        hid_ref[...] = hidden
        hidden_b = hidden.astype(BF16)
        hidb_ref[...] = hidden_b
        n_ref[...] = normed
        i_ref[...] = inverse
        lo_ref[...] = latent
        lf_ref[...] = nt(hidden_b, f_ref[...]).astype(BF16)

    full = lambda array: pl.BlockSpec(array.shape, lambda i: (0,) * array.ndim)
    block = min(256, count)
    part = lambda size: pl.BlockSpec((block, size), lambda i: (i, 0))
    operands = [mixed, weights, outer, factors, rows, gain, shift, next_factors]
    return pl.pallas_call(
        kernel,
        grid=(count // block,),
        in_specs=[
            part(width),
            full(weights),
            full(outer),
            full(factors),
            part(width),
            full(gain),
            full(shift),
            full(next_factors),
        ],
        out_specs=[part(width), part(width), part(width), part(1), part(rank), part(2 * rank)],
        out_shape=[
            jax.ShapeDtypeStruct((count, width), F32),
            jax.ShapeDtypeStruct((count, width), BF16),
            jax.ShapeDtypeStruct((count, width), F32),
            jax.ShapeDtypeStruct((count, 1), F32),
            jax.ShapeDtypeStruct((count, rank), BF16),
            jax.ShapeDtypeStruct((count, 2 * rank), BF16),
        ],
        cost_estimate=pl.CostEstimate(
            flops=2 * count * width * width,
            bytes_accessed=2 * width * width + 14 * count * width,
            transcendentals=count,
        ),
        name="out_forward",
    )(*operands)


class Whole:
    def __init__(self, upper, lower):
        self.operands = [upper, lower]
        self.shards, _, self.width, self.units = upper.shape
        self.sub = min(512, self.units)
        self.inner = self.units // self.sub
        self.pick = lambda t, s: t
        width, sub = self.width, self.sub
        self.specs = [
            pl.BlockSpec((1, 2, width, sub), lambda t, b, s: (t, 0, 0, b)),
            pl.BlockSpec((1, sub, width), lambda t, b, s: (t, b, 0)),
        ]

    def up(self, refs, rows, i):
        return nn(rows, refs[0][0, i])

    def up_back(self, refs, grads, i):
        return nt(grads, refs[0][0, i])

    def down(self, refs):
        return refs[1][0]


class Gathered:
    def __init__(self, packed, skip):
        self.operands = [packed, packed]
        shards, self.parts, rows, self.units = packed.shape
        self.shards = shards - skip
        self.width = self.units
        self.sub = self.units // 2
        self.inner = 2
        width, sub = self.width, self.sub
        low = self.units // self.parts
        high = rows - low
        self.pick = lambda t, s: lax.rem(s[0] + skip + t, shards)
        self.specs = [
            pl.BlockSpec((1, self.parts, high, sub), lambda t, b, s: (self.pick(t, s), 0, 0, b)),
            pl.BlockSpec((1, sub // low, low, width), lambda t, b, s: (self.pick(t, s), b, high // low, 0)),
        ]

    def gate_up(self, refs, i):
        half = self.parts // 2
        return refs[0][0, i * half : (i + 1) * half].reshape(self.width, self.sub)

    def up(self, refs, rows, i):
        return nn(rows, self.gate_up(refs, i))

    def up_back(self, refs, grads, i):
        return nt(grads, self.gate_up(refs, i))

    def down(self, refs):
        return refs[1][0].reshape(self.sub, self.width)


def ffn_forward(weights, hidden_b, latent, fb, da, total, down, end, pre, first, number):
    count, width = total.shape
    shards, units = weights.shards, weights.units
    rank = da.shape[1]
    sub, inner = weights.sub, weights.inner
    steps = shards * inner
    scalars = jnp.reshape(lax.axis_index("tensor"), (1,)).astype(jnp.int32)

    def kernel(place_ref, w0_ref, w1_ref, hb_ref, l_ref, fb_ref, da_ref, t_ref, d_ref, *rest):
        refs = (w0_ref, w1_ref)
        step = pl.program_id(0) * inner + pl.program_id(1)
        if pre is not None:
            rest = rest[1:]
        if end:
            db_ref, g_ref, s_ref, c_ref = rest[:4]
            pre_ref, res_ref, mid_ref, midb_ref, ld_ref, ldg_ref, acc_ref, lat_ref = rest[4:]
        else:
            pre_ref, acc_ref, lat_ref = rest

        @pl.when(step == 0)
        def _():
            acc_ref[...] = t_ref[...]
            lat_ref[...] = d_ref[...]

        h = hb_ref[...]
        lat = l_ref[...]
        factor = fb_ref[0]
        gate = weights.up(refs, h, 0) + nn(lat[:, :rank], factor[:rank])
        up = weights.up(refs, h, 1) + nn(lat[:, rank:], factor[rank:])
        pre_ref[0] = gate.astype(BF16)
        pre_ref[1] = up.astype(BF16)
        active = (gate * jax.nn.sigmoid(gate) * up).astype(BF16)
        acc_ref[...] += nn(active, weights.down(refs))
        lat_ref[...] += nt(active, da_ref[0])

        if end:

            @pl.when(step == steps - 1)
            def _():
                latent_down = lat_ref[...].astype(BF16)
                sums = acc_ref[...] + nn(latent_down, db_ref[...])
                result, normed, inverse = norm_forward(sums, g_ref[...], s_ref[...])
                res_ref[...] = result.astype(BF16)
                grad = norm_backward(c_ref[...], normed, inverse, g_ref[...])
                mid_ref[...] = grad
                grad_b = grad.astype(BF16)
                midb_ref[...] = grad_b
                ld_ref[...] = latent_down
                ldg_ref[...] = nt(grad_b, db_ref[...]).astype(BF16)

    full = lambda array: pl.BlockSpec(array.shape, lambda t, b, s: (0,) * array.ndim)
    fixed = lambda size: pl.BlockSpec((count, size), lambda t, b, s: (0, 0))
    operands = [*weights.operands, hidden_b, latent, fb, da, total, down]
    specs = [
        *weights.specs,
        full(hidden_b),
        full(latent),
        pl.BlockSpec((1, 2 * rank, sub), lambda t, b, s: (weights.pick(t, s), 0, b)),
        pl.BlockSpec((1, rank, sub), lambda t, b, s: (weights.pick(t, s), 0, b)),
        full(total),
        full(down),
    ]
    out_specs = [pl.BlockSpec((2, count, sub), lambda t, b, s: (0, 0, (first + t) * inner + b))]
    out_shape = [jax.ShapeDtypeStruct((2, count, number * units), BF16)]
    scratch = []
    aliases = {}
    if pre is not None:
        aliases = {len(operands) + 1: 0}
        operands.append(pre)
        specs.append(pl.BlockSpec(memory_space=pl.ANY))
    if end:
        operands += list(end)
        specs += [full(array) for array in end]
        out_specs += [fixed(width)] * 3 + [fixed(rank)] * 2
        out_shape += [
            jax.ShapeDtypeStruct((count, width), BF16),
            jax.ShapeDtypeStruct((count, width), F32),
            jax.ShapeDtypeStruct((count, width), BF16),
            jax.ShapeDtypeStruct((count, rank), BF16),
            jax.ShapeDtypeStruct((count, rank), BF16),
        ]
        scratch = [pltpu.VMEM((count, width), F32), pltpu.VMEM((count, rank), F32)]
    else:
        out_specs += [fixed(width), fixed(rank)]
        out_shape += [
            jax.ShapeDtypeStruct((count, width), F32),
            jax.ShapeDtypeStruct((count, rank), F32),
        ]
    return pl.pallas_call(
        kernel,
        grid_spec=pltpu.PrefetchScalarGridSpec(
            num_scalar_prefetch=1,
            grid=(shards, inner),
            in_specs=specs,
            out_specs=out_specs,
            scratch_shapes=scratch,
        ),
        out_shape=out_shape,
        input_output_aliases=aliases,
        cost_estimate=pl.CostEstimate(
            flops=6 * count * width * shards * units,
            bytes_accessed=6 * width * shards * units + 4 * count * shards * units,
            transcendentals=count * shards * units,
        ),
        name="ffn_forward",
    )(scalars, *operands)


def ffn_backward(weights, grad_b, pre, latent_down_grad, latent_ffn, fb, da, total, end):
    count, width = total.shape
    shards, units = weights.shards, weights.units
    rank = da.shape[1]
    sub, inner = weights.sub, weights.inner
    steps = shards * inner
    scalars = jnp.reshape(lax.axis_index("tensor"), (1,)).astype(jnp.int32)

    def kernel(place_ref, w0_ref, w1_ref, gb_ref, pre_ref, ldg_ref, lf_ref, fb_ref, da_ref, t_ref, *rest):
        refs = (w0_ref, w1_ref)
        step = pl.program_id(0) * inner + pl.program_id(1)
        ld_ref, fa_ref, hb_ref, n_ref, i_ref, gain_ref, lo_ref, ob_ref, oa_ref, m_ref, wo_ref = rest[:11]
        split_ref, first_ref, mixed_ref, common_ref, acc_ref, lat_ref = rest[11:]

        @pl.when(step == 0)
        def _():
            acc_ref[...] = t_ref[...]
            lat_ref[...] = jnp.zeros_like(lat_ref)

        ldg = ldg_ref[...]
        lf = lf_ref[...]
        factor = fb_ref[0]
        grad_active = nt(gb_ref[...], weights.down(refs)) + nn(ldg, da_ref[0])
        gate = pre_ref[0].astype(F32)
        up = pre_ref[1].astype(F32)
        sigma = jax.nn.sigmoid(gate)
        swish = gate * sigma
        active = (swish * up).astype(BF16)
        grad_gate = (grad_active * up * (sigma + swish * (1.0 - sigma))).astype(BF16)
        grad_up = (grad_active * swish).astype(BF16)
        split = jnp.concatenate(
            [tn(ldg, active), tn(lf[:, :rank], grad_gate), tn(lf[:, rank:], grad_up)], axis=0
        )
        split_ref[0] = split.astype(BF16)
        acc_ref[...] += weights.up_back(refs, grad_gate, 0) + weights.up_back(refs, grad_up, 1)
        lat_ref[...] += jnp.concatenate(
            [nt(grad_gate, factor[:rank]), nt(grad_up, factor[rank:])], axis=1
        )

        @pl.when(step == steps - 1)
        def _():
            lat = lat_ref[...].astype(BF16)
            sums = acc_ref[...] + nn(lat, fa_ref[...])
            first = norm_backward(sums, n_ref[...], i_ref[...], gain_ref[...])
            first_ref[...] = first
            branch = first.astype(BF16)
            log = nt(branch, ob_ref[...]).astype(BF16)
            common_ref[...] = jnp.concatenate(
                [
                    tn(ld_ref[...], gb_ref[...]),
                    tn(lat, hb_ref[...]),
                    tn(lo_ref[...], branch),
                    tn(log, m_ref[...]),
                ],
                axis=0,
            ).astype(BF16)
            mixed_ref[...] = (nt(branch, wo_ref[...]) + nn(log, oa_ref[...])).astype(BF16)

    full = lambda array: pl.BlockSpec(array.shape, lambda t, b, s: (0,) * array.ndim)
    fixed = lambda rows, size: pl.BlockSpec((rows, size), lambda t, b, s: (0, 0))
    operands = [*weights.operands, grad_b, pre, latent_down_grad, latent_ffn, fb, da, total, *end]
    specs = [
        *weights.specs,
        full(grad_b),
        pl.BlockSpec((2, count, sub), lambda t, b, s: (0, 0, t * inner + b)),
        full(latent_down_grad),
        full(latent_ffn),
        pl.BlockSpec((1, 2 * rank, sub), lambda t, b, s: (weights.pick(t, s), 0, b)),
        pl.BlockSpec((1, rank, sub), lambda t, b, s: (weights.pick(t, s), 0, b)),
        full(total),
        *[full(array) for array in end],
    ]
    out_specs = [pl.BlockSpec((1, 3 * rank, sub), lambda t, b, s: (t, 0, b))]
    out_shape = [jax.ShapeDtypeStruct((shards, 3 * rank, units), BF16)]
    out_specs += [fixed(count, width), fixed(count, width), fixed(5 * rank, width)]
    out_shape += [
        jax.ShapeDtypeStruct((count, width), F32),
        jax.ShapeDtypeStruct((count, width), BF16),
        jax.ShapeDtypeStruct((5 * rank, width), BF16),
    ]
    scratch = [pltpu.VMEM((count, width), F32), pltpu.VMEM((count, 2 * rank), F32)]
    return pl.pallas_call(
        kernel,
        grid_spec=pltpu.PrefetchScalarGridSpec(
            num_scalar_prefetch=1,
            grid=(shards, inner),
            in_specs=specs,
            out_specs=out_specs,
            scratch_shapes=scratch,
        ),
        out_shape=out_shape,
        cost_estimate=pl.CostEstimate(
            flops=6 * count * width * shards * units,
            bytes_accessed=6 * width * shards * units + 4 * count * shards * units,
            transcendentals=count * shards * units,
        ),
        name="ffn_backward",
    )(scalars, *operands)


def norm_forward(rows, gain, shift):
    centre = jnp.mean(rows, axis=-1, keepdims=True)
    centred = rows - centre
    spread = jnp.mean(centred * centred, axis=-1, keepdims=True)
    inverse = lax.rsqrt(spread + 1e-12)
    normed = centred * inverse
    return (normed * gain + shift, normed, inverse)


def norm_backward(grads, normed, inverse, gain):
    scaled = grads * gain
    first_mean = jnp.mean(scaled, axis=-1, keepdims=True)
    second_mean = jnp.mean(scaled * normed, axis=-1, keepdims=True)
    return inverse * (scaled - first_mean - normed * second_mean)


def rope_tables(length, extra):
    half = HEAD_DIM // 2
    step = 64
    freq = 10000.0 ** (-(2.0 * np.arange(half)) / HEAD_DIM)
    freq = np.tile(freq, LANES // half)
    sign = np.where(np.arange(LANES) % HEAD_DIM < half, -1.0, 1.0)
    coarse = ((np.arange(length + extra) % length)[::step, None] * freq).astype(np.float64)
    fine = np.arange(step)[:, None] * freq
    f = lambda array: jnp.asarray(array, F32)
    cos_c, sin_c = f(np.cos(coarse))[:, None], f(np.sin(coarse))[:, None]
    cos_f, sin_f = f(np.cos(fine))[None], f(np.sin(fine))[None]
    cosine = (cos_c * cos_f - sin_c * sin_f).reshape(-1, LANES)
    sine = ((sin_c * cos_f + cos_c * sin_f) * f(sign)).reshape(-1, LANES)
    return cosine, sine


def window(array, start, count):
    return lax.dynamic_slice_in_dim(array, start, count, 0)


def gather_weight(local, parts, part):
    rows = local.shape[0] // parts
    piece = window(local, part * rows, rows)
    return lax.all_gather(piece, ALL, axis=0, tiled=True)


def gather_ffn(w_gate_up, w_down, parts, part):
    _, width, units = w_gate_up.shape
    upper = w_gate_up.reshape(2 * width, units)
    if units == width and width % (128 * parts // 8) == 0 and parts == 8:
        high, low = 2 * width // parts, units // parts
        piece = jnp.concatenate(
            [window(upper, part * high, high), window(w_down, part * low, low)], axis=0
        )
        whole = lax.all_gather(piece, ALL, axis=0, tiled=True)
        return (whole.reshape(-1, parts, high + low, units),)
    return (
        gather_weight(upper, parts, part).reshape(-1, 2, width, units),
        gather_weight(w_down, parts, part).reshape(-1, units, width),
    )


def flip(bit):
    return [(i, i ^ bit) for i in range(4)]


def send_round(piece):
    shards = lax.axis_size("tensor")
    return [lax.ppermute(piece, "tensor", cyclic(shards, k)) for k in range(1, shards)]


def spread_first(stack):
    return lax.ppermute(stack, "yx", flip(1)), lax.ppermute(stack, "yx", flip(2))


def spread_second(across, along):
    half = across.shape[0] // 2
    return (
        lax.ppermute(across[:half], "yx", flip(2)),
        lax.ppermute(along[half:], "yx", flip(1)),
    )


def swap_core(near):
    return lax.ppermute(near, "core", [(0, 1), (1, 0)])


def assemble(own, near, far, outs, store):
    shards = near.shape[1] + 1
    rows, cols = own.shape[1:]
    scalars = jnp.stack(
        [lax.axis_index("tensor"), lax.axis_index("yx"), lax.axis_index("core")]
    ).astype(jnp.int32)

    def behind(t, s):
        return lax.rem(s[0] - t + shards, shards)

    def kernel(scalar_ref, own_ref, near_ref, far_ref, *out_refs):
        mine = behind(pl.program_id(0), scalar_ref) == 0
        first = scalar_ref[2] == 0

        @pl.when(mine)
        def _():
            for j in range(8):
                store(own_ref[j], j, out_refs)

        for low_ref, high_ref, here in ((near_ref, far_ref, first), (far_ref, near_ref, jnp.logical_not(first))):

            @pl.when(jnp.logical_and(jnp.logical_not(mine), here))
            def _():
                for i in range(4):
                    side = lax.bitwise_xor(scalar_ref[1], i)
                    store(low_ref[side, 0], 2 * i, out_refs)
                    store(high_ref[side, 0], 2 * i + 1, out_refs)

    other = pl.BlockSpec(
        (4, 1, rows, cols), lambda t, s: (0, jnp.maximum(behind(t, s) - 1, 0), 0, 0)
    )
    return pl.pallas_call(
        kernel,
        grid_spec=pltpu.PrefetchScalarGridSpec(
            num_scalar_prefetch=1,
            grid=(shards,),
            in_specs=[pl.BlockSpec((8, rows, cols), lambda t, s: (0, 0, 0)), other, other],
            out_specs=[spec for _, spec in outs],
        ),
        out_shape=[jax.ShapeDtypeStruct(shape, BF16) for shape, _ in outs],
        cost_estimate=pl.CostEstimate(
            flops=0, bytes_accessed=32 * shards * rows * cols, transcendentals=0
        ),
    )(scalars, own, near, far)


def assemble_qkv(own, near, far, width, local):
    shards = near.shape[1] + 1
    size = width // 8
    short = local // 8
    head = 3 * size

    def store(piece, j, outs):
        for p in range(3):
            outs[0][0, p, j * size : (j + 1) * size] = piece[p * size : (p + 1) * size]
        for c in range(width // local):
            outs[1][j * short : (j + 1) * short, c * local : (c + 1) * local] = piece[
                head + c * short : head + (c + 1) * short
            ]

    outs = [
        (
            (shards, 3, width, local),
            pl.BlockSpec((1, 3, width, local), lambda t, s: (t, 0, 0, 0)),
        ),
        ((shards * local, width), pl.BlockSpec((local, width), lambda t, s: (t, 0))),
    ]
    return assemble(own, near, far, outs, store)


def in_order(blocks, place):
    shards = len(blocks)
    stack = jnp.stack(blocks)
    return jnp.stack(
        [
            lax.dynamic_index_in_dim(stack, lax.rem(place - t + shards, shards), 0, keepdims=False)
            for t in range(shards)
        ]
    )


def cyclic(size, step):
    return [(i, (i + step) % size) for i in range(size)]


def send_grads(share):
    shards = lax.axis_size("tensor")
    place = lax.axis_index("tensor")
    received = [share(place)]
    for step in range(1, shards):
        sent = share(lax.rem(place + step, shards))
        received.append(lax.ppermute(sent, "tensor", cyclic(shards, step)))
    return received


def add_all(blocks):
    total = blocks[0].astype(F32)
    for block in blocks[1:]:
        total = total + block.astype(F32)
    return total


def line_gather(block):
    shards = lax.axis_size("tensor")
    blocks = [(block, 0)]
    up = down = block
    for step in range(1, shards):
        links = [(i, i + 1) for i in range(step - 1, shards - 1)]
        up = lax.ppermute(up, "tensor", links)
        down = lax.ppermute(down, "tensor", [(shards - 1 - i, shards - 1 - j) for i, j in links])
        blocks += [(up, -step), (down, step)]
    return blocks


def after(array, *marks):
    return lax.optimization_barrier((array, *marks))[0]


def place_sums(every, plan, adapters, place):
    count, rows, width = every.shape
    rows -= 16
    owners = jnp.sum(
        every[:, rows, :adapters].astype(jnp.int32) * jnp.arange(adapters, dtype=jnp.int32), axis=1
    )
    scalars = jnp.concatenate([jnp.reshape(place, (1,)), owners]).astype(jnp.int32)

    def kernel(scalar_ref, every_ref, *refs):
        outs, total_ref = refs[:-1], refs[-1]
        adapter = pl.program_id(0)
        total_ref[...] = jnp.zeros_like(total_ref)
        for s in range(count):

            @pl.when(scalar_ref[1 + s] == adapter)
            def _():
                total_ref[...] += every_ref[s, :rows].astype(F32)

        for (first, size, columns), out in zip(plan, outs):
            if columns is None:
                out[0] = total_ref[first : first + size]
            else:
                start = pl.multiple_of(scalar_ref[0] * columns, LANES)
                out[0] = total_ref[first : first + size, pl.ds(start, columns)]

    shapes = [(adapters, size, width if columns is None else columns) for _, size, columns in plan]
    return pl.pallas_call(
        kernel,
        grid_spec=pltpu.PrefetchScalarGridSpec(
            num_scalar_prefetch=1,
            grid=(adapters,),
            in_specs=[pl.BlockSpec(every.shape, lambda i, s: (0, 0, 0))],
            out_specs=[pl.BlockSpec((1,) + shape[1:], lambda i, s: (i, 0, 0)) for shape in shapes],
            scratch_shapes=[pltpu.VMEM((rows, width), F32)],
        ),
        out_shape=[jax.ShapeDtypeStruct(shape, F32) for shape in shapes],
        cost_estimate=pl.CostEstimate(
            flops=count * rows * width,
            bytes_accessed=(2 * count + 4 * adapters) * rows * width,
            transcendentals=0,
        ),
        name="place_sums",
    )(scalars, every)


def after(array, *marks):
    return lax.optimization_barrier((array, *marks))[0]


def layer(
    layer_input,
    output_grad,
    segments,
    adapter_ids,
    ln_gain,
    ln_bias,
    w_qkv,
    w_out,
    w_gate_up,
    w_down,
    qkv_a,
    qkv_b,
    out_a,
    out_b,
    ffn_a,
    ffn_b,
    down_a,
    down_b,
):
    seq_count, length = segments.shape
    assert seq_count == 1
    width = layer_input.shape[1]
    shards = lax.axis_size("tensor")
    parts = lax.axis_size(DP)
    place = lax.axis_index("tensor")
    part = lax.axis_index(DP)
    members = shards // 2
    half = length // 2
    count = length // shards
    group = place // members
    member = lax.rem(place, members)
    local = w_qkv.shape[2]
    units = w_down.shape[0]
    rank = out_b.shape[1]

    adapter = adapter_ids[0, 0]
    pick = lambda stack: lax.dynamic_index_in_dim(stack, adapter, 0, keepdims=False)
    qa, ob, fa, db = pick(qkv_a), pick(out_b), pick(ffn_a), pick(down_b)
    small = jnp.concatenate(
        [
            pick(qkv_b),
            pick(out_a),
            pick(ffn_b).reshape(-1, local),
            pick(down_a).reshape(-1, local),
        ],
        axis=0,
    )
    labels = segments[0]
    long = labels[: length - half + 1] == labels[half - 1 :]
    start = jnp.sum(jnp.where(long, jnp.arange(length - half + 1, dtype=jnp.int32), 0))
    group_start = start + group * half
    own_start = start + place * count
    x_group = roll_rows([(layer_input, 0)], place, group_start, half, BF16)
    x_own_b = window(x_group, member * count, count)
    cotangent = roll_rows([(output_grad, 0)], place, own_start, count, F32)
    labels_twice = jnp.concatenate([labels, labels[:half]])
    labels_group = window(labels_twice, group_start, half)
    labels_own = window(labels_group, member * count, count)
    cosine, sine = rope_tables(length, half)
    tables = (window(cosine, group_start, half), window(sine, group_start, half))
    tables_own = tuple(window(table, member * count, count) for table in tables)

    ffn_all = gather_ffn(w_gate_up, w_down, parts, part)
    if parts == 8:
        qkv_pieces = w_qkv.reshape(3, 8, width // 8, local).transpose(1, 0, 2, 3)
        out_pieces = w_out.reshape(8, local // 8, width // local, local).transpose(0, 2, 1, 3)
        pieces = jnp.concatenate(
            [
                qkv_pieces.reshape(8, 3 * width // 8, local),
                out_pieces.reshape(8, width // 8, local),
            ],
            axis=1,
        )
        piece = lax.dynamic_index_in_dim(pieces, part, 0, keepdims=False)
        joined = send_round(jnp.concatenate([piece, small], axis=0))
        size = piece.shape[0]
        small = in_order([small] + [block[size:] for block in joined], place)
        stack = jnp.concatenate([block[:size] for block in joined], axis=0)
        stack = after(stack, x_group, cotangent)
        across, along = spread_first(stack)
        corner = jnp.concatenate(spread_second(across, along), axis=0)
        near = jnp.stack([stack, across, along, corner]).reshape(4, shards - 1, size, local)
        far = swap_core(near)
        qkv_all, out_all = assemble_qkv(pieces, near, far, width, local)
    else:
        qkv_all = gather_weight(w_qkv.reshape(3 * width, local), parts, part)
        qkv_all = qkv_all.reshape(shards, 3, width, local)
        out_all = gather_weight(w_out, parts, part)
        small = lax.all_gather(small, "tensor", axis=0)
    cuts = np.cumsum([3 * rank, rank, 2 * rank * (units // local)])
    rejoin = lambda piece: piece.transpose(1, 0, 2).reshape(piece.shape[1], -1)
    qb = rejoin(small[:, : cuts[0]])
    oa = rejoin(small[:, cuts[0] : cuts[1]])
    fb = small[:, cuts[1] : cuts[2]].reshape(shards, 2 * rank, units)
    da = small[:, cuts[2] :].reshape(shards, rank, units)

    latent_qkv = nt(x_group, qa).astype(BF16)
    latent_own = window(latent_qkv, member * count, count)
    query, keys, values = project_qkv(
        x_group, x_own_b, qkv_all, latent_qkv, latent_own, qb, tables, tables_own
    )
    mixed, logs = attend(query, keys, values, labels_own, labels_group)
    hidden, hidden_b, normed, inverse, latent_out, latent_ffn = out_forward(
        mixed, out_all, oa, ob, x_own_b, ln_gain[:1], ln_bias[:1], fa
    )

    zero = jnp.zeros((count, rank), F32)
    end = (db, ln_gain[1:], ln_bias[1:], cotangent)
    packed = len(ffn_all) == 1
    if packed:
        mine = lambda stack: lax.dynamic_slice_in_dim(stack, place, 1, 0)
        own = Whole(w_gate_up[None], w_down[None])
        pre, total, down = ffn_forward(
            own, hidden_b, latent_ffn, mine(fb), mine(da), hidden, zero, None, None, 0, shards
        )
        others, every = Gathered(ffn_all[0], 1), Gathered(ffn_all[0], 0)
    else:
        pre, total, down = None, hidden, zero
        others = every = Whole(*ffn_all)
    pre, result, grad_mid, grad_ffn, latent_down, latent_down_grad = ffn_forward(
        others, hidden_b, latent_ffn, fb, da, total, down, end, pre, shards - others.shards, shards
    )
    rolled = lax.all_gather(result, "tensor", axis=0, tiled=True)

    end = (
        latent_down, fa, hidden_b, normed, inverse, ln_gain[:1], latent_out, ob, oa, mixed, out_all,
    )
    split, grad_first, grad_mixed, common = ffn_backward(
        every, grad_ffn, pre, latent_down_grad, latent_ffn, fb, da, grad_mid, end
    )

    dq = None
    received = []
    before = None
    for d in range(1, members):
        target = lax.rem(member + d, members)
        dq, dk, dv = attend_back(
            query, keys, values, mixed, grad_mixed, logs, labels_own, labels_group, tables,
            tables_own, target, dq, False,
        )
        sent, *part_of = project_back(
            [dk, dv], 1, qkv_all, qb, qa, latent_qkv, x_group, target, None, None
        )
        before = part_of if before is None else [a + b for a, b in zip(before, part_of)]
        links = [
            (g * members + i, g * members + (i + d) % members)
            for g in range(2)
            for i in range(members)
        ]
        received.append(lax.ppermute(sent, "tensor", links))

    def early_share(target):
        entry = lax.rem(target - place + shards, shards) if packed else target
        mine = lax.dynamic_index_in_dim(split, entry, 0, keepdims=False)
        return jnp.concatenate([common, mine.reshape(-1, width)], axis=0)

    def late_share(target):
        mine = lax.dynamic_index_in_dim(qkv_b_part, target, 0, keepdims=False)
        return jnp.concatenate([qkv_a_part, mine.reshape(-1, width)], axis=0)

    common = after(common, sent)
    early = send_grads(early_share)
    dq, dk, dv = attend_back(
        query, keys, values, mixed, grad_mixed, logs, labels_own, labels_group, tables, tables_own,
        member, dq, True,
    )
    back, qkv_a_part, qkv_b_part = project_back(
        [dq, dk, dv], 0, qkv_all, qb, qa, latent_qkv, x_group, member, grad_first, before
    )
    late = send_grads(late_share)

    adapters = qkv_a.shape[0]
    hot = (adapter == jnp.arange(adapters, dtype=jnp.int32)).astype(BF16)
    flag = jnp.zeros((16, width), BF16).at[0, :adapters].set(hot)
    for piece in received:
        back = back + after(piece, back).astype(F32)
    back = back.astype(BF16)
    blocks = line_gather(back)
    output = roll_rows([(after(rolled, back), 0)], place, -start, length, BF16)
    early_sum = add_all([early[0]] + [after(piece, output) for piece in early[1:]]).astype(BF16)
    late_sum = add_all([late[0]] + [after(piece, output) for piece in late[1:]]).astype(BF16)
    every_sum = lax.all_gather(jnp.concatenate([early_sum, late_sum, flag], axis=0), DP, axis=0)
    plan = [
        (0, rank, None),
        (rank, 2 * rank, None),
        (3 * rank, rank, None),
        (4 * rank, rank, local),
    ]
    straight = units == width
    if straight:
        plan += [(5 * rank, rank, None), (6 * rank, 2 * rank, None)]
    else:
        plan += [(5 * rank, 3 * rank * units // width, None)]
    mark = early_sum.shape[0]
    plan += [
        (mark, 3 * rank, None),
        (mark + 3 * rank, 3 * rank * local // width, None),
    ]
    grads = place_sums(every_sum, plan, adapters, place)
    down_b_grad, ffn_a_grad, out_b_grad, out_a_grad = grads[:4]
    if straight:
        down_a_grad, ffn_b_grad = grads[4:6]
    else:
        own_split = grads[4].reshape(adapters, 3 * rank, units)
        down_a_grad, ffn_b_grad = own_split[:, :rank], own_split[:, rank:]
    qkv_a_grad, qkv_b_grad = grads[-2:]
    qkv_b_grad = qkv_b_grad.reshape(adapters, 3 * rank, local)

    blocks = [(after(block, output, qkv_a_grad, out_b_grad), i) for block, i in blocks]
    grad_whole = roll_rows(blocks, place, -start, length, F32)
    return (
        output,
        grad_whole,
        qkv_a_grad,
        qkv_b_grad,
        out_a_grad,
        out_b_grad,
        ffn_a_grad,
        ffn_b_grad,
        down_a_grad,
        down_b_grad,
    )


def solution(mesh):
    devices = mesh.devices
    mesh = Mesh(
        devices.reshape(devices.shape[0] // 2, 2, devices.shape[1]), ("yx", "core", "tensor")
    )
    in_specs = (
        P(DP, None),
        P(DP, None),
        P(DP, None),
        P(DP, None),
        P(),
        P(),
        P(None, None, "tensor"),
        P("tensor", None),
        P(None, None, "tensor"),
        P("tensor", None),
        P(),
        P(None, None, "tensor"),
        P(None, None, "tensor"),
        P(),
        P(),
        P(None, None, "tensor"),
        P(None, None, "tensor"),
        P(),
    )
    out_specs = (
        P(DP, None),
        P(DP, None),
        P(),
        P(None, None, "tensor"),
        P(None, None, "tensor"),
        P(),
        P(),
        P(None, None, "tensor"),
        P(None, None, "tensor"),
        P(),
    )
    return jax.shard_map(layer, mesh=mesh, in_specs=in_specs, out_specs=out_specs, check_vma=False)
```

```python
import jax
import jax.numpy as jnp
import numpy as np
from jax import lax
from jax.experimental import pallas as pl
from jax.experimental.pallas import tpu as pltpu
from jax.sharding import Mesh
from jax.sharding import PartitionSpec as P


HEAD_DIM = 64
LANES = 128
DP = ("yx", "core")
ALL = ("tensor", "yx", "core")
F32 = jnp.float32
BF16 = jnp.bfloat16


def nt(left, right):
    return lax.dot_general(left, right, (((1,), (1,)), ((), ())), preferred_element_type=F32)


def tn(left, right):
    return lax.dot_general(left, right, (((0,), (0,)), ((), ())), preferred_element_type=F32)


def nn(left, right):
    return jnp.dot(left, right, preferred_element_type=F32)


def roll_rows(pieces, place, shift, count, dtype):
    pieces, offsets = zip(*pieces)
    number = len(pieces)
    size, width = pieces[0].shape
    group = lax.axis_size("tensor") if number > 1 else 1
    length = group * size
    unit = LANES
    units = length // unit
    block = min(1024, count)
    shift = lax.rem(shift + length, length)
    first = shift // unit
    scalars = jnp.stack([first, shift - first * unit, place]).astype(jnp.int32)

    def kernel(scalar_ref, *refs):
        out_ref = refs[number]
        step = pl.program_id(0)
        if number > 1:
            rows_ref = refs[number + 1]

            @pl.when(step == 0)
            def _():
                for k in range(number):
                    member = scalar_ref[2] + offsets[k]

                    @pl.when(jnp.logical_and(member >= 0, member < group))
                    def _():
                        rows_ref[pl.ds(pl.multiple_of(member * size, size), size)] = refs[k][...]
        else:
            rows_ref = refs[0]
        offset = scalar_ref[1]
        row = lax.broadcasted_iota(jnp.int32, (unit, 2 * unit), 0)
        column = lax.broadcasted_iota(jnp.int32, (unit, 2 * unit), 1)
        move = jnp.where(column == row + offset, 1.0, 0.0).astype(BF16)
        for s in range(block // unit):
            base = scalar_ref[0] + step * (block // unit) + s
            low = rows_ref[pl.ds(pl.multiple_of(lax.rem(base, units) * unit, unit), unit)]
            high = rows_ref[pl.ds(pl.multiple_of(lax.rem(base + 1, units) * unit, unit), unit)]
            pair = jnp.concatenate([low, high], axis=0)
            out_ref[s * unit : (s + 1) * unit] = nn(move, pair).astype(dtype)

    return pl.pallas_call(
        kernel,
        grid_spec=pltpu.PrefetchScalarGridSpec(
            num_scalar_prefetch=1,
            grid=(count // block,),
            in_specs=[pl.BlockSpec((size, width), lambda i, s: (0, 0))] * number,
            out_specs=pl.BlockSpec((block, width), lambda i, s: (i, 0)),
            scratch_shapes=[pltpu.VMEM((length, width), BF16)] if number > 1 else [],
        ),
        out_shape=jax.ShapeDtypeStruct((count, width), dtype),
        cost_estimate=pl.CostEstimate(
            flops=4 * count * unit * width,
            bytes_accessed=2 * length * width + 4 * count * width,
            transcendentals=0,
        ),
        name="roll_rows",
    )(scalars, *pieces)


def spin(values, cosine, sine):
    lane = lax.broadcasted_iota(jnp.int32, (1, LANES), 1)
    first = lax.rem(lane, HEAD_DIM) < HEAD_DIM // 2
    parts = []
    for start in range(0, values.shape[1], LANES):
        piece = values[:, start : start + LANES]
        ahead = pltpu.roll(piece, LANES - HEAD_DIM // 2, 1)
        behind = pltpu.roll(piece, HEAD_DIM // 2, 1)
        parts.append(piece * cosine + jnp.where(first, ahead, behind) * sine)
    return parts[0] if len(parts) == 1 else jnp.concatenate(parts, axis=1)


def project_qkv(group, own, weights, latent, latent_own, factors, tables, tables_own):
    shards, _, width, local = weights.shape
    count, total = own.shape[0], group.shape[0]
    rank = latent.shape[1] // 3
    scale = HEAD_DIM ** (-0.5)

    def kernel(x_ref, o_ref, w_ref, l_ref, lo_ref, f_ref, c_ref, s_ref, co_ref, so_ref, q_ref, k_ref, v_ref):
        x = x_ref[...]
        lat = l_ref[...]
        factor = f_ref[...]
        query = nn(o_ref[...], w_ref[0, 0]) + nn(lo_ref[...][:, :rank], factor[:rank])
        q_ref[...] = (spin(query, co_ref[...], so_ref[...]).astype(BF16) * scale).astype(BF16)
        key = nn(x, w_ref[0, 1]) + nn(lat[:, rank : 2 * rank], factor[rank : 2 * rank])
        k_ref[...] = spin(key, c_ref[...], s_ref[...]).astype(BF16)
        value = nn(x, w_ref[0, 2]) + nn(lat[:, 2 * rank :], factor[2 * rank :])
        v_ref[...] = value.astype(BF16)

    def whole(array):
        return pl.BlockSpec(array.shape, lambda i: (0,) * array.ndim)

    def columns(rows):
        return pl.BlockSpec((rows, local), lambda i: (0, i))

    cosine, sine = tables
    cosine_own, sine_own = tables_own
    return pl.pallas_call(
        kernel,
        grid=(shards,),
        in_specs=[
            whole(group),
            whole(own),
            pl.BlockSpec((1, 3, width, local), lambda i: (i, 0, 0, 0)),
            whole(latent),
            whole(latent_own),
            columns(factors.shape[0]),
            whole(cosine),
            whole(sine),
            whole(cosine_own),
            whole(sine_own),
        ],
        out_specs=[columns(count), columns(total), columns(total)],
        out_shape=[
            jax.ShapeDtypeStruct((count, width), BF16),
            jax.ShapeDtypeStruct((total, width), BF16),
            jax.ShapeDtypeStruct((total, width), BF16),
        ],
        cost_estimate=pl.CostEstimate(
            flops=2 * width * width * (count + 2 * total),
            bytes_accessed=2 * (4 * width * width + 6 * total * width),
            transcendentals=0,
        ),
        name="project_qkv",
    )(group, own, weights, latent, latent_own, factors, cosine, sine, cosine_own, sine_own)


def head_lanes():
    return lax.broadcasted_iota(jnp.int32, (1, LANES), 1) // HEAD_DIM


def attend(query, keys, values, labels_own, labels):
    count, width = query.shape
    total = keys.shape[0]
    pairs = width // LANES

    def kernel(q_ref, k_ref, v_ref, own_ref, all_ref, out_ref, log_ref):
        q = q_ref[...]
        k = k_ref[...]
        flipped = v_ref[...].astype(F32).T
        same = all_ref[...] == own_ref[...]
        lanes = head_lanes()
        sides = lax.broadcasted_iota(jnp.int32, (LANES, 1), 0) // HEAD_DIM
        outs = []
        logs = []
        for head in range(2):
            masked = jnp.where(lanes == head, q, jnp.zeros_like(q))
            scores = jnp.where(same, nt(k, masked), -1e30)
            top = jnp.max(scores, axis=0, keepdims=True)
            expo = jnp.exp(scores - top).astype(BF16)
            stacked = jnp.where(sides == head, flipped, 1.0).astype(BF16)
            product = nn(stacked, expo)
            other = (1 - head) * HEAD_DIM
            weight_sum = product[other : other + 1]
            outs.append(product[head * HEAD_DIM : (head + 1) * HEAD_DIM] / weight_sum)
            logs.append(top + jnp.log(weight_sum))
        out_ref[...] = jnp.concatenate(outs, axis=0).T.astype(BF16)
        log_ref[0, 0:1] = logs[0]
        log_ref[0, 1:2] = logs[1]

    pair = lambda rows: pl.BlockSpec((rows, LANES), lambda i: (0, i))
    return pl.pallas_call(
        kernel,
        grid=(pairs,),
        in_specs=[
            pair(count),
            pair(total),
            pair(total),
            pl.BlockSpec((1, count), lambda i: (0, 0)),
            pl.BlockSpec((total, 1), lambda i: (0, 0)),
        ],
        out_specs=[pair(count), pl.BlockSpec((1, 8, count), lambda i: (i, 0, 0))],
        out_shape=[
            jax.ShapeDtypeStruct((count, width), BF16),
            jax.ShapeDtypeStruct((pairs, 8, count), F32),
        ],
        cost_estimate=pl.CostEstimate(
            flops=16 * count * total * width,
            bytes_accessed=4 * (count + total) * width,
            transcendentals=2 * pairs * count * total,
        ),
        name="attend",
    )(query, keys, values, labels_own[None, :], labels[:, None])


def attend_back(query, keys, values, mixed, grads, logs, labels_own, labels, tables, tables_own, block, before, last):
    count, width = query.shape
    pairs = width // LANES
    scale = HEAD_DIM ** (-0.5)
    cosine, sine = tables
    cosine_own, sine_own = tables_own
    chained = before is not None

    def kernel(block_ref, q_ref, k_ref, v_ref, m_ref, g_ref, log_ref, own_ref, all_ref, c_ref, s_ref, co_ref, so_ref, *rest):
        before_ref = rest[0] if chained else None
        dq_ref, dk_ref, dv_ref = rest[-3:]
        q = q_ref[...]
        k = k_ref[...]
        v = v_ref[...]
        g = g_ref[...]
        same = all_ref[...] == own_ref[...]
        lanes = head_lanes()
        sides = lax.broadcasted_iota(jnp.int32, (LANES, 1), 0) // HEAD_DIM
        k_flipped = k.astype(F32).T
        product = g.astype(F32) * m_ref[...].astype(F32)
        high = product.astype(BF16)
        low = (product - high.astype(F32)).astype(BF16)
        picks = (
            lax.broadcasted_iota(jnp.int32, (8, LANES), 1) // HEAD_DIM
            == lax.broadcasted_iota(jnp.int32, (8, LANES), 0)
        ).astype(F32).astype(BF16)
        delta = nt(picks, high) + nt(picks, low)
        dq = jnp.zeros((LANES, count), F32)
        dk = jnp.zeros((count, LANES), F32)
        dv = jnp.zeros((count, LANES), F32)
        for head in range(2):
            q_masked = jnp.where(lanes == head, q, jnp.zeros_like(q))
            g_masked = jnp.where(lanes == head, g, jnp.zeros_like(g))
            scores = jnp.where(same, nt(k, q_masked), -1e30)
            prob = jnp.exp(scores - log_ref[0, head : head + 1])
            grad_prob = nt(v, g_masked)
            grad_score = (prob * (grad_prob - delta[head : head + 1])).astype(BF16)
            dv = dv + nn(prob.astype(BF16), g_masked)
            dk = dk + nn(grad_score, q_masked)
            k_side = jnp.where(sides == head, k_flipped, 0.0).astype(BF16)
            dq = dq + nn(k_side, grad_score)
        dq = dq.T * scale
        if chained:
            dq = dq + before_ref[...]
        dq_ref[...] = spin(dq, co_ref[...], -so_ref[...]).astype(BF16) if last else dq
        dk_ref[...] = spin(dk, c_ref[...], -s_ref[...]).astype(BF16)
        dv_ref[...] = dv.astype(BF16)

    pair = pl.BlockSpec((count, LANES), lambda i, s: (0, i))
    chosen = pl.BlockSpec((count, LANES), lambda i, s: (s[0], i))
    rows = lambda array: pl.BlockSpec((count, array.shape[1]), lambda i, s: (s[0], 0))
    whole = lambda array: pl.BlockSpec(array.shape, lambda i, s: (0,) * array.ndim)
    labels_own = labels_own[None, :]
    labels = labels[:, None]
    operands = [query, keys, values, mixed, grads, logs, labels_own, labels, cosine, sine, cosine_own, sine_own]
    specs = [
        pair,
        chosen,
        chosen,
        pair,
        pair,
        pl.BlockSpec((1, 8, count), lambda i, s: (i, 0, 0)),
        whole(labels_own),
        rows(labels),
        rows(cosine),
        rows(sine),
        whole(cosine_own),
        whole(sine_own),
    ]
    if chained:
        operands.append(before)
        specs.append(pair)
    return pl.pallas_call(
        kernel,
        grid_spec=pltpu.PrefetchScalarGridSpec(
            num_scalar_prefetch=1, grid=(pairs,), in_specs=specs, out_specs=[pair] * 3
        ),
        out_shape=[
            jax.ShapeDtypeStruct((count, width), BF16 if last else F32),
            jax.ShapeDtypeStruct((count, width), BF16),
            jax.ShapeDtypeStruct((count, width), BF16),
        ],
        cost_estimate=pl.CostEstimate(
            flops=40 * count * count * width,
            bytes_accessed=2 * 9 * count * width,
            transcendentals=2 * pairs * count * count,
        ),
        name="attend_back",
    )(jnp.reshape(block, (1,)), *operands)


def project_back(grads, first, weights, factors, outer, latent, rows, block, base, before):
    shards, _, width, local = weights.shape
    count = grads[0].shape[0]
    rank = factors.shape[0] // 3
    number = len(grads)
    based = base is not None
    added = before is not None
    depth = number * rank

    def kernel(block_ref, w_ref, f_ref, a_ref, l_ref, x_ref, *rest):
        g_refs = rest[:number]
        base_ref = rest[number] if based else None
        before_refs = rest[number + based : number + based + 2] if added else None
        out_ref, part_ref, b_ref, acc_ref, lat_ref = rest[-5:]
        step = pl.program_id(0)

        @pl.when(step == 0)
        def _():
            acc_ref[...] = base_ref[...] if based else jnp.zeros_like(acc_ref)
            lat_ref[...] = jnp.zeros_like(lat_ref)

        total = acc_ref[...]
        lats = []
        parts = []
        for j in range(number):
            p = first + j
            g = g_refs[j][...]
            total = total + nt(g, w_ref[0, p])
            lats.append(nt(g, f_ref[p * rank : (p + 1) * rank]))
            parts.append(tn(l_ref[:, p * rank : (p + 1) * rank], g))
        acc_ref[...] = total
        lat_ref[...] += jnp.concatenate(lats, axis=1)
        if added:
            parts = parts[:1] + [
                part + before_refs[1][step, j * rank : (j + 1) * rank]
                for j, part in enumerate(parts[1:])
            ]
        b_ref[step] = jnp.concatenate(parts, axis=0).astype(b_ref.dtype)

        @pl.when(step == shards - 1)
        def _():
            lat = lat_ref[...].astype(BF16)
            final = acc_ref[...] + nn(lat, a_ref[first * rank :])
            out_ref[...] = final.astype(out_ref.dtype)
            part = tn(lat, x_ref[...])
            if added:
                none = jnp.zeros((rank, width), F32)
                part = part + jnp.concatenate([none, before_refs[0][...]], axis=0)
            part_ref[...] = part.astype(part_ref.dtype)

    whole = lambda array: pl.BlockSpec(array.shape, lambda i, s: (0,) * array.ndim)
    chosen = lambda array: pl.BlockSpec((count, array.shape[1]), lambda i, s: (s[0], 0))
    columns = lambda size: pl.BlockSpec((size, local), lambda i, s: (0, i))
    fixed = lambda size: pl.BlockSpec((size, width), lambda i, s: (0, 0))
    operands = [weights, factors, outer, latent, rows, *grads]
    specs = [
        pl.BlockSpec((1, 3, width, local), lambda i, s: (i, 0, 0, 0)),
        columns(3 * rank),
        whole(outer),
        chosen(latent),
        chosen(rows),
        *[columns(count) for _ in grads],
    ]
    if based:
        operands.append(base)
        specs.append(fixed(count))
    if added:
        operands += list(before)
        specs += [whole(array) for array in before]
    return pl.pallas_call(
        kernel,
        grid_spec=pltpu.PrefetchScalarGridSpec(
            num_scalar_prefetch=1,
            grid=(shards,),
            in_specs=specs,
            out_specs=[
                fixed(count),
                fixed(depth),
                pl.BlockSpec((shards, depth, local), lambda i, s: (0, 0, 0)),
            ],
            scratch_shapes=[
                pltpu.VMEM((count, width), F32),
                pltpu.VMEM((count, depth), F32),
            ],
        ),
        out_shape=[
            jax.ShapeDtypeStruct((count, width), F32 if based else BF16),
            jax.ShapeDtypeStruct((depth, width), BF16 if based else F32),
            jax.ShapeDtypeStruct((shards, depth, local), BF16 if based else F32),
        ],
        cost_estimate=pl.CostEstimate(
            flops=2 * number * count * width * width,
            bytes_accessed=6 * width * width + 2 * (number + 4) * count * width,
            transcendentals=0,
        ),
        name="project_back",
    )(jnp.reshape(block, (1,)), *operands)


def out_forward(mixed, weights, outer, factors, rows, gain, shift, next_factors):
    count, width = mixed.shape
    rank = factors.shape[0]

    def kernel(m_ref, w_ref, a_ref, b_ref, x_ref, g_ref, s_ref, f_ref, hid_ref, hidb_ref, n_ref, i_ref, lo_ref, lf_ref):
        m = m_ref[...]
        latent = nt(m, a_ref[...]).astype(BF16)
        total = x_ref[...].astype(F32) + nn(m, w_ref[...]) + nn(latent, b_ref[...])
        hidden, normed, inverse = norm_forward(total, g_ref[...], s_ref[...])
        hid_ref[...] = hidden
        hidden_b = hidden.astype(BF16)
        hidb_ref[...] = hidden_b
        n_ref[...] = normed
        i_ref[...] = inverse
        lo_ref[...] = latent
        lf_ref[...] = nt(hidden_b, f_ref[...]).astype(BF16)

    full = lambda array: pl.BlockSpec(array.shape, lambda i: (0,) * array.ndim)
    block = min(256, count)
    part = lambda size: pl.BlockSpec((block, size), lambda i: (i, 0))
    operands = [mixed, weights, outer, factors, rows, gain, shift, next_factors]
    return pl.pallas_call(
        kernel,
        grid=(count // block,),
        in_specs=[
            part(width),
            full(weights),
            full(outer),
            full(factors),
            part(width),
            full(gain),
            full(shift),
            full(next_factors),
        ],
        out_specs=[part(width), part(width), part(width), part(1), part(rank), part(2 * rank)],
        out_shape=[
            jax.ShapeDtypeStruct((count, width), F32),
            jax.ShapeDtypeStruct((count, width), BF16),
            jax.ShapeDtypeStruct((count, width), F32),
            jax.ShapeDtypeStruct((count, 1), F32),
            jax.ShapeDtypeStruct((count, rank), BF16),
            jax.ShapeDtypeStruct((count, 2 * rank), BF16),
        ],
        cost_estimate=pl.CostEstimate(
            flops=2 * count * width * width,
            bytes_accessed=2 * width * width + 14 * count * width,
            transcendentals=count,
        ),
        name="out_forward",
    )(*operands)


class Whole:
    def __init__(self, upper, lower):
        self.operands = [upper, lower]
        self.shards, _, self.width, self.units = upper.shape
        self.sub = min(512, self.units)
        self.inner = self.units // self.sub
        self.pick = lambda t, s: t
        width, sub = self.width, self.sub
        self.specs = [
            pl.BlockSpec((1, 2, width, sub), lambda t, b, s: (t, 0, 0, b)),
            pl.BlockSpec((1, sub, width), lambda t, b, s: (t, b, 0)),
        ]

    def up(self, refs, rows, i):
        return nn(rows, refs[0][0, i])

    def up_back(self, refs, grads, i):
        return nt(grads, refs[0][0, i])

    def down(self, refs):
        return refs[1][0]


class Gathered:
    def __init__(self, packed, skip):
        self.operands = [packed, packed]
        shards, self.parts, rows, self.units = packed.shape
        self.shards = shards - skip
        self.width = self.units
        self.sub = self.units // 2
        self.inner = 2
        width, sub = self.width, self.sub
        low = self.units // self.parts
        high = rows - low
        self.pick = lambda t, s: lax.rem(s[0] + skip + t, shards)
        self.specs = [
            pl.BlockSpec((1, self.parts, high, sub), lambda t, b, s: (self.pick(t, s), 0, 0, b)),
            pl.BlockSpec((1, sub // low, low, width), lambda t, b, s: (self.pick(t, s), b, high // low, 0)),
        ]

    def gate_up(self, refs, i):
        half = self.parts // 2
        return refs[0][0, i * half : (i + 1) * half].reshape(self.width, self.sub)

    def up(self, refs, rows, i):
        return nn(rows, self.gate_up(refs, i))

    def up_back(self, refs, grads, i):
        return nt(grads, self.gate_up(refs, i))

    def down(self, refs):
        return refs[1][0].reshape(self.sub, self.width)


def ffn_forward(weights, hidden_b, latent, fb, da, total, down, end, pre, first, number):
    count, width = total.shape
    shards, units = weights.shards, weights.units
    rank = da.shape[1]
    sub, inner = weights.sub, weights.inner
    steps = shards * inner
    scalars = jnp.reshape(lax.axis_index("tensor"), (1,)).astype(jnp.int32)

    def kernel(place_ref, w0_ref, w1_ref, hb_ref, l_ref, fb_ref, da_ref, t_ref, d_ref, *rest):
        refs = (w0_ref, w1_ref)
        step = pl.program_id(0) * inner + pl.program_id(1)
        if pre is not None:
            rest = rest[1:]
        if end:
            db_ref, g_ref, s_ref = rest[:3]
            pre_ref, res_ref, sums_ref, ld_ref, acc_ref, lat_ref = rest[3:]
        else:
            pre_ref, acc_ref, lat_ref = rest

        @pl.when(step == 0)
        def _():
            acc_ref[...] = t_ref[...]
            lat_ref[...] = d_ref[...]

        h = hb_ref[...]
        lat = l_ref[...]
        factor = fb_ref[0]
        gate = weights.up(refs, h, 0) + nn(lat[:, :rank], factor[:rank])
        up = weights.up(refs, h, 1) + nn(lat[:, rank:], factor[rank:])
        pre_ref[0] = gate.astype(BF16)
        pre_ref[1] = up.astype(BF16)
        active = (gate * jax.nn.sigmoid(gate) * up).astype(BF16)
        acc_ref[...] += nn(active, weights.down(refs))
        lat_ref[...] += nt(active, da_ref[0])

        if end:

            @pl.when(step == steps - 1)
            def _():
                latent_down = lat_ref[...].astype(BF16)
                sums = acc_ref[...] + nn(latent_down, db_ref[...])
                result, _, _ = norm_forward(sums, g_ref[...], s_ref[...])
                res_ref[...] = result.astype(BF16)
                sums_ref[...] = sums
                ld_ref[...] = latent_down

    full = lambda array: pl.BlockSpec(array.shape, lambda t, b, s: (0,) * array.ndim)
    fixed = lambda size: pl.BlockSpec((count, size), lambda t, b, s: (0, 0))
    operands = [*weights.operands, hidden_b, latent, fb, da, total, down]
    specs = [
        *weights.specs,
        full(hidden_b),
        full(latent),
        pl.BlockSpec((1, 2 * rank, sub), lambda t, b, s: (weights.pick(t, s), 0, b)),
        pl.BlockSpec((1, rank, sub), lambda t, b, s: (weights.pick(t, s), 0, b)),
        full(total),
        full(down),
    ]
    out_specs = [pl.BlockSpec((2, count, sub), lambda t, b, s: (0, 0, (first + t) * inner + b))]
    out_shape = [jax.ShapeDtypeStruct((2, count, number * units), BF16)]
    scratch = []
    aliases = {}
    if pre is not None:
        aliases = {len(operands) + 1: 0}
        operands.append(pre)
        specs.append(pl.BlockSpec(memory_space=pl.ANY))
    if end:
        operands += list(end)
        specs += [full(array) for array in end]
        out_specs += [fixed(width)] * 2 + [fixed(rank)]
        out_shape += [
            jax.ShapeDtypeStruct((count, width), BF16),
            jax.ShapeDtypeStruct((count, width), F32),
            jax.ShapeDtypeStruct((count, rank), BF16),
        ]
        scratch = [pltpu.VMEM((count, width), F32), pltpu.VMEM((count, rank), F32)]
    else:
        out_specs += [fixed(width), fixed(rank)]
        out_shape += [
            jax.ShapeDtypeStruct((count, width), F32),
            jax.ShapeDtypeStruct((count, rank), F32),
        ]
    return pl.pallas_call(
        kernel,
        grid_spec=pltpu.PrefetchScalarGridSpec(
            num_scalar_prefetch=1,
            grid=(shards, inner),
            in_specs=specs,
            out_specs=out_specs,
            scratch_shapes=scratch,
        ),
        out_shape=out_shape,
        input_output_aliases=aliases,
        cost_estimate=pl.CostEstimate(
            flops=6 * count * width * shards * units,
            bytes_accessed=6 * width * shards * units + 4 * count * shards * units,
            transcendentals=count * shards * units,
        ),
        name="ffn_forward",
    )(scalars, *operands)


def ffn_backward(weights, sums, cotangent, gain_two, db, pre, latent_ffn, fb, da, end):
    count, width = sums.shape
    shards, units = weights.shards, weights.units
    rank = da.shape[1]
    sub, inner = weights.sub, weights.inner
    steps = shards * inner
    scalars = jnp.reshape(lax.axis_index("tensor"), (1,)).astype(jnp.int32)

    def kernel(place_ref, w0_ref, w1_ref, sums_ref, c_ref, g2_ref, db_ref, pre_ref, lf_ref, fb_ref, da_ref, *rest):
        refs = (w0_ref, w1_ref)
        step = pl.program_id(0) * inner + pl.program_id(1)
        ld_ref, fa_ref, hb_ref, n_ref, i_ref, gain_ref, lo_ref, ob_ref, oa_ref, m_ref, wo_ref = rest[:11]
        split_ref, first_ref, mixed_ref, common_ref, acc_ref, lat_ref, gb_ref, ldg_ref = rest[11:]

        @pl.when(step == 0)
        def _():
            _, normed, inverse = norm_forward(sums_ref[...], g2_ref[...], 0.0)
            grad = norm_backward(c_ref[...], normed, inverse, g2_ref[...])
            acc_ref[...] = grad
            grad_b = grad.astype(BF16)
            gb_ref[...] = grad_b
            ldg_ref[...] = nt(grad_b, db_ref[...]).astype(BF16)
            lat_ref[...] = jnp.zeros_like(lat_ref)

        ldg = ldg_ref[...]
        lf = lf_ref[...]
        factor = fb_ref[0]
        grad_active = nt(gb_ref[...], weights.down(refs)) + nn(ldg, da_ref[0])
        gate = pre_ref[0].astype(F32)
        up = pre_ref[1].astype(F32)
        sigma = jax.nn.sigmoid(gate)
        swish = gate * sigma
        active = (swish * up).astype(BF16)
        grad_gate = (grad_active * up * (sigma + swish * (1.0 - sigma))).astype(BF16)
        grad_up = (grad_active * swish).astype(BF16)
        split = jnp.concatenate(
            [tn(ldg, active), tn(lf[:, :rank], grad_gate), tn(lf[:, rank:], grad_up)], axis=0
        )
        split_ref[0] = split.astype(BF16)
        acc_ref[...] += weights.up_back(refs, grad_gate, 0) + weights.up_back(refs, grad_up, 1)
        lat_ref[...] += jnp.concatenate(
            [nt(grad_gate, factor[:rank]), nt(grad_up, factor[rank:])], axis=1
        )

        @pl.when(step == steps - 1)
        def _():
            lat = lat_ref[...].astype(BF16)
            sums = acc_ref[...] + nn(lat, fa_ref[...])
            first = norm_backward(sums, n_ref[...], i_ref[...], gain_ref[...])
            first_ref[...] = first
            branch = first.astype(BF16)
            log = nt(branch, ob_ref[...]).astype(BF16)
            common_ref[...] = jnp.concatenate(
                [
                    tn(ld_ref[...], gb_ref[...]),
                    tn(lat, hb_ref[...]),
                    tn(lo_ref[...], branch),
                    tn(log, m_ref[...]),
                ],
                axis=0,
            ).astype(BF16)
            mixed_ref[...] = (nt(branch, wo_ref[...]) + nn(log, oa_ref[...])).astype(BF16)

    full = lambda array: pl.BlockSpec(array.shape, lambda t, b, s: (0,) * array.ndim)
    fixed = lambda rows, size: pl.BlockSpec((rows, size), lambda t, b, s: (0, 0))
    operands = [*weights.operands, sums, cotangent, gain_two, db, pre, latent_ffn, fb, da, *end]
    specs = [
        *weights.specs,
        full(sums),
        full(cotangent),
        full(gain_two),
        full(db),
        pl.BlockSpec((2, count, sub), lambda t, b, s: (0, 0, t * inner + b)),
        full(latent_ffn),
        pl.BlockSpec((1, 2 * rank, sub), lambda t, b, s: (weights.pick(t, s), 0, b)),
        pl.BlockSpec((1, rank, sub), lambda t, b, s: (weights.pick(t, s), 0, b)),
        *[full(array) for array in end],
    ]
    out_specs = [pl.BlockSpec((1, 3 * rank, sub), lambda t, b, s: (t, 0, b))]
    out_shape = [jax.ShapeDtypeStruct((shards, 3 * rank, units), BF16)]
    out_specs += [fixed(count, width), fixed(count, width), fixed(5 * rank, width)]
    out_shape += [
        jax.ShapeDtypeStruct((count, width), F32),
        jax.ShapeDtypeStruct((count, width), BF16),
        jax.ShapeDtypeStruct((5 * rank, width), BF16),
    ]
    scratch = [
        pltpu.VMEM((count, width), F32),
        pltpu.VMEM((count, 2 * rank), F32),
        pltpu.VMEM((count, width), BF16),
        pltpu.VMEM((count, rank), BF16),
    ]
    return pl.pallas_call(
        kernel,
        grid_spec=pltpu.PrefetchScalarGridSpec(
            num_scalar_prefetch=1,
            grid=(shards, inner),
            in_specs=specs,
            out_specs=out_specs,
            scratch_shapes=scratch,
        ),
        out_shape=out_shape,
        cost_estimate=pl.CostEstimate(
            flops=6 * count * width * shards * units,
            bytes_accessed=6 * width * shards * units + 4 * count * shards * units,
            transcendentals=count * shards * units,
        ),
        name="ffn_backward",
    )(scalars, *operands)


def norm_forward(rows, gain, shift):
    centre = jnp.mean(rows, axis=-1, keepdims=True)
    centred = rows - centre
    spread = jnp.mean(centred * centred, axis=-1, keepdims=True)
    inverse = lax.rsqrt(spread + 1e-12)
    normed = centred * inverse
    return (normed * gain + shift, normed, inverse)


def norm_backward(grads, normed, inverse, gain):
    scaled = grads * gain
    first_mean = jnp.mean(scaled, axis=-1, keepdims=True)
    second_mean = jnp.mean(scaled * normed, axis=-1, keepdims=True)
    return inverse * (scaled - first_mean - normed * second_mean)


def rope_tables(length, extra):
    half = HEAD_DIM // 2
    step = 64
    freq = 10000.0 ** (-(2.0 * np.arange(half)) / HEAD_DIM)
    freq = np.tile(freq, LANES // half)
    sign = np.where(np.arange(LANES) % HEAD_DIM < half, -1.0, 1.0)
    coarse = ((np.arange(length + extra) % length)[::step, None] * freq).astype(np.float64)
    fine = np.arange(step)[:, None] * freq
    f = lambda array: jnp.asarray(array, F32)
    cos_c, sin_c = f(np.cos(coarse))[:, None], f(np.sin(coarse))[:, None]
    cos_f, sin_f = f(np.cos(fine))[None], f(np.sin(fine))[None]
    cosine = (cos_c * cos_f - sin_c * sin_f).reshape(-1, LANES)
    sine = ((sin_c * cos_f + cos_c * sin_f) * f(sign)).reshape(-1, LANES)
    return cosine, sine


def window(array, start, count):
    return lax.dynamic_slice_in_dim(array, start, count, 0)


def gather_weight(local, parts, part):
    rows = local.shape[0] // parts
    piece = window(local, part * rows, rows)
    return lax.all_gather(piece, ALL, axis=0, tiled=True)


def gather_ffn(w_gate_up, w_down, parts, part):
    _, width, units = w_gate_up.shape
    upper = w_gate_up.reshape(2 * width, units)
    if units == width and width % (128 * parts // 8) == 0 and parts == 8:
        high, low = 2 * width // parts, units // parts
        piece = jnp.concatenate(
            [window(upper, part * high, high), window(w_down, part * low, low)], axis=0
        )
        whole = lax.all_gather(piece, ALL, axis=0, tiled=True)
        return (whole.reshape(-1, parts, high + low, units),)
    return (
        gather_weight(upper, parts, part).reshape(-1, 2, width, units),
        gather_weight(w_down, parts, part).reshape(-1, units, width),
    )


def flip(bit):
    return [(i, i ^ bit) for i in range(4)]


def send_round(piece):
    shards = lax.axis_size("tensor")
    return [lax.ppermute(piece, "tensor", cyclic(shards, k)) for k in range(1, shards)]


def spread_first(stack):
    return lax.ppermute(stack, "yx", flip(1)), lax.ppermute(stack, "yx", flip(2))


def spread_second(across, along):
    half = across.shape[0] // 2
    return (
        lax.ppermute(across[:half], "yx", flip(2)),
        lax.ppermute(along[half:], "yx", flip(1)),
    )


def swap_core(near):
    return lax.ppermute(near, "core", [(0, 1), (1, 0)])


def assemble(own, near, far, outs, store):
    shards = near.shape[1] + 1
    rows, cols = own.shape[1:]
    scalars = jnp.stack(
        [lax.axis_index("tensor"), lax.axis_index("yx"), lax.axis_index("core")]
    ).astype(jnp.int32)

    def behind(t, s):
        return lax.rem(s[0] - t + shards, shards)

    def kernel(scalar_ref, own_ref, near_ref, far_ref, *out_refs):
        mine = behind(pl.program_id(0), scalar_ref) == 0
        first = scalar_ref[2] == 0

        @pl.when(mine)
        def _():
            for j in range(8):
                store(own_ref[j], j, out_refs)

        for low_ref, high_ref, here in ((near_ref, far_ref, first), (far_ref, near_ref, jnp.logical_not(first))):

            @pl.when(jnp.logical_and(jnp.logical_not(mine), here))
            def _():
                for i in range(4):
                    side = lax.bitwise_xor(scalar_ref[1], i)
                    store(low_ref[side, 0], 2 * i, out_refs)
                    store(high_ref[side, 0], 2 * i + 1, out_refs)

    other = pl.BlockSpec(
        (4, 1, rows, cols), lambda t, s: (0, jnp.maximum(behind(t, s) - 1, 0), 0, 0)
    )
    return pl.pallas_call(
        kernel,
        grid_spec=pltpu.PrefetchScalarGridSpec(
            num_scalar_prefetch=1,
            grid=(shards,),
            in_specs=[pl.BlockSpec((8, rows, cols), lambda t, s: (0, 0, 0)), other, other],
            out_specs=[spec for _, spec in outs],
        ),
        out_shape=[jax.ShapeDtypeStruct(shape, BF16) for shape, _ in outs],
        cost_estimate=pl.CostEstimate(
            flops=0, bytes_accessed=32 * shards * rows * cols, transcendentals=0
        ),
    )(scalars, own, near, far)


def assemble_qkv(own, near, far, width, local):
    shards = near.shape[1] + 1
    size = width // 8
    short = local // 8
    head = 3 * size

    def store(piece, j, outs):
        for p in range(3):
            outs[0][0, p, j * size : (j + 1) * size] = piece[p * size : (p + 1) * size]
        for c in range(width // local):
            outs[1][j * short : (j + 1) * short, c * local : (c + 1) * local] = piece[
                head + c * short : head + (c + 1) * short
            ]

    outs = [
        (
            (shards, 3, width, local),
            pl.BlockSpec((1, 3, width, local), lambda t, s: (t, 0, 0, 0)),
        ),
        ((shards * local, width), pl.BlockSpec((local, width), lambda t, s: (t, 0))),
    ]
    return assemble(own, near, far, outs, store)


def in_order(blocks, place):
    shards = len(blocks)
    stack = jnp.stack(blocks)
    return jnp.stack(
        [
            lax.dynamic_index_in_dim(stack, lax.rem(place - t + shards, shards), 0, keepdims=False)
            for t in range(shards)
        ]
    )


def cyclic(size, step):
    return [(i, (i + step) % size) for i in range(size)]


def send_grads(share):
    shards = lax.axis_size("tensor")
    place = lax.axis_index("tensor")
    received = [share(place)]
    for step in range(1, shards):
        sent = share(lax.rem(place + step, shards))
        received.append(lax.ppermute(sent, "tensor", cyclic(shards, step)))
    return received


def add_all(blocks):
    total = blocks[0].astype(F32)
    for block in blocks[1:]:
        total = total + block.astype(F32)
    return total


def line_gather(block):
    shards = lax.axis_size("tensor")
    blocks = [(block, 0)]
    up = down = block
    for step in range(1, shards):
        links = [(i, i + 1) for i in range(step - 1, shards - 1)]
        up = lax.ppermute(up, "tensor", links)
        down = lax.ppermute(down, "tensor", [(shards - 1 - i, shards - 1 - j) for i, j in links])
        blocks += [(up, -step), (down, step)]
    return blocks


def after(array, *marks):
    return lax.optimization_barrier((array, *marks))[0]


def place_sums(every, plan, adapters, place):
    count, rows, width = every.shape
    rows -= 16
    owners = jnp.sum(
        every[:, rows, :adapters].astype(jnp.int32) * jnp.arange(adapters, dtype=jnp.int32), axis=1
    )
    scalars = jnp.concatenate([jnp.reshape(place, (1,)), owners]).astype(jnp.int32)

    def kernel(scalar_ref, every_ref, *refs):
        outs, total_ref = refs[:-1], refs[-1]
        adapter = pl.program_id(0)
        total_ref[...] = jnp.zeros_like(total_ref)
        for s in range(count):

            @pl.when(scalar_ref[1 + s] == adapter)
            def _():
                total_ref[...] += every_ref[s, :rows].astype(F32)

        for (first, size, columns), out in zip(plan, outs):
            if columns is None:
                out[0] = total_ref[first : first + size]
            else:
                start = pl.multiple_of(scalar_ref[0] * columns, LANES)
                out[0] = total_ref[first : first + size, pl.ds(start, columns)]

    shapes = [(adapters, size, width if columns is None else columns) for _, size, columns in plan]
    return pl.pallas_call(
        kernel,
        grid_spec=pltpu.PrefetchScalarGridSpec(
            num_scalar_prefetch=1,
            grid=(adapters,),
            in_specs=[pl.BlockSpec(every.shape, lambda i, s: (0, 0, 0))],
            out_specs=[pl.BlockSpec((1,) + shape[1:], lambda i, s: (i, 0, 0)) for shape in shapes],
            scratch_shapes=[pltpu.VMEM((rows, width), F32)],
        ),
        out_shape=[jax.ShapeDtypeStruct(shape, F32) for shape in shapes],
        cost_estimate=pl.CostEstimate(
            flops=count * rows * width,
            bytes_accessed=(2 * count + 4 * adapters) * rows * width,
            transcendentals=0,
        ),
        name="place_sums",
    )(scalars, every)


def after(array, *marks):
    return lax.optimization_barrier((array, *marks))[0]


def layer(
    layer_input,
    output_grad,
    segments,
    adapter_ids,
    ln_gain,
    ln_bias,
    w_qkv,
    w_out,
    w_gate_up,
    w_down,
    qkv_a,
    qkv_b,
    out_a,
    out_b,
    ffn_a,
    ffn_b,
    down_a,
    down_b,
):
    seq_count, length = segments.shape
    assert seq_count == 1
    width = layer_input.shape[1]
    shards = lax.axis_size("tensor")
    parts = lax.axis_size(DP)
    place = lax.axis_index("tensor")
    part = lax.axis_index(DP)
    members = shards // 2
    half = length // 2
    count = length // shards
    group = place // members
    member = lax.rem(place, members)
    local = w_qkv.shape[2]
    units = w_down.shape[0]
    rank = out_b.shape[1]

    adapter = adapter_ids[0, 0]
    pick = lambda stack: lax.dynamic_index_in_dim(stack, adapter, 0, keepdims=False)
    qa, ob, fa, db = pick(qkv_a), pick(out_b), pick(ffn_a), pick(down_b)
    small = jnp.concatenate(
        [
            pick(qkv_b),
            pick(out_a),
            pick(ffn_b).reshape(-1, local),
            pick(down_a).reshape(-1, local),
        ],
        axis=0,
    )
    labels = segments[0]
    long = labels[: length - half + 1] == labels[half - 1 :]
    start = jnp.sum(jnp.where(long, jnp.arange(length - half + 1, dtype=jnp.int32), 0))
    group_start = start + group * half
    own_start = start + place * count
    x_group = roll_rows([(layer_input, 0)], place, group_start, half, BF16)
    x_own_b = window(x_group, member * count, count)
    cotangent = roll_rows([(output_grad, 0)], place, own_start, count, F32)
    labels_twice = jnp.concatenate([labels, labels[:half]])
    labels_group = window(labels_twice, group_start, half)
    labels_own = window(labels_group, member * count, count)
    cosine, sine = rope_tables(length, half)
    tables = (window(cosine, group_start, half), window(sine, group_start, half))
    tables_own = tuple(window(table, member * count, count) for table in tables)

    ffn_all = gather_ffn(w_gate_up, w_down, parts, part)
    if parts == 8:
        qkv_pieces = w_qkv.reshape(3, 8, width // 8, local).transpose(1, 0, 2, 3)
        out_pieces = w_out.reshape(8, local // 8, width // local, local).transpose(0, 2, 1, 3)
        pieces = jnp.concatenate(
            [
                qkv_pieces.reshape(8, 3 * width // 8, local),
                out_pieces.reshape(8, width // 8, local),
            ],
            axis=1,
        )
        piece = lax.dynamic_index_in_dim(pieces, part, 0, keepdims=False)
        joined = send_round(jnp.concatenate([piece, small], axis=0))
        size = piece.shape[0]
        small = in_order([small] + [block[size:] for block in joined], place)
        stack = jnp.concatenate([block[:size] for block in joined], axis=0)
        stack = after(stack, x_group, cotangent)
        across, along = spread_first(stack)
        corner = jnp.concatenate(spread_second(across, along), axis=0)
        near = jnp.stack([stack, across, along, corner]).reshape(4, shards - 1, size, local)
        far = swap_core(near)
        qkv_all, out_all = assemble_qkv(pieces, near, far, width, local)
    else:
        qkv_all = gather_weight(w_qkv.reshape(3 * width, local), parts, part)
        qkv_all = qkv_all.reshape(shards, 3, width, local)
        out_all = gather_weight(w_out, parts, part)
        small = lax.all_gather(small, "tensor", axis=0)
    cuts = np.cumsum([3 * rank, rank, 2 * rank * (units // local)])
    rejoin = lambda piece: piece.transpose(1, 0, 2).reshape(piece.shape[1], -1)
    qb = rejoin(small[:, : cuts[0]])
    oa = rejoin(small[:, cuts[0] : cuts[1]])
    fb = small[:, cuts[1] : cuts[2]].reshape(shards, 2 * rank, units)
    da = small[:, cuts[2] :].reshape(shards, rank, units)

    latent_qkv = nt(x_group, qa).astype(BF16)
    latent_own = window(latent_qkv, member * count, count)
    query, keys, values = project_qkv(
        x_group, x_own_b, qkv_all, latent_qkv, latent_own, qb, tables, tables_own
    )
    mixed, logs = attend(query, keys, values, labels_own, labels_group)
    hidden, hidden_b, normed, inverse, latent_out, latent_ffn = out_forward(
        mixed, out_all, oa, ob, x_own_b, ln_gain[:1], ln_bias[:1], fa
    )

    zero = jnp.zeros((count, rank), F32)
    end = (db, ln_gain[1:], ln_bias[1:])
    packed = len(ffn_all) == 1
    if packed:
        mine = lambda stack: lax.dynamic_slice_in_dim(stack, place, 1, 0)
        own = Whole(w_gate_up[None], w_down[None])
        pre, total, down = ffn_forward(
            own, hidden_b, latent_ffn, mine(fb), mine(da), hidden, zero, None, None, 0, shards
        )
        others, every = Gathered(ffn_all[0], 1), Gathered(ffn_all[0], 0)
    else:
        pre, total, down = None, hidden, zero
        others = every = Whole(*ffn_all)
    pre, result, sums, latent_down = ffn_forward(
        others, hidden_b, latent_ffn, fb, da, total, down, end, pre, shards - others.shards, shards
    )
    rolled = lax.all_gather(result, "tensor", axis=0, tiled=True)

    end = (
        latent_down, fa, hidden_b, normed, inverse, ln_gain[:1], latent_out, ob, oa, mixed, out_all,
    )
    split, grad_first, grad_mixed, common = ffn_backward(
        every, sums, cotangent, ln_gain[1:], db, pre, latent_ffn, fb, da, end
    )

    dq = None
    received = []
    before = None
    for d in range(1, members):
        target = lax.rem(member + d, members)
        dq, dk, dv = attend_back(
            query, keys, values, mixed, grad_mixed, logs, labels_own, labels_group, tables,
            tables_own, target, dq, False,
        )
        sent, *part_of = project_back(
            [dk, dv], 1, qkv_all, qb, qa, latent_qkv, x_group, target, None, None
        )
        before = part_of if before is None else [a + b for a, b in zip(before, part_of)]
        links = [
            (g * members + i, g * members + (i + d) % members)
            for g in range(2)
            for i in range(members)
        ]
        received.append(lax.ppermute(sent, "tensor", links))

    def early_share(target):
        entry = lax.rem(target - place + shards, shards) if packed else target
        mine = lax.dynamic_index_in_dim(split, entry, 0, keepdims=False)
        return jnp.concatenate([common, mine.reshape(-1, width)], axis=0)

    def late_share(target):
        mine = lax.dynamic_index_in_dim(qkv_b_part, target, 0, keepdims=False)
        return jnp.concatenate([qkv_a_part, mine.reshape(-1, width)], axis=0)

    common = after(common, sent)
    early = send_grads(early_share)
    dq, dk, dv = attend_back(
        query, keys, values, mixed, grad_mixed, logs, labels_own, labels_group, tables, tables_own,
        member, dq, True,
    )
    back, qkv_a_part, qkv_b_part = project_back(
        [dq, dk, dv], 0, qkv_all, qb, qa, latent_qkv, x_group, member, grad_first, before
    )
    late = send_grads(late_share)

    adapters = qkv_a.shape[0]
    hot = (adapter == jnp.arange(adapters, dtype=jnp.int32)).astype(BF16)
    flag = jnp.zeros((16, width), BF16).at[0, :adapters].set(hot)
    for piece in received:
        back = back + after(piece, back).astype(F32)
    back = back.astype(BF16)
    blocks = line_gather(back)
    output = roll_rows([(after(rolled, back), 0)], place, -start, length, BF16)
    early_sum = add_all([early[0]] + [after(piece, output) for piece in early[1:]]).astype(BF16)
    late_sum = add_all([late[0]] + [after(piece, output) for piece in late[1:]]).astype(BF16)
    every_sum = lax.all_gather(jnp.concatenate([early_sum, late_sum, flag], axis=0), DP, axis=0)
    plan = [
        (0, rank, None),
        (rank, 2 * rank, None),
        (3 * rank, rank, None),
        (4 * rank, rank, local),
    ]
    straight = units == width
    if straight:
        plan += [(5 * rank, rank, None), (6 * rank, 2 * rank, None)]
    else:
        plan += [(5 * rank, 3 * rank * units // width, None)]
    mark = early_sum.shape[0]
    plan += [
        (mark, 3 * rank, None),
        (mark + 3 * rank, 3 * rank * local // width, None),
    ]
    grads = place_sums(every_sum, plan, adapters, place)
    down_b_grad, ffn_a_grad, out_b_grad, out_a_grad = grads[:4]
    if straight:
        down_a_grad, ffn_b_grad = grads[4:6]
    else:
        own_split = grads[4].reshape(adapters, 3 * rank, units)
        down_a_grad, ffn_b_grad = own_split[:, :rank], own_split[:, rank:]
    qkv_a_grad, qkv_b_grad = grads[-2:]
    qkv_b_grad = qkv_b_grad.reshape(adapters, 3 * rank, local)

    blocks = [(after(block, output, qkv_a_grad, out_b_grad), i) for block, i in blocks]
    grad_whole = roll_rows(blocks, place, -start, length, F32)
    return (
        output,
        grad_whole,
        qkv_a_grad,
        qkv_b_grad,
        out_a_grad,
        out_b_grad,
        ffn_a_grad,
        ffn_b_grad,
        down_a_grad,
        down_b_grad,
    )


def solution(mesh):
    devices = mesh.devices
    mesh = Mesh(
        devices.reshape(devices.shape[0] // 2, 2, devices.shape[1]), ("yx", "core", "tensor")
    )
    in_specs = (
        P(DP, None),
        P(DP, None),
        P(DP, None),
        P(DP, None),
        P(),
        P(),
        P(None, None, "tensor"),
        P("tensor", None),
        P(None, None, "tensor"),
        P("tensor", None),
        P(),
        P(None, None, "tensor"),
        P(None, None, "tensor"),
        P(),
        P(),
        P(None, None, "tensor"),
        P(None, None, "tensor"),
        P(),
    )
    out_specs = (
        P(DP, None),
        P(DP, None),
        P(),
        P(None, None, "tensor"),
        P(None, None, "tensor"),
        P(),
        P(),
        P(None, None, "tensor"),
        P(None, None, "tensor"),
        P(),
    )
    return jax.shard_map(layer, mesh=mesh, in_specs=in_specs, out_specs=out_specs, check_vma=False)
```
